32 devices in a mesh: dp: 8 (over z, y), tensor: 4 (over x, core).
Axes of the slice: x: 2, y: 2, z: 4, core: 2. Of those that a mesh axis runs over, the one named last changes fastest.
Arguments:
- text_in: bfloat16 [16384, 768], P(('dp', 'tensor')), may hold values from -6 to 6
- layout_in: bfloat16 [16384, 192], P(('dp', 'tensor')), may hold values from -6 to 6
- token_mask: int32 [16384], P(('dp', 'tensor')), may hold values 0 or 1
- box_mask: int32 [16384], P(('dp', 'tensor')), may hold values 0 or 1
- cot_text: bfloat16 [16384, 768], P(('dp', 'tensor')), may hold values from -6 to 6
- cot_layout: bfloat16 [16384, 192], P(('dp', 'tensor')), may hold values from -6 to 6
- text_query_weight: bfloat16 [768, 768], replicated, may hold values from -0.21875 to 0.21875
- text_query_bias: bfloat16 [768], replicated, may hold values from -2.5 to 2.5
- text_key_weight: bfloat16 [768, 768], replicated, may hold values from -0.21875 to 0.21875
- text_value_weight: bfloat16 [768, 768], replicated, may hold values from -0.21875 to 0.21875
- text_value_bias: bfloat16 [768], replicated, may hold values from -2.5 to 2.5
- text_output_weight: bfloat16 [768, 768], replicated, may hold values from -1.75 to 1.75
- text_output_bias: bfloat16 [768], replicated, may hold values from -2.5 to 2.5
- text_attend_gain: bfloat16 [768], replicated, may hold values from 0.25 to 1.75
- text_attend_shift: bfloat16 [768], replicated, may hold values from -2.5 to 2.5
- text_up_weight: bfloat16 [768, 3072], P(None, 'tensor'), may hold values from -0.21875 to 0.21875
- text_up_bias: bfloat16 [3072], P('tensor'), may hold values from -2.5 to 2.5
- text_down_weight: bfloat16 [3072, 768], P('tensor'), may hold values from -0.109375 to 0.109375
- text_down_bias: bfloat16 [768], replicated, may hold values from -2.5 to 2.5
- text_feed_gain: bfloat16 [768], replicated, may hold values from 0.25 to 1.75
- text_feed_shift: bfloat16 [768], replicated, may hold values from -2.5 to 2.5
- layout_query_weight: bfloat16 [192, 192], replicated, may hold values from -0.4375 to 0.4375
- layout_query_bias: bfloat16 [192], replicated, may hold values from -2.5 to 2.5
- layout_key_weight: bfloat16 [192, 192], replicated, may hold values from -0.4375 to 0.4375
- layout_value_weight: bfloat16 [192, 192], replicated, may hold values from -0.4375 to 0.4375
- layout_value_bias: bfloat16 [192], replicated, may hold values from -2.5 to 2.5
- layout_output_weight: bfloat16 [192, 192], replicated, may hold values from -3.5 to 3.5
- layout_output_bias: bfloat16 [192], replicated, may hold values from -2.5 to 2.5
- layout_attend_gain: bfloat16 [192], replicated, may hold values from 0.25 to 1.75
- layout_attend_shift: bfloat16 [192], replicated, may hold values from -2.5 to 2.5
- layout_up_weight: bfloat16 [192, 768], P(None, 'tensor'), may hold values from -0.4375 to 0.4375
- layout_up_bias: bfloat16 [768], P('tensor'), may hold values from -2.5 to 2.5
- layout_down_weight: bfloat16 [768, 192], P('tensor'), may hold values from -0.21875 to 0.21875
- layout_down_bias: bfloat16 [192], replicated, may hold values from -2.5 to 2.5
- layout_feed_gain: bfloat16 [192], replicated, may hold values from 0.25 to 1.75
- layout_feed_shift: bfloat16 [192], replicated, may hold values from -2.5 to 2.5
Outputs:
- text_out: bfloat16 [16384, 768], P(('dp', 'tensor'))
- layout_out: bfloat16 [16384, 192], P(('dp', 'tensor'))
- text_in_grad: float32 [16384, 768], P(('dp', 'tensor'))
- layout_in_grad: float32 [16384, 192], P(('dp', 'tensor'))
- grad_text_query_weight: float32 [768, 768], replicated
- grad_text_query_bias: float32 [768], replicated
- grad_text_key_weight: float32 [768, 768], replicated
- grad_text_value_weight: float32 [768, 768], replicated
- grad_text_value_bias: float32 [768], replicated
- grad_text_output_weight: float32 [768, 768], replicated
- grad_text_output_bias: float32 [768], replicated
- grad_text_attend_gain: float32 [768], replicated
- grad_text_attend_shift: float32 [768], replicated
- grad_text_up_weight: float32 [768, 3072], P(None, 'tensor')
- grad_text_up_bias: float32 [3072], P('tensor')
- grad_text_down_weight: float32 [3072, 768], P('tensor')
- grad_text_down_bias: float32 [768], replicated
- grad_text_feed_gain: float32 [768], replicated
- grad_text_feed_shift: float32 [768], replicated
- grad_layout_query_weight: float32 [192, 192], replicated
- grad_layout_query_bias: float32 [192], replicated
- grad_layout_key_weight: float32 [192, 192], replicated
- grad_layout_value_weight: float32 [192, 192], replicated
- grad_layout_value_bias: float32 [192], replicated
- grad_layout_output_weight: float32 [192, 192], replicated
- grad_layout_output_bias: float32 [192], replicated
- grad_layout_attend_gain: float32 [192], replicated
- grad_layout_attend_shift: float32 [192], replicated
- grad_layout_up_weight: float32 [192, 768], P(None, 'tensor')
- grad_layout_up_bias: float32 [768], P('tensor')
- grad_layout_down_weight: float32 [768, 192], P('tensor')
- grad_layout_down_bias: float32 [192], replicated
- grad_layout_feed_gain: float32 [192], replicated
- grad_layout_feed_shift: float32 [192], replicated
The draws below stay inside these ranges and needn't reach their ends.
All inputs are finite; a program needn't handle non-finite values. No bound on the sum of `token_mask` or of `box_mask` on one device may be relied on, other than what follows from the above.
Results may differ from the reference program's by a relative error of at most 0.013.
The reference program's roundings to bfloat16 on the way count: a program that leaves them out, or rounds other values in their place, can miss the bound.
Values may be sent and summed in bfloat16 or wider, within the bound.
A program may use at most 192 MiB of HBM per device.

```python
import math
import jax
import jax.numpy as jnp
from jax import lax

D = 768
DL = 192
HEADS = 12
FF = 3072
FFL = 768
PAGE = 512
TOKENS = 16384


def place_ends(values, key, low, high):
    longest = values.shape.index(max(values.shape))
    spots = []
    for shift in (0, 1):
        where = [jax.random.randint(jax.random.fold_in(key, axis), (), 0, length) for axis, length in enumerate(values.shape)]
        where[longest] = (where[longest] + shift) % values.shape[longest]
        spots.append(tuple(where))
    return values.at[spots[0]].set(low).at[spots[1]].set(high)


def shard_levels(own_key, dims, pieces, smallest, largest):
    level = 1.0
    for axis_at, blocks in pieces:
        heights = jax.random.uniform(jax.random.fold_in(jax.random.fold_in(own_key, 6), axis_at), (blocks,), jnp.float32, smallest / len(pieces), largest / len(pieces))
        level = level * jnp.repeat(jnp.exp(heights), dims[axis_at] // blocks).reshape((-1,) + (1,) * (len(dims) - 1 - axis_at))
    return level


def noise(own_key, dims, deviation, reach, split=(), dtype=jnp.bfloat16):
    loudness = shard_levels(own_key, dims, split, -0.22, 0.18) if split else 1.0
    result = jax.random.normal(own_key, dims, jnp.float32) * deviation * loudness
    return jnp.minimum(jnp.maximum(result, -reach), reach).astype(dtype)


def setup_inputs(seed: int = 0) -> dict:
    keys = jax.random.split(jax.random.key(seed), 37)
    text_in = noise(keys[0], (TOKENS, D), 1.0, 6.0, ((0, 32),))
    layout_in = noise(keys[1], (TOKENS, DL), 1.0, 6.0, ((0, 32),))
    token_mask = place_ends((jax.random.randint(keys[2], (TOKENS,), 0, 100) < 15).astype(jnp.int32), jax.random.fold_in(keys[2], 1), 0, 1)
    box_mask = place_ends((jax.random.randint(keys[3], (TOKENS,), 0, 100) < 15).astype(jnp.int32), jax.random.fold_in(keys[3], 1), 0, 1)
    cot_text = noise(keys[4], (TOKENS, D), 1.0, 6.0, ((0, 32),))
    cot_layout = noise(keys[5], (TOKENS, DL), 1.0, 6.0, ((0, 32),))
    text_query_weight = noise(keys[6], (D, D), D ** -0.5, 0.21875)
    text_query_bias = noise(keys[7], (D,), 0.3, 2.5)
    text_key_weight = noise(keys[8], (D, D), D ** -0.5, 0.21875)
    text_value_weight = noise(keys[9], (D, D), D ** -0.5, 0.21875)
    text_value_bias = noise(keys[10], (D,), 0.3, 2.5)
    text_output_weight = noise(keys[11], (D, D), (max(D // 64, 1)) ** -0.5, 1.75)
    text_output_bias = noise(keys[12], (D,), 0.3, 2.5)
    text_attend_gain = jnp.clip(1.0 + 0.15 * jax.random.normal(keys[13], (D,), jnp.float32), 0.25, 1.75).astype(jnp.bfloat16)
    text_attend_shift = noise(keys[14], (D,), 0.3, 2.5)
    text_up_weight = noise(keys[15], (D, FF), D ** -0.5, 0.21875, ((1, 4),))
    text_up_bias = noise(keys[16], (FF,), 0.3, 2.5, ((0, 4),))
    text_down_weight = noise(keys[17], (FF, D), FF ** -0.5, 0.109375, ((0, 4),))
    text_down_bias = noise(keys[18], (D,), 0.3, 2.5)
    text_feed_gain = jnp.clip(1.0 + 0.15 * jax.random.normal(keys[19], (D,), jnp.float32), 0.25, 1.75).astype(jnp.bfloat16)
    text_feed_shift = noise(keys[20], (D,), 0.3, 2.5)
    layout_query_weight = noise(keys[21], (DL, DL), DL ** -0.5, 0.4375)
    layout_query_bias = noise(keys[22], (DL,), 0.3, 2.5)
    layout_key_weight = noise(keys[23], (DL, DL), DL ** -0.5, 0.4375)
    layout_value_weight = noise(keys[24], (DL, DL), DL ** -0.5, 0.4375)
    layout_value_bias = noise(keys[25], (DL,), 0.3, 2.5)
    layout_output_weight = noise(keys[26], (DL, DL), (max(DL // 64, 1)) ** -0.5, 3.5)
    layout_output_bias = noise(keys[27], (DL,), 0.3, 2.5)
    layout_attend_gain = jnp.clip(1.0 + 0.15 * jax.random.normal(keys[28], (DL,), jnp.float32), 0.25, 1.75).astype(jnp.bfloat16)
    layout_attend_shift = noise(keys[29], (DL,), 0.3, 2.5)
    layout_up_weight = noise(keys[30], (DL, FFL), DL ** -0.5, 0.4375, ((1, 4),))
    layout_up_bias = noise(keys[31], (FFL,), 0.3, 2.5, ((0, 4),))
    layout_down_weight = noise(keys[32], (FFL, DL), FFL ** -0.5, 0.21875, ((0, 4),))
    layout_down_bias = noise(keys[33], (DL,), 0.3, 2.5)
    layout_feed_gain = jnp.clip(1.0 + 0.15 * jax.random.normal(keys[34], (DL,), jnp.float32), 0.25, 1.75).astype(jnp.bfloat16)
    layout_feed_shift = noise(keys[35], (DL,), 0.3, 2.5)
    return {"text_in": text_in, "layout_in": layout_in, "token_mask": token_mask, "box_mask": box_mask, "cot_text": cot_text, "cot_layout": cot_layout, "text_query_weight": text_query_weight, "text_query_bias": text_query_bias, "text_key_weight": text_key_weight, "text_value_weight": text_value_weight, "text_value_bias": text_value_bias, "text_output_weight": text_output_weight, "text_output_bias": text_output_bias, "text_attend_gain": text_attend_gain, "text_attend_shift": text_attend_shift, "text_up_weight": text_up_weight, "text_up_bias": text_up_bias, "text_down_weight": text_down_weight, "text_down_bias": text_down_bias, "text_feed_gain": text_feed_gain, "text_feed_shift": text_feed_shift, "layout_query_weight": layout_query_weight, "layout_query_bias": layout_query_bias, "layout_key_weight": layout_key_weight, "layout_value_weight": layout_value_weight, "layout_value_bias": layout_value_bias, "layout_output_weight": layout_output_weight, "layout_output_bias": layout_output_bias, "layout_attend_gain": layout_attend_gain, "layout_attend_shift": layout_attend_shift, "layout_up_weight": layout_up_weight, "layout_up_bias": layout_up_bias, "layout_down_weight": layout_down_weight, "layout_down_bias": layout_down_bias, "layout_feed_gain": layout_feed_gain, "layout_feed_shift": layout_feed_shift}


@jax.custom_vjp
def low(v):
    return lax.optimization_barrier(v.astype(jnp.bfloat16)).astype(jnp.float32)

@jax.custom_vjp
def low_back(v):
    return v

def low_keep(v):
    return (low(v), None)

def low_pass(kept, grad):
    return (grad,)

def back_keep(v):
    return (v, None)

def back_low(kept, grad):
    return (low(grad),)
low.defvjp(low_keep, low_pass)
low_back.defvjp(back_keep, back_low)
NORM_EPS = 1e-05
HIGHEST = lax.Precision.HIGHEST
SUFFIXES = ('query_weight', 'query_bias', 'key_weight', 'value_weight', 'value_bias', 'output_weight', 'output_bias', 'attend_gain', 'attend_shift', 'up_weight', 'up_bias', 'down_weight', 'down_bias', 'feed_gain', 'feed_shift')

def product_full(first, second):
    return jnp.dot(first, second, precision=HIGHEST)

def round_both(values):
    return low_back(low(values))

def norm_rows(values, gain, shift):
    average = lax.optimization_barrier(jnp.mean(values, axis=-1, keepdims=True))
    centered = values - average
    variance = lax.optimization_barrier(jnp.mean(centered * centered, axis=-1, keepdims=True))
    return centered * lax.rsqrt(variance + NORM_EPS) * gain + shift

def by_page(matrix):
    page_count = matrix.shape[0] // PAGE
    return matrix.reshape(page_count, PAGE, HEADS, matrix.shape[1] // HEADS)

def scores_of(queries, key_rows):
    factor = queries.shape[-1] ** (-0.5)
    return jnp.einsum('bqhd,bkhd->bhqk', queries, key_rows, precision=HIGHEST) * factor

def context_of(weights, values):
    merged = jnp.einsum('bhqk,bkhd->bqhd', weights, values, precision=HIGHEST)
    return merged.reshape(merged.shape[0] * merged.shape[1], merged.shape[2] * merged.shape[3])

def stream_tail(params, prefix, inputs, context):
    mixing = low_back(product_full(context, params[prefix + 'output_weight']) + params[prefix + 'output_bias'])
    hidden = norm_rows(inputs + mixing, params[prefix + 'attend_gain'], params[prefix + 'attend_shift'])
    preact = low_back(product_full(low(hidden), params[prefix + 'up_weight']) + params[prefix + 'up_bias'])
    active = low(jax.nn.gelu(preact))
    feed_out = low_back(product_full(active, params[prefix + 'down_weight']) + params[prefix + 'down_bias'])
    return norm_rows(hidden + feed_out, params[prefix + 'feed_gain'], params[prefix + 'feed_shift'])

def block_layer(params, frozen, text_rows, layout_rows, twin_rows):
    text_queries = round_both(product_full(text_rows, params['text_query_weight']) + params['text_query_bias'])
    text_keys = round_both(product_full(text_rows, params['text_key_weight']))
    text_values = round_both(product_full(text_rows, params['text_value_weight']) + params['text_value_bias'])
    layout_queries = round_both(product_full(layout_rows, params['layout_query_weight']) + params['layout_query_bias'])
    layout_keys = round_both(product_full(layout_rows, params['layout_key_weight']))
    layout_values = round_both(product_full(layout_rows, params['layout_value_weight']) + params['layout_value_bias'])
    frozen_queries = low(product_full(twin_rows, frozen['text_query_weight']) + frozen['text_query_bias'])
    frozen_keys = low(product_full(twin_rows, frozen['text_key_weight']))
    text_scores = low_back(scores_of(by_page(text_queries), by_page(text_keys)))
    layout_scores = low_back(scores_of(by_page(layout_queries), by_page(layout_keys)))
    frozen_scores = scores_of(by_page(frozen_queries), by_page(frozen_keys))
    text_weights = low(jax.nn.softmax(text_scores + layout_scores, axis=-1))
    layout_weights = low(jax.nn.softmax(layout_scores + frozen_scores, axis=-1))
    text_context = round_both(context_of(text_weights, by_page(text_values)))
    layout_context = round_both(context_of(layout_weights, by_page(layout_values)))
    return (stream_tail(params, 'text_', text_rows, text_context), stream_tail(params, 'layout_', layout_rows, layout_context))

def whole_layer(params, frozen, text_all, layout_all, twin_all):
    page_total = text_all.shape[0] // PAGE
    per_block = math.gcd(page_total, 8)
    block_count = page_total // per_block
    block_rows = per_block * PAGE

    def advance(carried, blocks):
        results = jax.checkpoint(block_layer)(params, frozen, blocks[0], blocks[1], blocks[2])
        return (carried, results)
    blocks = (text_all.reshape(block_count, block_rows, text_all.shape[1]), layout_all.reshape(block_count, block_rows, layout_all.shape[1]), twin_all.reshape(block_count, block_rows, twin_all.shape[1]))
    _, (text_out, layout_out) = lax.scan(advance, jnp.zeros((), jnp.float32), blocks)
    return (text_out.reshape(text_all.shape), layout_out.reshape(layout_all.shape))

def reference(text_in, layout_in, token_mask, box_mask, cot_text, cot_layout, text_query_weight, text_query_bias, text_key_weight, text_value_weight, text_value_bias, text_output_weight, text_output_bias, text_attend_gain, text_attend_shift, text_up_weight, text_up_bias, text_down_weight, text_down_bias, text_feed_gain, text_feed_shift, layout_query_weight, layout_query_bias, layout_key_weight, layout_value_weight, layout_value_bias, layout_output_weight, layout_output_bias, layout_attend_gain, layout_attend_shift, layout_up_weight, layout_up_bias, layout_down_weight, layout_down_bias, layout_feed_gain, layout_feed_shift):
    weights = (text_query_weight, text_query_bias, text_key_weight, text_value_weight, text_value_bias, text_output_weight, text_output_bias, text_attend_gain, text_attend_shift, text_up_weight, text_up_bias, text_down_weight, text_down_bias, text_feed_gain, text_feed_shift, layout_query_weight, layout_query_bias, layout_key_weight, layout_value_weight, layout_value_bias, layout_output_weight, layout_output_bias, layout_attend_gain, layout_attend_shift, layout_up_weight, layout_up_bias, layout_down_weight, layout_down_bias, layout_feed_gain, layout_feed_shift)
    labels = [prefix + suffix for prefix in ('text_', 'layout_') for suffix in SUFFIXES]
    params = dict(zip(labels, [weight.astype(jnp.float32) for weight in weights]))
    frozen = {'text_query_weight': text_query_weight.astype(jnp.float32), 'text_query_bias': text_query_bias.astype(jnp.float32), 'text_key_weight': text_key_weight.astype(jnp.float32)}
    text_float = text_in.astype(jnp.float32)
    layout_float = layout_in.astype(jnp.float32)
    (text_out, layout_out), backward = jax.vjp(whole_layer, params, frozen, text_float, layout_float, text_float)
    text_cot = cot_text.astype(jnp.float32) * (0.5 + 1.5 * token_mask.astype(jnp.float32))[:, None]
    layout_cot = cot_layout.astype(jnp.float32) * (0.5 + 1.5 * box_mask.astype(jnp.float32))[:, None]
    grad_params, _, text_grad, layout_grad, _ = backward((text_cot, layout_cot))
    return (text_out.astype(jnp.bfloat16), layout_out.astype(jnp.bfloat16), text_grad, layout_grad, grad_params['text_query_weight'], grad_params['text_query_bias'], grad_params['text_key_weight'], grad_params['text_value_weight'], grad_params['text_value_bias'], grad_params['text_output_weight'], grad_params['text_output_bias'], grad_params['text_attend_gain'], grad_params['text_attend_shift'], grad_params['text_up_weight'], grad_params['text_up_bias'], grad_params['text_down_weight'], grad_params['text_down_bias'], grad_params['text_feed_gain'], grad_params['text_feed_shift'], grad_params['layout_query_weight'], grad_params['layout_query_bias'], grad_params['layout_key_weight'], grad_params['layout_value_weight'], grad_params['layout_value_bias'], grad_params['layout_output_weight'], grad_params['layout_output_bias'], grad_params['layout_attend_gain'], grad_params['layout_attend_shift'], grad_params['layout_up_weight'], grad_params['layout_up_bias'], grad_params['layout_down_weight'], grad_params['layout_down_bias'], grad_params['layout_feed_gain'], grad_params['layout_feed_shift'])
```

```python
import functools

import jax
import jax.numpy as jnp
from jax import lax
from jax.experimental import pallas as pl
from jax.experimental.pallas import tpu as pltpu
from jax.sharding import PartitionSpec as P

HEADS = 12
PAGE = 512
NORM_EPS = 1e-05
MESH = pl.DeviceIdType.MESH
F32 = jnp.float32
BF16 = jnp.bfloat16
TILE = 256
ROWS = 64


def low(values):
    return values.astype(BF16)


def dot(first, second):
    return jnp.dot(first, second, preferred_element_type=F32)


def dot_nt(first, second):
    return lax.dot_general(first, second, (((1,), (1,)), ((), ())), preferred_element_type=F32)


def tile(index, size=TILE):
    return pl.ds(pl.multiple_of(index * size, size), size)


def loop(count, body):
    def step(index, carry):
        body(index)
        return carry

    lax.fori_loop(0, count, step, 0)


def flip(bit):
    return 1 - 2 * bit


def wide(vector_ref):
    return vector_ref[...].astype(F32)[None, :]


def lane_mean(values):
    return jnp.mean(values, axis=-1, keepdims=True)


def row_sum(values):
    return jnp.sum(values, axis=0, keepdims=True)


def normed(values):
    centered = values - lane_mean(values)
    scale = lax.rsqrt(lane_mean(centered * centered) + NORM_EPS)
    return centered * scale, scale


def normed_back(unit, scale, grad):
    return (grad - lane_mean(grad) - unit * lane_mean(grad * unit)) * scale


def padded(rows, unit):
    return -(-rows // unit) * unit


def landing(rows, stages):
    total = 0
    for _ in range(stages):
        rows = rows // 2 if rows % 32 == 0 else rows
        total += rows
    return total


def copy_to(source, target, send, recv, device):
    return pltpu.make_async_remote_copy(
        src_ref=source,
        dst_ref=target,
        send_sem=send,
        recv_sem=recv,
        device_id=device,
        device_id_type=MESH,
    )


def greet(devices):
    barrier = pltpu.get_barrier_semaphore()
    for device in devices:
        pl.semaphore_signal(barrier, inc=1, device_id=device, device_id_type=MESH)
    pl.semaphore_wait(barrier, len(devices))


def mask_column(mask_ref, column_ref):
    scale = 0.5 + 1.5 * mask_ref[...].astype(F32)
    column_ref[...] = jnp.transpose(jnp.broadcast_to(scale, (8, PAGE)))


def head_rows(target, text_rows, layout_rows, pair, side):
    head = 2 * pair + side
    target[side, 128:256, :] = jnp.zeros((128, PAGE), BF16)
    target[side, side * 64 : side * 64 + 64, :] = text_rows[tile(head, 64), :]
    spot = pl.ds(pl.multiple_of(128 + (head % 8) * 16, 16), 16)
    target[side, spot, :] = layout_rows[tile(head, 16), :]


def forward_kernel(shapes, *refs):
    (
        x_ref,
        lx_t_ref,
        token_mask,
        box_mask,
        cot_ref,
        lcot_ref,
        wq,
        bq,
        wk,
        wv,
        bv,
        wo,
        bo,
        attend_gain,
        attend_shift,
        up_hbm,
        up_bias,
        down_hbm,
        down_bias,
        feed_gain,
        feed_shift,
        lwq,
        lbq,
        lwk,
        lwv,
        lbv,
        lwo,
        lbo,
        lattend_gain,
        lattend_shift,
        lup,
        lup_bias,
        ldown,
        ldown_bias,
        lfeed_gain,
        lfeed_shift,
        out_ref,
        lout_ref,
        qn,
        kn,
        vn,
        q_t,
        lqn,
        lkn,
        lvn,
        lq_t,
        lse,
        ctx_t,
        lctx_t,
        asum,
        lasum,
        hidden_grad,
        lhidden_grad,
        grads_up,
        grads_down,
        vec,
        wu,
        wd,
        small,
        small_bias,
        v_t,
        lv_t,
        masked,
        ctx,
        lctx,
        hid,
        lhid,
        hlow,
        lhlow,
        h_t,
        lh_t,
        feed,
        lfeed,
        act,
        lact,
        slope,
        lslope,
        fgrad,
        lfgrad,
        pgrad,
        column,
        lcolumn,
        rises,
        lx,
        lcot,
        lout,
        local_sem,
        send_sem,
        recv_sem,
    ) = refs
    up_rows, down_rows = shapes
    d, me = lax.axis_index("dp"), lax.axis_index("tensor")
    c, x, y = me % 2, me // 2, d % 2
    width, lwidth = x_ref.shape[1], lx_t_ref.shape[0]
    core = (d, me + flip(c))
    across = (d, me + 2 * flip(x))
    beside = (d + flip(y), me)
    other = me + 2 * flip(x)
    half = width // 2
    mine = pl.ds(pl.multiple_of(y * half, half), half)

    small[me, 0:lwidth, 0:lwidth] = lup[...]
    small[me, lwidth : 2 * lwidth, 0:lwidth] = ldown[...]
    for j in range(width // TILE):
        small_bias[me, j : j + 1, :] = wide(up_bias)[:, j * TILE : (j + 1) * TILE]
    small_bias[me, 3:4, 0:lwidth] = wide(lup_bias)

    keep_up = pltpu.make_async_copy(up_hbm, wu.at[me], local_sem.at[0])
    keep_down = pltpu.make_async_copy(down_hbm, wd.at[me], local_sem.at[1])
    keep_up.start()
    keep_down.start()
    greet((core, across, beside))

    def send(index, source, target, device):
        return copy_to(source, target, send_sem.at[index], recv_sem.at[index], device)

    copies = [
        send(0, up_hbm.at[mine], wu.at[me, mine], across),
        send(1, small.at[me], small.at[me], across),
        send(2, small_bias.at[me], small_bias.at[me], across),
        send(3, up_hbm, wu.at[me], core),
        send(4, small.at[me], small.at[me], core),
        send(5, small_bias.at[me], small_bias.at[me], core),
        send(6, down_hbm.at[mine], wd.at[me, mine], across),
        send(7, down_hbm, wd.at[me], core),
        send(8, wu.at[other, mine], wu.at[other, mine], beside),
        send(9, wu.at[other, mine], wu.at[other, mine], core),
        send(10, small.at[other], small.at[other], core),
        send(11, small_bias.at[other], small_bias.at[other], core),
        send(12, wd.at[other, mine], wd.at[other, mine], beside),
        send(13, wd.at[other, mine], wd.at[other, mine], core),
    ]
    rest = pl.ds(pl.multiple_of((1 - y) * half, half), half)
    copies += [
        send(14, wu.at[other, rest], wu.at[other, rest], core),
        send(15, wd.at[other, rest], wd.at[other, rest], core),
    ]
    for copy in copies[:8]:
        copy.start()

    lx[...] = jnp.transpose(lx_t_ref[...])
    lcot[...] = jnp.transpose(lcot_ref[...])
    mask_column(token_mask, column)
    mask_column(box_mask, lcolumn)
    masked[...] = jnp.zeros_like(masked)
    vec[...] = jnp.zeros_like(vec)

    rises[0:1, :] = wide(bq)
    rises[1:2, :] = wide(bv)
    rises[2:3, :] = wide(bo)

    def project(j):
        cols = tile(j)
        rows = x_ref[...]
        queries = low(dot(rows, wq[:, cols]) + rises[0:1, cols]) * 0.125
        qn[:, cols] = queries
        q_t[cols, :] = jnp.transpose(queries)
        kn[:, cols] = low(dot(rows, wk[:, cols]))
        values = low(dot(rows, wv[:, cols]) + rises[1:2, cols])
        vn[:, cols] = values
        v_t[cols, :] = jnp.transpose(values)

    loop(width // TILE, project)
    pad = jnp.zeros((PAGE, 256 - lwidth), BF16)
    rows = lx[...]
    queries = low(dot(rows, lwq[...]) + wide(lbq)) * 0.25
    queries = jnp.concatenate([queries, pad], axis=1)
    lqn[...] = queries
    lq_t[...] = jnp.transpose(queries)
    lkn[...] = jnp.concatenate([low(dot(rows, lwk[...])), pad], axis=1)
    values = low(dot(rows, lwv[...]) + wide(lbv))
    values = jnp.concatenate([values, pad], axis=1)
    lvn[...] = values
    lv_t[...] = jnp.transpose(values)
    lctx_t[...] = jnp.zeros_like(lctx_t)

    def attend(pair):
        keys = jnp.concatenate([kn[:, tile(pair, 128)], lkn[:, tile(pair // 4, 128)]], axis=1)
        for side in range(2):
            head = 2 * pair + side
            head_rows(masked, q_t, lq_t, pair, side)
            joint = dot(keys, masked[side])
            highest = jnp.max(joint, axis=0, keepdims=True)
            exponent = jnp.exp(joint - highest)
            totals = row_sum(exponent)
            weights = low(exponent * (1.0 / totals))
            lse[pl.ds(head, 1), :] = highest + jnp.log(totals)
            values = jnp.concatenate([v_t[tile(head, 64), :], lv_t[tile(head, 16), :]], axis=0)
            context = low(dot(values, weights))
            ctx_t[tile(head, 64), :] = context[0:64]
            lctx_t[tile(head, 16), :] = context[64:80]

    loop(HEADS // 2, attend)
    copies[0].wait_recv()
    copies[8].start()
    copies[9].start()
    copies[1].wait_recv()
    copies[2].wait_recv()
    copies[10].start()
    copies[11].start()

    def untranspose(j):
        ctx[:, tile(j)] = jnp.transpose(ctx_t[tile(j), :])

    loop(width // TILE, untranspose)
    lctx[...] = jnp.transpose(lctx_t[...])

    def mix(j):
        cols = tile(j)
        asum[:, cols] = (
            x_ref[:, cols].astype(F32) + dot(ctx[...], wo[:, cols]) + rises[2:3, cols]
        )

    loop(width // TILE, mix)
    lasum[...] = lx[...].astype(F32) + dot(lctx[:, 0:lwidth], lwo[...]) + wide(lbo)

    def first_norm(source, gain, shift, hidden, hidden_low):
        gain, shift = wide(gain), wide(shift)

        def rows_of(i):
            r = tile(i, ROWS)
            unit, _ = normed(source[r, :])
            value = unit * gain + shift
            hidden[r, :] = value
            hidden_low[r, :] = low(value)

        loop(PAGE // ROWS, rows_of)

    first_norm(asum, attend_gain, attend_shift, hid, hlow)
    first_norm(lasum, lattend_gain, lattend_shift, lhid, lhlow)
    h_t[...] = jnp.transpose(hlow[...])
    lh_t[...] = jnp.transpose(lhlow[...])
    feed[...] = jnp.zeros_like(feed)
    lfeed[...] = jnp.zeros_like(lfeed)

    def shard_at(s):
        return (x + s // 2 - 2 * x * (s // 2)) * 2 + c + s % 2 - 2 * c * (s % 2)

    def gelu(u):
        square = u * u
        inner = 0.7978845608028654 * (u + 0.044715 * (square * u))
        wave = jnp.tanh(inner)
        rise = 0.5 * (1.0 + wave)
        bend = 0.5 * u * (1.0 - wave * wave)
        grow = 0.7978845608028654 * (1.0 + 0.134145 * square)
        return u * rise, rise + bend * grow

    def feed_forward(s):
        t = shard_at(s)

        @pl.when(s == 0)
        def _():
            keep_up.wait()
            keep_down.wait()

        @pl.when(s == 1)
        def _():
            for index in (3, 4, 5, 7):
                copies[index].wait_recv()

        @pl.when(s == 2)
        def _():
            copies[6].wait_recv()
            copies[12].start()
            copies[13].start()
            copies[8].wait_recv()
            copies[14].start()
            copies[12].wait_recv()
            copies[15].start()

        @pl.when(s == 3)
        def _():
            for index in (9, 10, 11, 13, 14, 15):
                copies[index].wait_recv()

        def up(j):
            cols = tile(j)
            preact = dot(hlow[...], wu[t, :, cols]) + small_bias[t, pl.ds(j, 1), :]
            value, gradient = gelu(preact)
            act[s, :, cols] = low(value)
            slope[s, :, cols] = low(gradient)

        loop(width // TILE, up)

        def down(j):
            cols = tile(j)
            feed[:, cols] += dot(act[s], wd[t, :, cols])

        loop(width // TILE, down)
        preact = dot(lhlow[...], small[t, 0:lwidth, 0:lwidth]) + small_bias[t, 3:4, 0:lwidth]
        value, gradient = gelu(preact)
        lact[s] = low(value)
        lslope[s] = low(gradient)
        lfeed[...] += dot(lact[s], small[t, lwidth : 2 * lwidth, 0:lwidth])

    loop(4, feed_forward)

    def second_norm(hidden, fed, bias, gain, shift, cot, scale, out, grad, grad_low):
        bias, gain, shift = wide(bias), wide(gain), wide(shift)

        def rows_of(i, sums):
            r = tile(i, ROWS)
            unit, spread = normed(hidden[r, :] + fed[r, :] + bias)
            out[r, :] = low(unit * gain + shift)
            outer = cot[r, :].astype(F32) * scale[r, 0:1]
            value = normed_back(unit, spread, outer * gain)
            grad[r, :] = value
            rounded = low(value)
            grad_low[r, :] = rounded
            return (
                sums[0] + row_sum(outer * unit),
                sums[1] + row_sum(outer),
                sums[2] + row_sum(rounded.astype(F32)),
            )

        zero = jnp.zeros((1, hidden.shape[1]), F32)
        return lax.fori_loop(0, PAGE // ROWS, rows_of, (zero, zero, zero))

    sums = second_norm(
        hid,
        feed,
        down_bias,
        feed_gain,
        feed_shift,
        cot_ref,
        column,
        out_ref,
        hidden_grad,
        fgrad,
    )
    for i in range(3):
        vec[i : i + 1, :] = sums[i]
    sums = second_norm(
        lhid,
        lfeed,
        ldown_bias,
        lfeed_gain,
        lfeed_shift,
        lcot,
        lcolumn,
        lout,
        lhidden_grad,
        lfgrad,
    )
    lout_ref[...] = jnp.transpose(lout[...])
    for i in range(3):
        vec[7:8, i * 256 : i * 256 + lwidth] = sums[i]

    down_half = down_rows // 2

    def up_place(t):
        return ((t % 2) * 2 + t // 2) * up_rows

    def down_place(t, piece):
        row = piece * 64
        return (
            (t % 2) * 2 * down_rows
            + (row // down_half) * down_rows
            + (t // 2) * down_half
            + row % down_half
        )

    def put_down(t, piece, cols, value):
        spot = pl.ds(pl.multiple_of(down_place(t, piece), 16), 64)
        grads_down[spot, cols] = value

    def feed_backward(s):
        t = shard_at(s)

        def hidden_units(j):
            cols = tile(j)
            active_grad = dot_nt(fgrad[...], wd[t, cols, :])
            value = active_grad * slope[s, :, cols].astype(F32)
            rounded = low(value)
            pgrad[:, cols] = rounded
            vec[pl.ds(3 + t, 1), cols] = row_sum(rounded.astype(F32))
            block = low(dot(jnp.transpose(act[s, :, cols]), fgrad[...]))
            for q in range(TILE // 64):
                put_down(t, j * (TILE // 64) + q, slice(None), block[q * 64 : q * 64 + 64])
            place = pl.ds(pl.multiple_of(up_place(t), 16), width)
            grads_up[place, cols] = low(dot(h_t[...], rounded))

        loop(width // TILE, hidden_units)

        def back(j):
            cols = tile(j)
            hidden_grad[:, cols] += dot_nt(pgrad[...], wu[t, cols, :])

        loop(width // TILE, back)

        active_grad = dot_nt(lfgrad[...], small[t, lwidth : 2 * lwidth, 0:lwidth])
        rounded = low(active_grad * lslope[s].astype(F32))
        spots = ((8, 0), (8, 256), (8, 512), (9, 0))
        for k, (row, lane) in enumerate(spots):

            @pl.when(t == k)
            def _():
                vec[row : row + 1, lane : lane + lwidth] = row_sum(rounded.astype(F32))

        lhidden_grad[...] += dot_nt(rounded, small[t, 0:lwidth, 0:lwidth])
        up_block = low(dot(lh_t[...], rounded))
        down_block = low(dot(jnp.transpose(lact[s]), lfgrad[...]))
        empty = jnp.zeros((64, 256 - lwidth), BF16)
        for which, block in enumerate((up_block, down_block)):
            for q in range(lwidth // 64):
                piece = jnp.concatenate([block[q * 64 : q * 64 + 64], empty], axis=1)
                put_down(t, width // 64 + which, slice(q * 256, q * 256 + 256), piece)

    loop(4, feed_backward)
    for copy in copies:
        copy.wait_send()


class Flow:
    def __init__(self, where, rows, axes, spread, source, base, work, recv, whole, sems):
        self.where, self.rows, self.axes, self.spread = where, rows, axes, spread
        self.source, self.base, self.work, self.recv = source, base, work, recv
        self.whole = whole
        self.halved = []
        for axis in axes:
            if rows % 32 == 0:
                rows //= 2
                self.halved.append(axis)
        self.send_sem, self.recv_sem, self.first = sems
        self.offset, self.size, self.stage = 0, self.rows, 0
        self.place, self.pending, self.sent = 0, None, []
        self.gathers = None

    def span(self, ref, offset, size):
        return ref.at[pl.ds(pl.multiple_of(offset, 16), size)]

    def launch(self, source, target, device):
        index = self.first + len(self.sent)
        copy = copy_to(source, target, self.send_sem.at[index], self.recv_sem.at[index], device)
        copy.start()
        self.sent.append(copy)
        return copy

    def scatter(self):
        bit, device = self.where[self.axes[self.stage]]
        if self.axes[self.stage] in self.halved:
            half = self.size // 2
            kept, given = self.offset + bit * half, self.offset + (1 - bit) * half
        else:
            half, kept, given = self.size, self.offset, self.offset
        outside = self.stage == 0 and self.source is not None
        origin = self.source if outside else self.work
        base = 0 if outside else self.base
        target = self.recv.at[pl.ds(self.place, half)]
        copy = self.launch(self.span(origin, base + given, half), target, device)
        if outside:
            kept = 0
        self.pending = (copy, kept, half)

    def absorb(self):
        copy, kept, half = self.pending
        copy.wait_recv()
        if half == self.size:
            copy.wait_send()
            self.sent[-1] = None
        block = max(b for b in range(16, 129, 16) if half % b == 0)
        place = self.place
        target, start = self.work, self.base + kept
        if self.stage + 1 == len(self.axes):
            target, start = self.whole, 0
            whole = self.whole.shape[0]
            self.gathers = []
            for axis in [a for a in self.spread if a in self.halved]:
                whole //= 2
                bit, _ = self.where[axis]
                start = start + bit * whole
                self.gathers.insert(0, (axis, whole))
            self.spot = start

        def add(i):
            mine = pl.ds(pl.multiple_of(self.base + kept + i * block, 16), block)
            theirs = pl.ds(pl.multiple_of(place + i * block, 16), block)
            result = pl.ds(pl.multiple_of(start + i * block, 16), block)
            target[result, :] = self.work[mine, :] + self.recv[theirs, :]

        loop(half // block, add)
        self.place += half
        self.offset, self.size = kept, half
        self.stage += 1

    def gather(self):
        axis, half = self.gathers.pop(0)
        bit, device = self.where[axis]
        span = self.span(self.whole, self.spot, half)
        copy = self.launch(span, span, device)
        self.pending = (copy, bit, half)

    def advance(self):
        if self.gathers is None:
            if self.stage > 0 or self.pending is not None:
                self.absorb()
            if self.stage < len(self.axes):
                self.scatter()
            else:
                self.gather()
            return
        if self.pending is None:
            return
        copy, bit, half = self.pending
        copy.wait_recv()
        self.pending = None
        self.spot = self.spot - bit * half
        if self.gathers:
            self.gather()

    def done(self):
        return self.gathers is not None and self.pending is None

    def drain(self):
        for copy in self.sent:
            if copy is not None:
                copy.wait_send()


def backward_kernel(plan, *refs):
    (
        x_ref,
        lx_t,
        wq,
        wk,
        wv,
        wo,
        attend_gain,
        lwq,
        lwk,
        lwv,
        lwo,
        lattend_gain,
        qn,
        kn,
        vn,
        q_t,
        lqn,
        lkn,
        lvn,
        lq_t,
        lse,
        ctx_t,
        lctx_t,
        asum,
        lasum,
        hidden_grad,
        lhidden_grad,
        up_hbm,
        down_hbm,
        vec_in,
        in_grad,
        lin_grad,
        up_out,
        down_out,
        shared_out,
        acc_up,
        acc_down,
        recv_up,
        recv_down,
        shared,
        recv_shared,
        sum_up,
        sum_down,
        sum_shared,
        mixed,
        lmixed,
        cgrad,
        cgrad_t,
        lcgrad,
        lcgrad_t,
        k_t,
        lk_t,
        x_t,
        lin,
        masked_q,
        masked_c,
        ldq_t,
        dq,
        dk,
        dv,
        ldq,
        ldk,
        ldv,
        vec,
        local_sem,
        send_sem,
        recv_sem,
    ) = refs
    dp_bits, up_rows, down_rows, shared_flows = plan
    d, me = lax.axis_index("dp"), lax.axis_index("tensor")
    c, x = me % 2, me // 2
    width, lwidth = x_ref.shape[1], lx_t.shape[0]
    where = {"core": (c, (d, me + flip(c))), "x": (x, (d, me + 2 * flip(x)))}
    for k in range(dp_bits):
        bit = (d // 2**k) % 2
        where[k] = (bit, (d + 2**k * flip(bit), me))
    deep = list(range(1, dp_bits))
    x_first, x_later = ["core", "x", 0] + deep, ["core", 0, "x"] + deep
    steps = 2 * (dp_bits + 2)

    keep_up = pltpu.make_async_copy(
        up_hbm.at[pl.ds(pl.multiple_of(c * 2 * up_rows, 16), 2 * up_rows)],
        acc_up,
        local_sem.at[0],
    )
    keep_down = pltpu.make_async_copy(
        down_hbm.at[pl.ds(pl.multiple_of(c * 2 * down_rows, 16), 2 * down_rows)],
        acc_down,
        local_sem.at[1],
    )
    keep_up.start()
    keep_down.start()

    def flow(rows, axes, spread, source, base, work, recv, whole, number):
        sems = (send_sem, recv_sem, number * steps)
        return Flow(where, rows, axes, spread, source, base, work, recv, whole, sems)

    pages = [0] + deep
    up_flow = flow(4 * up_rows, x_first, pages, up_hbm, 0, acc_up, recv_up, sum_up, 0)
    down_flow = flow(
        4 * down_rows, x_later, pages, down_hbm, 0, acc_down, recv_down, sum_down, 1
    )
    shared_list = []
    spot = 0
    for i, (base, rows) in enumerate(shared_flows):
        axes = x_later if i % 2 else x_first
        size = landing(rows, len(axes))
        target, whole = recv_shared.at[pl.ds(spot, size)], sum_shared.at[pl.ds(base, rows)]
        spot += size
        shared_list.append(flow(rows, axes, axes, None, base, shared, target, whole, 2 + i))

    greet([device for _, device in where.values()])
    up_flow.advance()
    down_flow.advance()

    shared[pl.ds(4 * width, shared.shape[0] - 4 * width), :] = jnp.zeros(
        (shared.shape[0] - 4 * width, width), BF16
    )
    masked_q[...] = jnp.zeros_like(masked_q)
    masked_c[...] = jnp.zeros_like(masked_c)
    vec[...] = vec_in[...]

    def norm_grad(source, gain, grad, result, result_low):
        gain = wide(gain)

        def rows_of(i, sums):
            r = tile(i, ROWS)
            unit, spread = normed(source[r, :])
            outer = grad[r, :]
            value = normed_back(unit, spread, outer * gain)
            result[r, :] = value
            rounded = low(value)
            result_low[r, :] = rounded
            return (
                sums[0] + row_sum(rounded.astype(F32)),
                sums[1] + row_sum(outer * unit),
                sums[2] + row_sum(outer),
            )

        zero = jnp.zeros((1, source.shape[1]), F32)
        return lax.fori_loop(0, PAGE // ROWS, rows_of, (zero, zero, zero))

    sums = norm_grad(asum, attend_gain, hidden_grad, in_grad, mixed)
    for i in range(3):
        vec[12 + i : 13 + i, :] = sums[i]
    sums = norm_grad(lasum, lattend_gain, lhidden_grad, lin, lmixed)
    for i in range(3):
        vec[15:16, i * 256 : i * 256 + lwidth] = sums[i]

    def context_back(j):
        cols = tile(j)
        value = low(dot_nt(mixed[...], wo[cols, :]))
        cgrad[:, cols] = value
        cgrad_t[cols, :] = jnp.transpose(value)
        shared[3 * width : 4 * width, cols] = low(dot(ctx_t[...], mixed[:, cols]))
        k_t[cols, :] = jnp.transpose(kn[:, cols])
        x_t[cols, :] = jnp.transpose(x_ref[:, cols])

    loop(width // TILE, context_back)
    pad = jnp.zeros((PAGE, 256 - lwidth), BF16)
    value = jnp.concatenate([low(dot_nt(lmixed[...], lwo[...])), pad], axis=1)
    lcgrad[...] = value
    lcgrad_t[...] = jnp.transpose(value)
    lk_t[...] = jnp.transpose(lkn[...])
    empty = jnp.zeros((64, 256 - lwidth), BF16)

    def put_layout(index, block):
        base = 4 * width + 64 * index
        for q in range(lwidth // 64):
            piece = jnp.concatenate([block[q * 64 : q * 64 + 64], empty], axis=1)
            shared[base : base + 64, q * 256 : q * 256 + 256] = piece

    put_layout(3, low(dot(lctx_t[0:lwidth, :], lmixed[...])))

    keep_up.wait()
    keep_down.wait()
    up_flow.advance()
    down_flow.advance()

    lane = lax.broadcasted_iota(jnp.int32, (PAGE, 128), 1)

    def attend_back(pair):
        text, block = tile(pair, 128), tile(pair // 4, 128)
        keys = jnp.concatenate([kn[:, text], lkn[:, block]], axis=1)
        values = jnp.concatenate([vn[:, text], lvn[:, block]], axis=1)
        grads = jnp.concatenate([cgrad[:, text], lcgrad[:, block]], axis=1)
        found = []
        for side in range(2):
            head = 2 * pair + side
            head_rows(masked_q, q_t, lq_t, pair, side)
            head_rows(masked_c, cgrad_t, lcgrad_t, pair, side)
            weights = jnp.exp(dot(keys, masked_q[side]) - lse[pl.ds(head, 1), :])
            value_grad = dot(low(weights), grads)
            text_wave = dot(vn[:, text], masked_c[side, 0:128, :])
            text_part = row_sum(text_wave * weights)
            text_score = low(weights * (text_wave - text_part))
            both_wave = dot(values, masked_c[side])
            both_part = row_sum(both_wave * weights)
            both_score = low(weights * (both_wave - both_part))
            query_grad = low(dot(k_t[tile(head, 64), :], text_score) * 0.125)
            ldq_t[tile(head, 16), :] = low(dot(lk_t[tile(head, 16), :], both_score) * 0.25)
            key_grad = dot(text_score, qn[:, text])
            lkey_grad = dot(both_score, lqn[:, block])
            own = (lane // 16) == (head % 8)
            ldv[:, block] = jnp.where(own, value_grad[:, 128:256], ldv[:, block])
            ldk[:, block] = jnp.where(own, lkey_grad, ldk[:, block])
            found.append((value_grad[:, 0:128], key_grad, query_grad))
        first = lane < 64
        dv[:, text] = low(jnp.where(first, found[0][0], found[1][0]))
        dk[:, text] = low(jnp.where(first, found[0][1], found[1][1]))
        dq[:, text] = jnp.transpose(jnp.concatenate([found[0][2], found[1][2]], axis=0))

    ldv[...] = jnp.zeros_like(ldv)
    ldk[...] = jnp.zeros_like(ldk)
    ldq_t[...] = jnp.zeros_like(ldq_t)
    loop(HEADS // 2, attend_back)

    up_flow.advance()

    ldq[...] = jnp.transpose(ldq_t[...])

    def project_back(j):
        cols = tile(j)
        shared[0:width, cols] = low(dot(x_t[...], dq[:, cols]))
        shared[width : 2 * width, cols] = low(dot(x_t[...], dk[:, cols]))
        shared[2 * width : 3 * width, cols] = low(dot(x_t[...], dv[:, cols]))
        vec[10:11, cols] = row_sum(dq[:, cols].astype(F32))
        vec[11:12, cols] = row_sum(dv[:, cols].astype(F32))

    loop(width // TILE, project_back)
    query, key, value = ldq[:, 0:lwidth], low(ldk[:, 0:lwidth]), low(ldv[:, 0:lwidth])
    put_layout(0, low(dot(lx_t[...], query)))
    put_layout(1, low(dot(lx_t[...], key)))
    put_layout(2, low(dot(lx_t[...], value)))
    vec[9:10, 256 : 256 + lwidth] = row_sum(query.astype(F32))
    vec[9:10, 512 : 512 + lwidth] = row_sum(value.astype(F32))
    shared[4 * width + 256 : 4 * width + 272, :] = low(vec[...])

    for item in shared_list:
        item.advance()
    down_flow.advance()

    def input_back(j):
        cols = tile(j)
        in_grad[:, cols] += (
            dot_nt(dq[...], wq[cols, :])
            + dot_nt(dk[...], wk[cols, :])
            + dot_nt(dv[...], wv[cols, :])
        )

    loop(width // TILE, input_back)
    lin_grad[...] = jnp.transpose(
        lin[...] + dot_nt(query, lwq[...]) + dot_nt(key, lwk[...]) + dot_nt(value, lwv[...])
    )

    flows = shared_list + [up_flow, down_flow]
    while not all(item.done() for item in flows):
        for item in flows:
            item.advance()
    outs = [
        pltpu.make_async_copy(sum_up, up_out, local_sem.at[2]),
        pltpu.make_async_copy(sum_down, down_out, local_sem.at[3]),
        pltpu.make_async_copy(sum_shared, shared_out, local_sem.at[4]),
    ]
    for copy in outs:
        copy.start()
    for item in flows:
        item.drain()
    for copy in outs:
        copy.wait()


def on_device(dp, tensor, *args):
    (
        text_in,
        layout_in,
        token_mask,
        box_mask,
        cot_text,
        cot_layout,
    ) = args[:6]
    text, layout = args[6:21], args[21:36]
    width, lwidth = text_in.shape[1], layout_in.shape[1]
    dp_bits = dp.bit_length() - 1
    up_rows, down_rows = width, width + 128
    first, second = padded(2 * width, 512), padded(2 * width + 272, 512)
    shared_flows = ((0, first), (first, second))
    shared_total = first + second

    def row(vector):
        return vector.reshape(1, vector.shape[0])

    vmem = pl.BlockSpec(memory_space=pltpu.VMEM)
    hbm = pl.BlockSpec(memory_space=pl.ANY)
    page = PAGE

    def shape(*dims, dtype=BF16):
        return jax.ShapeDtypeStruct(dims, dtype)

    inputs = (text_in, layout_in.T, row(token_mask), row(box_mask), cot_text, cot_layout.T)
    inputs += text + layout
    specs = [vmem] * len(inputs)
    specs[15] = hbm
    specs[17] = hbm
    outs = (
        shape(page, width),
        shape(lwidth, page),
        shape(page, width),
        shape(page, width),
        shape(page, width),
        shape(width, page),
        shape(page, 256),
        shape(page, 256),
        shape(page, 256),
        shape(256, page),
        shape(16, page, dtype=F32),
        shape(width, page),
        shape(256, page),
        shape(page, width, dtype=F32),
        shape(page, lwidth, dtype=F32),
        shape(page, width, dtype=F32),
        shape(page, lwidth, dtype=F32),
        shape(4 * up_rows, width),
        shape(4 * down_rows, width),
        shape(16, width, dtype=F32),
    )
    scratch = [
        pltpu.VMEM((4, width, width), BF16),
        pltpu.VMEM((4, width, width), BF16),
        pltpu.VMEM((4, 2 * lwidth, 256), BF16),
        pltpu.VMEM((4, 8, 256), F32),
        pltpu.VMEM((width, page), BF16),
        pltpu.VMEM((256, page), BF16),
        pltpu.VMEM((2, 256, page), BF16),
        pltpu.VMEM((page, width), BF16),
        pltpu.VMEM((page, 256), BF16),
        pltpu.VMEM((page, width), F32),
        pltpu.VMEM((page, lwidth), F32),
        pltpu.VMEM((page, width), BF16),
        pltpu.VMEM((page, lwidth), BF16),
        pltpu.VMEM((width, page), BF16),
        pltpu.VMEM((lwidth, page), BF16),
        pltpu.VMEM((page, width), F32),
        pltpu.VMEM((page, lwidth), F32),
        pltpu.VMEM((4, page, width), BF16),
        pltpu.VMEM((4, page, lwidth), BF16),
        pltpu.VMEM((4, page, width), BF16),
        pltpu.VMEM((4, page, lwidth), BF16),
        pltpu.VMEM((page, width), BF16),
        pltpu.VMEM((page, lwidth), BF16),
        pltpu.VMEM((page, width), BF16),
        pltpu.VMEM((page, 8), F32),
        pltpu.VMEM((page, 8), F32),
        pltpu.VMEM((8, width), F32),
        pltpu.VMEM((page, lwidth), BF16),
        pltpu.VMEM((page, lwidth), BF16),
        pltpu.VMEM((page, lwidth), BF16),
        pltpu.SemaphoreType.DMA((2,)),
        pltpu.SemaphoreType.DMA((16,)),
        pltpu.SemaphoreType.DMA((16,)),
    ]
    made = pl.pallas_call(
        functools.partial(forward_kernel, (up_rows, down_rows)),
        out_shape=outs,
        in_specs=specs,
        out_specs=[vmem] * len(outs),
        scratch_shapes=scratch,
        compiler_params=pltpu.CompilerParams(
            collective_id=0, has_side_effects=True, vmem_limit_bytes=67043328
        ),
        name="attend_and_feed",
    )(*inputs)
    text_out, layout_out = made[:2]

    inputs = (text_in, layout_in.T)
    inputs += (text[0], text[2], text[3], text[5], text[7])
    inputs += (layout[0], layout[2], layout[3], layout[5], layout[7])
    inputs += tuple(made[2:])
    specs = [vmem] * len(inputs)
    specs[-3] = hbm
    specs[-2] = hbm
    outs = (
        shape(page, width, dtype=F32),
        shape(lwidth, page, dtype=F32),
        shape(up_rows, width),
        shape(down_rows, width),
        shape(shared_total, width),
    )
    count = 2 * (dp_bits + 2) * (2 + len(shared_flows))
    scratch = [
        pltpu.VMEM((2 * up_rows, width), BF16),
        pltpu.VMEM((2 * down_rows, width), BF16),
        pltpu.VMEM((landing(4 * up_rows, dp_bits + 2), width), BF16),
        pltpu.VMEM((landing(4 * down_rows, dp_bits + 2), width), BF16),
        pltpu.VMEM((shared_total, width), BF16),
        pltpu.VMEM((sum(landing(rows, dp_bits + 2) for _, rows in shared_flows), width), BF16),
        pltpu.VMEM((up_rows, width), BF16),
        pltpu.VMEM((down_rows, width), BF16),
        pltpu.VMEM((shared_total, width), BF16),
        pltpu.VMEM((page, width), BF16),
        pltpu.VMEM((page, lwidth), BF16),
        pltpu.VMEM((page, width), BF16),
        pltpu.VMEM((width, page), BF16),
        pltpu.VMEM((page, 256), BF16),
        pltpu.VMEM((256, page), BF16),
        pltpu.VMEM((width, page), BF16),
        pltpu.VMEM((256, page), BF16),
        pltpu.VMEM((width, page), BF16),
        pltpu.VMEM((page, lwidth), F32),
        pltpu.VMEM((2, 256, page), BF16),
        pltpu.VMEM((2, 256, page), BF16),
        pltpu.VMEM((256, page), BF16),
        pltpu.VMEM((page, width), BF16),
        pltpu.VMEM((page, width), BF16),
        pltpu.VMEM((page, width), BF16),
        pltpu.VMEM((page, 256), BF16),
        pltpu.VMEM((page, 256), F32),
        pltpu.VMEM((page, 256), F32),
        pltpu.VMEM((16, width), F32),
        pltpu.SemaphoreType.DMA((5,)),
        pltpu.SemaphoreType.DMA((count,)),
        pltpu.SemaphoreType.DMA((count,)),
    ]
    in_grad, lin_grad, up_sum, down_sum, shared = pl.pallas_call(
        functools.partial(backward_kernel, (dp_bits, up_rows, down_rows, shared_flows)),
        out_shape=outs,
        in_specs=specs,
        out_specs=[vmem, vmem, hbm, hbm, hbm],
        scratch_shapes=scratch,
        compiler_params=pltpu.CompilerParams(
            collective_id=1, has_side_effects=True, vmem_limit_bytes=67043328
        ),
        name="backward_and_reduce",
    )(*inputs)

    me = lax.axis_index("tensor")
    vec = shared[4 * width + 256 : 4 * width + 272].astype(F32)

    def square(index):
        return shared[index * width : (index + 1) * width].astype(F32)

    def unpack(block):
        parts = [block[:, q * 256 : q * 256 + lwidth] for q in range(lwidth // 64)]
        return jnp.concatenate(parts, axis=0).astype(F32)

    def layout_square(index):
        base = 4 * width + 64 * index
        return unpack(shared[base : base + 64])

    def strip(index, part):
        return vec[index, part * 256 : part * 256 + lwidth]

    up_bias = lax.dynamic_index_in_dim(vec, 3 + me, 0, keepdims=False)
    lup_bias = lax.dynamic_index_in_dim(
        jnp.stack([strip(8, 0), strip(8, 1), strip(8, 2), strip(9, 0)]), me, 0, keepdims=False
    )
    return (
        text_out,
        layout_out.T,
        in_grad,
        lin_grad.T,
        square(0),
        vec[10],
        square(1),
        square(2),
        vec[11],
        square(3),
        vec[12],
        vec[13],
        vec[14],
        up_sum[:width].astype(F32),
        up_bias,
        down_sum[:width].astype(F32),
        vec[2],
        vec[0],
        vec[1],
        layout_square(0),
        strip(9, 1),
        layout_square(1),
        layout_square(2),
        strip(9, 2),
        layout_square(3),
        strip(15, 0),
        strip(15, 1),
        strip(15, 2),
        unpack(down_sum[width : width + 64]),
        lup_bias,
        unpack(down_sum[width + 64 : width + 128]),
        strip(7, 2),
        strip(7, 0),
        strip(7, 1),
    )


def solution(mesh):
    rows = P(("dp", "tensor"), None)
    line = P(("dp", "tensor"))
    weights = (P(),) * 9 + (P(None, "tensor"), P("tensor"), P("tensor", None)) + (P(),) * 3
    in_specs = (rows, rows, line, line, rows, rows) + weights + weights
    out_specs = (rows,) * 4 + weights + weights
    return jax.shard_map(
        functools.partial(on_device, mesh.shape["dp"], mesh.shape["tensor"]),
        mesh=mesh,
        in_specs=in_specs,
        out_specs=out_specs,
        check_vma=False,
    )
```

```python
import functools

import jax
import jax.numpy as jnp
from jax import lax
from jax.experimental import pallas as pl
from jax.experimental.pallas import tpu as pltpu
from jax.sharding import PartitionSpec as P

HEADS = 12
PAGE = 512
NORM_EPS = 1e-05
MESH = pl.DeviceIdType.MESH
F32 = jnp.float32
BF16 = jnp.bfloat16
TILE = 256
ROWS = 64


def low(values):
    return values.astype(BF16)


def dot(first, second):
    return jnp.dot(first, second, preferred_element_type=F32)


def dot_nt(first, second):
    return lax.dot_general(first, second, (((1,), (1,)), ((), ())), preferred_element_type=F32)


def tile(index, size=TILE):
    return pl.ds(pl.multiple_of(index * size, size), size)


def loop(count, body):
    def step(index, carry):
        body(index)
        return carry

    lax.fori_loop(0, count, step, 0)


def flip(bit):
    return 1 - 2 * bit


def wide(vector_ref):
    return vector_ref[...].astype(F32)[None, :]


def lane_mean(values):
    return jnp.mean(values, axis=-1, keepdims=True)


def row_sum(values):
    return jnp.sum(values, axis=0, keepdims=True)


def normed(values):
    centered = values - lane_mean(values)
    scale = lax.rsqrt(lane_mean(centered * centered) + NORM_EPS)
    return centered * scale, scale


def normed_back(unit, scale, grad):
    return (grad - lane_mean(grad) - unit * lane_mean(grad * unit)) * scale


def landing(rows, stages):
    total = 0
    for stage in range(stages):
        rows = rows // 2 if rows % 32 == 0 and stage + 1 < stages else rows
        total += rows
    return total


def copy_to(source, target, send, recv, device):
    return pltpu.make_async_remote_copy(
        src_ref=source,
        dst_ref=target,
        send_sem=send,
        recv_sem=recv,
        device_id=device,
        device_id_type=MESH,
    )


def greet(devices):
    barrier = pltpu.get_barrier_semaphore()
    for device in devices:
        pl.semaphore_signal(barrier, inc=1, device_id=device, device_id_type=MESH)
    pl.semaphore_wait(barrier, len(devices))


def mask_column(text_mask, layout_mask, column_ref):
    parts = []
    for mask_ref in (text_mask, layout_mask):
        scale = 0.5 + 1.5 * mask_ref[...].astype(F32)
        parts.append(jnp.broadcast_to(scale, (8, PAGE)))
    column_ref[...] = jnp.transpose(jnp.concatenate(parts, axis=0))


def head_rows(target, text_rows, layout_rows, pair, side):
    head = 2 * pair + side
    top = side * 256
    target[top + 128 : top + 256, :] = jnp.zeros((128, PAGE), BF16)
    target[top + side * 64 : top + side * 64 + 64, :] = text_rows[tile(head, 64), :]
    spot = pl.ds(pl.multiple_of(top + 128 + (head % 8) * 16, 16), 16)
    target[spot, :] = layout_rows[tile(head, 16), :]


class Flow:
    def __init__(self, where, axes, spread, rows, give, keep, lands, whole, sems, ready):
        self.steps, self.ready = [], ready
        send_sem, recv_sem, index = sems
        offset, size, place = 0, rows, 0
        halved = []
        for stage, axis in enumerate(axes):
            bit, device = where[axis]
            recv = lands[min(stage, 1)]
            if stage == 1:
                place = 0
            if size % 32 == 0 and stage + 1 < len(axes):
                half = size // 2
                kept, given = offset + bit * half, offset + (1 - bit) * half
                halved.append(axis)
            else:
                half, kept, given = size, offset, offset
            first = stage == 0 and give is not keep
            source = give.at[pl.ds(0, half)] if first else self.span(keep, given, half)
            kept = 0 if first else kept
            copy = copy_to(
                source,
                recv.at[pl.ds(place, half)],
                send_sem.at[index],
                recv_sem.at[index],
                device,
            )
            last = stage + 1 == len(axes)
            target, start = keep, kept
            if last:
                target, start = whole, 0
                step, gathers = whole.shape[0], []
                for other in spread:
                    if other in halved:
                        step //= 2
                        start = start + where[other][0] * step
                        gathers.insert(0, (other, step))
            swap = half == size and not last
            self.steps.append((axis, copy, (keep, kept, recv, place, target, start, half, swap)))
            offset, size = kept, half
            place += half
            index += 1
        spot = start
        for axis, step in gathers:
            bit, device = where[axis]
            span = self.span(whole, spot, step)
            copy = copy_to(span, span, send_sem.at[index], recv_sem.at[index], device)
            self.steps.append((axis, copy, None))
            spot = spot - bit * step
            index += 1

    def span(self, ref, offset, size):
        return ref.at[pl.ds(pl.multiple_of(offset, 16), size)]

    def launch(self, step, waits):
        axis, copy, _ = self.steps[step]
        if waits:
            pl.semaphore_wait(self.ready[axis], 1)
        copy.start()

    def absorb(self, step):
        _, copy, rest = self.steps[step]
        copy.wait_recv()
        if rest is not None:
            keep, kept, recv, place, target, start, half, swap = rest
            if swap:
                copy.wait_send()
            block = max(b for b in range(16, 129, 16) if half % b == 0)

            def add(i):
                mine = pl.ds(pl.multiple_of(kept + i * block, 16), block)
                theirs = pl.ds(pl.multiple_of(place + i * block, 16), block)
                result = pl.ds(pl.multiple_of(start + i * block, 16), block)
                target[result, :] = keep[mine, :] + recv[theirs, :]

            loop(half // block, add)

    def drain(self):
        for _, copy, rest in self.steps[1 if self.ready is None else 0 :]:
            if rest is None or not rest[-1]:
                copy.wait_send()


class Script:
    def __init__(self, flows, greeted):
        self.flows, self.greeted = flows, greeted
        self.started, self.taken = [0] * len(flows), [0] * len(flows)
        self.points = {}

    def write(self, point, number):
        kind, flow = divmod(number, len(self.flows))
        done = self.started if kind else self.taken
        step = done[flow]
        done[flow] += 1
        waits = False
        if kind and self.flows[flow].ready is not None:
            axis = self.flows[flow].steps[step][0]
            waits = axis not in self.greeted
            self.greeted.add(axis)
        self.points.setdefault(point, []).append((kind, flow, step, waits))

    def play(self, point):
        for kind, flow, step, waits in self.points.get(point, ()):
            if kind:
                self.flows[flow].launch(step, waits)
            else:
                self.flows[flow].absorb(step)

    def finish(self, point):
        flows, going = self.flows, True
        while going:
            going = False
            for i, flow in enumerate(flows):
                if self.started[i] > self.taken[i]:
                    self.write(point, i)
                    going = True
                if self.started[i] == self.taken[i] and self.taken[i] < len(flow.steps):
                    self.write(point, len(flows) + i)
                    going = True


def layer_kernel(plan, *refs):
    (
        x_ref,
        lx_t,
        token_mask,
        box_mask,
        cot_ref,
        lcot_ref,
        wq_hbm,
        bq,
        wk_hbm,
        wv_hbm,
        bv,
        wo_hbm,
        bo,
        attend_gain,
        attend_shift,
        up_hbm,
        up_bias,
        down_hbm,
        down_bias,
        feed_gain,
        feed_shift,
        lwq,
        lbq,
        lwk,
        lwv,
        lbv,
        lwo,
        lbo,
        lattend_gain,
        lattend_shift,
        lup,
        lup_bias,
        ldown,
        ldown_bias,
        lfeed_gain,
        lfeed_shift,
        out_ref,
        lout_ref,
        in_grad_out,
        lin_grad,
        sums_out,
        pool,
        acc,
        staging,
        recv,
        sums,
        small,
        small_bias,
        qn,
        kn,
        vn,
        q_t,
        v_t,
        lqn,
        lkn,
        lvn,
        lq_t,
        lv_t,
        lse,
        masked,
        masked_c,
        ctx_t,
        lctx_t,
        lctx,
        asum,
        lasum,
        hlow,
        lhlow,
        h_t,
        lh_t,
        feed,
        lfeed,
        lact,
        lslope,
        column,
        rises,
        lx,
        lcot,
        lcgrad_t,
        ldq_t,
        ldk,
        ldv,
        vec,
        local_sem,
        gather_send,
        gather_recv,
        send_sem,
        recv_sem,
        ready_sem,
    ) = refs
    dp_bits, feed_flows, shared_flows, moves = plan
    fgrad, lfgrad, lout, turned = hlow, lhlow, lx, masked_c
    d, me = lax.axis_index("dp"), lax.axis_index("tensor")
    c, x = me % 2, me // 2
    width, lwidth = x_ref.shape[1], lx_t.shape[0]
    tiles = width // TILE
    where = {"core": (c, (d, me + flip(c))), "x": (x, (d, me + 2 * flip(x)))}
    for k in range(dp_bits):
        bit = (d // 2**k) % 2
        where[k] = (bit, (d + 2**k * flip(bit), me))
    core, across = where["core"][1], where["x"][1]
    y, beside = where[0]
    z, ahead = where[1]
    other = me + 2 * flip(x)

    def part(start, size):
        return pool.at[pl.ds(start, size)]

    wu, wd = part(0, 4 * width), part(4 * width, 4 * width)
    act_at, slope_at = 8 * width, 8 * width + 4 * PAGE
    wq, wk = part(act_at, width), part(act_at + width, width)
    wv, wo = part(act_at + 2 * width, width), part(act_at + 3 * width, width)
    ctx = part(act_at + 4 * width, PAGE)
    shared_rows = sum(rows for rows, _ in shared_flows)
    shared, shared_sum = part(0, shared_rows), part(shared_rows, shared_rows)
    spot = 2 * shared_rows
    dq, dk, dv = part(spot, PAGE), part(spot + PAGE, PAGE), part(spot + 2 * PAGE, PAGE)
    cgrad = part(spot + 3 * PAGE, PAGE)
    x_t = pool.at[pl.ds(spot + 4 * PAGE, width), pl.ds(0, PAGE)]

    def shard_rows(base, t, start=0, size=width):
        return pl.ds(pl.multiple_of(base + t * width + start, 16), size)

    small[me, 0:lwidth, 0:lwidth] = lup[...]
    small[me, lwidth : 2 * lwidth, 0:lwidth] = ldown[...]
    for j in range(tiles):
        small_bias[me, j : j + 1, :] = wide(up_bias)[:, j * TILE : (j + 1) * TILE]
    small_bias[me, 3:4, 0:lwidth] = wide(lup_bias)

    def load(index, source, target):
        copy = pltpu.make_async_copy(source, target, local_sem.at[index])
        copy.start()
        return copy

    loads = [load(i, s, t) for i, (s, t) in enumerate(((wq_hbm, wq), (wk_hbm, wk), (wv_hbm, wv)))]
    load_wo = load(3, wo_hbm, wo)
    keep_up = load(4, up_hbm, pool.at[shard_rows(0, me)])
    keep_down = load(5, down_hbm, pool.at[shard_rows(4 * width, me)])
    greet([device for _, device in where.values()])

    count = [0]

    def send(source, target, device):
        index = count[0]
        count[0] += 1
        return copy_to(source, target, gather_send.at[index], gather_recv.at[index], device)

    def relay(place, device):
        return send(pool.at[place], pool.at[place], device)

    quarter = width // 4
    first = {}
    y_at, z_at = y * quarter, 2 * quarter + z * quarter
    for name, base, hbm in (("up", 0, up_hbm), ("down", 4 * width, down_hbm)):
        for way, start in (("y", y_at), ("z", z_at)):
            source = hbm.at[pl.ds(pl.multiple_of(start, 16), quarter)]
            place = shard_rows(base, me, start, quarter)
            first[name, way] = send(source, pool.at[place], across)
    small_across = [send(ref.at[me], ref.at[me], across) for ref in (small, small_bias)]
    small_core = [send(ref.at[me], ref.at[me], core) for ref in (small, small_bias)]
    up_core = send(up_hbm, pool.at[shard_rows(0, me)], core)
    down_core = send(down_hbm, pool.at[shard_rows(4 * width, me)], core)
    small_relay = [send(ref.at[other], ref.at[other], core) for ref in (small, small_bias)]
    forward, pass_own, pass_got = {}, {}, {}
    for name, base in (("up", 0), ("down", 4 * width)):
        for way, start, rest, device in (
            ("y", y_at, (1 - y) * quarter, beside),
            ("z", z_at, 2 * quarter + (1 - z) * quarter, ahead),
        ):
            own = shard_rows(base, other, start, quarter)
            got = shard_rows(base, other, rest, quarter)
            forward[name, way] = relay(own, device)
            pass_own[name, way] = relay(own, core)
            pass_got[name, way] = relay(got, core)
    gather_all = (
        list(first.values())
        + small_across
        + small_core
        + [up_core, down_core]
        + small_relay
        + list(forward.values())
        + list(pass_own.values())
        + list(pass_got.values())
    )
    first["up", "y"].start()
    first["up", "z"].start()
    for copy in small_across + small_core + [up_core, down_core]:
        copy.start()
    first["down", "y"].start()
    first["down", "z"].start()

    def hand_on(name, way):
        first[name, way].wait_recv()
        forward[name, way].start()
        pass_own[name, way].start()

    def hand_over(name, way):
        forward[name, way].wait_recv()
        pass_got[name, way].start()

    lx[...] = jnp.transpose(lx_t[...])
    lcot[...] = jnp.transpose(lcot_ref[...])
    mask_column(token_mask, box_mask, column)
    masked[...] = jnp.zeros_like(masked)
    vec[...] = jnp.zeros_like(vec)
    rises[0:1, :] = wide(bq)
    rises[1:2, :] = wide(bv)
    rises[2:3, :] = wide(bo)
    for copy in loads:
        copy.wait()

    def project(j):
        cols = tile(j)
        rows = x_ref[...]
        queries = low(dot(rows, wq[:, cols]) + rises[0:1, cols]) * 0.125
        qn[:, cols] = queries
        q_t[cols, :] = jnp.transpose(queries)
        kn[:, cols] = low(dot(rows, wk[:, cols]))
        values = low(dot(rows, wv[:, cols]) + rises[1:2, cols])
        vn[:, cols] = values
        v_t[cols, :] = jnp.transpose(values)

    loop(tiles, project)
    pad = jnp.zeros((PAGE, 256 - lwidth), BF16)
    rows = lx[...]
    queries = low(dot(rows, lwq[...]) + wide(lbq)) * 0.25
    queries = jnp.concatenate([queries, pad], axis=1)
    lqn[...] = queries
    lq_t[...] = jnp.transpose(queries)
    lkn[...] = jnp.concatenate([low(dot(rows, lwk[...])), pad], axis=1)
    values = low(dot(rows, lwv[...]) + wide(lbv))
    values = jnp.concatenate([values, pad], axis=1)
    lvn[...] = values
    lv_t[...] = jnp.transpose(values)
    lctx_t[...] = jnp.zeros_like(lctx_t)

    def attend(pair):
        keys = jnp.concatenate([kn[:, tile(pair, 128)], lkn[:, tile(pair // 4, 128)]], axis=1)
        for side in range(2):
            head = 2 * pair + side
            head_rows(masked, q_t, lq_t, pair, side)
            joint = dot(keys, masked[side * 256 : side * 256 + 256, :])
            highest = jnp.max(joint, axis=0, keepdims=True)
            exponent = jnp.exp(joint - highest)
            totals = row_sum(exponent)
            weights = low(exponent * (1.0 / totals))
            lse[pl.ds(head, 1), :] = highest + jnp.log(totals)
            values = jnp.concatenate([v_t[tile(head, 64), :], lv_t[tile(head, 16), :]], axis=0)
            context = low(dot(values, weights))
            ctx_t[tile(head, 64), :] = context[0:64]
            lctx_t[tile(head, 16), :] = context[64:80]

        @pl.when(pair == 3)
        def _():
            hand_on("up", "y")

    loop(HEADS // 2, attend)

    def untranspose(j):
        ctx[:, tile(j)] = jnp.transpose(ctx_t[tile(j), :])

    loop(tiles, untranspose)
    lctx[...] = jnp.transpose(lctx_t[...])
    load_wo.wait()

    def mix(j):
        cols = tile(j)
        asum[:, cols] = x_ref[:, cols].astype(F32) + dot(ctx[...], wo[:, cols]) + rises[2:3, cols]

    loop(tiles, mix)
    lasum[...] = lx[...].astype(F32) + dot(lctx[:, 0:lwidth], lwo[...]) + wide(lbo)

    def first_norm(source, gain, shift, hidden, hidden_low):
        gain, shift = wide(gain), wide(shift)

        def rows_of(i):
            r = tile(i, ROWS)
            unit, _ = normed(source[r, :])
            value = unit * gain + shift
            hidden[r, :] = value
            hidden_low[r, :] = low(value)

        loop(PAGE // ROWS, rows_of)

    hand_on("up", "z")
    for copy in small_across:
        copy.wait_recv()
    for copy in small_relay:
        copy.start()
    first_norm(asum, attend_gain, attend_shift, feed, hlow)
    first_norm(lasum, lattend_gain, lattend_shift, lfeed, lhlow)
    h_t[...] = jnp.transpose(hlow[...])
    lh_t[...] = jnp.transpose(lhlow[...])

    def shard_at(s):
        return (x + s // 2 - 2 * x * (s // 2)) * 2 + c + s % 2 - 2 * c * (s % 2)

    def page_rows(base, s):
        return pl.ds(pl.multiple_of(base + s * PAGE, PAGE), PAGE)

    def gelu(u):
        square = u * u
        inner = 0.7978845608028654 * (u + 0.044715 * (square * u))
        wave = jnp.tanh(inner)
        rise = 0.5 * (1.0 + wave)
        bend = 0.5 * u * (1.0 - wave * wave)
        grow = 0.7978845608028654 * (1.0 + 0.134145 * square)
        return u * rise, rise + bend * grow

    keep_up.wait()

    def feed_up(s):
        t = shard_at(s)

        @pl.when(s == 1)
        def _():
            up_core.wait_recv()
            for copy in small_core:
                copy.wait_recv()
            hand_over("up", "y")

        @pl.when(s == 2)
        def _():
            hand_on("down", "y")
            hand_over("up", "z")

        @pl.when(s == 3)
        def _():
            for copy in small_relay:
                copy.wait_recv()
            for way in ("y", "z"):
                pass_own["up", way].wait_recv()
                pass_got["up", way].wait_recv()

        def up(j):
            cols = tile(j)
            weights = pool[shard_rows(0, t), cols]
            preact = dot(hlow[...], weights) + small_bias[t, pl.ds(j, 1), :]
            value, gradient = gelu(preact)
            pool[page_rows(act_at, s), cols] = low(value)
            pool[page_rows(slope_at, s), cols] = low(gradient)

        loop(tiles, up)
        preact = dot(lhlow[...], small[t, 0:lwidth, 0:lwidth]) + small_bias[t, 3:4, 0:lwidth]
        value, gradient = gelu(preact)
        lact[s] = low(value)
        lslope[s] = low(gradient)

    loop(4, feed_up)
    keep_down.wait()

    def feed_down(s):
        t = shard_at(s)

        @pl.when(s == 1)
        def _():
            down_core.wait_recv()
            hand_on("down", "z")

        @pl.when(s == 2)
        def _():
            hand_over("down", "y")
            hand_over("down", "z")

        @pl.when(s == 3)
        def _():
            for way in ("y", "z"):
                pass_own["down", way].wait_recv()
                pass_got["down", way].wait_recv()

        def down(j):
            cols = tile(j)
            active = pool[page_rows(act_at, s), :]
            feed[:, cols] += dot(active, pool[shard_rows(4 * width, t), cols])

        loop(tiles, down)
        lfeed[...] += dot(lact[s], small[t, lwidth : 2 * lwidth, 0:lwidth])

    loop(4, feed_down)

    def second_norm(fed, bias, gain, shift, cot, scale, out, grad_low):
        bias, gain, shift = wide(bias), wide(gain), wide(shift)

        def rows_of(i, sums):
            r = tile(i, ROWS)
            unit, spread = normed(fed[r, :] + bias)
            out[r, :] = low(unit * gain + shift)
            outer = cot[r, :].astype(F32) * column[r, scale : scale + 1]
            value = normed_back(unit, spread, outer * gain)
            fed[r, :] = value
            rounded = low(value)
            grad_low[r, :] = rounded
            return (
                sums[0] + row_sum(outer * unit),
                sums[1] + row_sum(outer),
                sums[2] + row_sum(rounded.astype(F32)),
            )

        zero = jnp.zeros((1, fed.shape[1]), F32)
        return lax.fori_loop(0, PAGE // ROWS, rows_of, (zero, zero, zero))

    found = second_norm(
        feed, down_bias, feed_gain, feed_shift, cot_ref, 0, out_ref, fgrad
    )
    for i in range(3):
        vec[i : i + 1, :] = found[i]
    found = second_norm(
        lfeed, ldown_bias, lfeed_gain, lfeed_shift, lcot, 8, lout, lfgrad
    )
    lout_ref[...] = jnp.transpose(lout[...])
    for i in range(3):
        vec[7:8, i * 256 : i * 256 + lwidth] = found[i]

    deep = tuple(range(2, dp_bits))
    flows = []
    index, keep_at, recv_at, sum_at = 0, 0, 2 * sums.shape[0], 0
    places = []
    for rows, order in feed_flows:
        order = order + deep
        depth = order.index("x")
        places.append((keep_at, rows >> depth))
        size = landing(4 * rows, len(order) + 1) - 2 * rows
        lands = recv.at[pl.ds(keep_at, 2 * rows)], recv.at[pl.ds(recv_at, size)]
        flows.append(
            Flow(
                where,
                ("core",) + order,
                [axis for axis in order if axis != "x"],
                4 * rows,
                staging.at[pl.ds(keep_at, 2 * rows)],
                acc.at[pl.ds(keep_at, 2 * rows)],
                lands,
                sums.at[pl.ds(sum_at, rows)],
                (send_sem, recv_sem, index),
                None,
            )
        )
        index += len(flows[-1].steps)
        keep_at += 2 * rows
        recv_at += size
        sum_at += rows
    feed_count = len(flows)
    ready = {axis: ready_sem.at[i] for i, axis in enumerate(where)}
    keep_at, recv_at = 0, 0
    for rows, order in shared_flows:
        order = ("core",) + order + deep
        size = landing(rows, len(order))
        mine = shared.at[pl.ds(keep_at, rows)]
        lands = (
            staging.at[pl.ds(recv_at, rows // 2)],
            staging.at[pl.ds(recv_at + rows // 2, size - rows // 2)],
        )
        flows.append(
            Flow(
                where,
                order,
                order,
                rows,
                mine,
                mine,
                lands,
                shared_sum.at[pl.ds(keep_at, rows)],
                (send_sem, recv_sem, index),
                ready,
            )
        )
        index += len(flows[-1].steps)
        keep_at += rows
        recv_at += size

    script = Script(flows, set())
    last = len(flows) - 1
    made = [("d", i) for i in range(tiles)] + [("up", i) for i in range(tiles)]
    made += [("context", 0)] + [("weight", i) for i in range(tiles)]
    if moves:
        for point, numbers in moves.items():
            for number in numbers:
                script.write(point, number)
    else:
        for i, point in enumerate(made):
            script.write(point, len(flows) + i)
            if point[0] == "up" and i + 1 == 2 * tiles:
                for k in range(feed_count):
                    script.write("sync", k)
        script.write(made[-1], len(flows) + last)
    script.finish("tail")
    act_now = script.play

    def put(number, target, xs, start, block, cols):
        base, grain = places[number]
        size = block.shape[0]
        row = start
        while row < start + size:
            high, inner = row // grain, row % grain
            length = min(grain - inner, start + size - row)
            place = pl.ds(pl.multiple_of(base + high * 2 * grain + xs * grain + inner, 16), length)
            target[place, cols] = block[row - start : row - start + length]
            row += length

    def down_grad(number, first_unit, units):
        def both(g):
            xs = x + g - 2 * x * g
            for parity, target in ((0, acc), (1, staging)):
                s = 2 * g + parity
                unit = pl.ds(first_unit, units)
                turned[0:units, :] = jnp.transpose(pool[page_rows(act_at, s), unit])

                def block(j):
                    cols = tile(j)
                    value = low(dot(turned[0:units, :], fgrad[:, cols]))
                    put(number, target, xs, 0, value, cols)

                loop(tiles, block)

        loop(2, both)

    for i in range(tiles):
        down_grad(i, i * TILE, TILE)
        if i + 1 < tiles:
            act_now(("d", i))
    empty = jnp.zeros((64, 256 - lwidth), BF16)

    def layout_grad(g):
        xs = x + g - 2 * x * g
        for parity, target in ((0, acc), (1, staging)):
            s = 2 * g + parity
            t = shard_at(s)
            active_grad = dot_nt(lfgrad[...], small[t, lwidth : 2 * lwidth, 0:lwidth])
            rounded = low(active_grad * lslope[s].astype(F32))
            total = row_sum(rounded.astype(F32))
            for k, (row, lane) in enumerate(((8, 0), (8, 256), (8, 512), (9, 0))):

                @pl.when(t == k)
                def _():
                    vec[row : row + 1, lane : lane + lwidth] = total

            lfeed[...] += dot_nt(rounded, small[t, 0:lwidth, 0:lwidth])
            up_block = low(dot(lh_t[...], rounded))
            down_block = low(dot(jnp.transpose(lact[s]), lfgrad[...]))
            for which, block in enumerate((up_block, down_block)):
                for q in range(lwidth // 64):
                    piece = jnp.concatenate([block[q * 64 : q * 64 + 64], empty], axis=1)
                    cols = slice(q * 256, q * 256 + 256)
                    put(tiles - 1, target, xs, TILE + 64 * which, piece, cols)

    loop(2, layout_grad)
    act_now(("d", tiles - 1))

    def units_grad(s):
        t = shard_at(s)

        def units(j):
            cols = tile(j)
            place = pl.ds(pl.multiple_of(4 * width + t * width + j * TILE, 16), TILE)
            active_grad = dot_nt(fgrad[...], pool[place, :])
            slope = pool[page_rows(slope_at, s), cols].astype(F32)
            rounded = low(active_grad * slope)
            pool[page_rows(slope_at, s), cols] = rounded
            vec[pl.ds(3 + t, 1), cols] = row_sum(rounded.astype(F32))

        loop(tiles, units)
        for k in range(4):

            @pl.when(s == k)
            def _():
                act_now(("units", k))

    loop(4, units_grad)

    def up_grad(number, start):
        def both(g):
            xs = x + g - 2 * x * g
            for parity, target in ((0, acc), (1, staging)):
                s = 2 * g + parity

                def block(j):
                    cols = tile(j)
                    value = low(
                        dot(h_t[start : start + TILE, :], pool[page_rows(slope_at, s), cols])
                    )
                    put(number, target, xs, 0, value, cols)

                loop(tiles, block)

        loop(2, both)

    for i in range(tiles):
        up_grad(tiles + i, i * TILE)
        act_now(("up", i))

    def hidden_back(s):
        t = shard_at(s)

        def back(j):
            cols = tile(j)
            place = pl.ds(pl.multiple_of(t * width + j * TILE, 16), TILE)
            feed[:, cols] += dot_nt(pool[page_rows(slope_at, s), :], pool[place, :])

        loop(tiles, back)
        for k in range(4):

            @pl.when(s == k)
            def _():
                act_now(("back", k))

    loop(4, hidden_back)
    for copy in gather_all:
        copy.wait_send()
    for item in flows[:feed_count]:
        item.steps[0][1].wait_send()
    for axis, (_, device) in where.items():
        pl.semaphore_signal(
            ready_sem.at[list(where).index(axis)],
            inc=1,
            device_id=device,
            device_id_type=MESH,
        )
    act_now("sync")
    wo_again, wq_again, wk_again, wv_again = (
        recv.at[pl.ds(i * width, width)] for i in range(4)
    )
    again = [
        load(3, wo_hbm, wo_again),
        load(0, wq_hbm, wq_again),
        load(1, wk_hbm, wk_again),
        load(2, wv_hbm, wv_again),
    ]
    mixed, lmixed = fgrad, lfgrad

    def norm_grad(source, gain, grad, grad_low):
        gain = wide(gain)

        def rows_of(i, sums):
            r = tile(i, ROWS)
            unit, spread = normed(source[r, :])
            outer = grad[r, :]
            value = normed_back(unit, spread, outer * gain)
            grad[r, :] = value
            rounded = low(value)
            grad_low[r, :] = rounded
            return (
                sums[0] + row_sum(rounded.astype(F32)),
                sums[1] + row_sum(outer * unit),
                sums[2] + row_sum(outer),
            )

        zero = jnp.zeros((1, source.shape[1]), F32)
        return lax.fori_loop(0, PAGE // ROWS, rows_of, (zero, zero, zero))

    found = norm_grad(asum, attend_gain, feed, mixed)
    for i in range(3):
        vec[12 + i : 13 + i, :] = found[i]
    found = norm_grad(lasum, lattend_gain, lfeed, lmixed)
    for i in range(3):
        vec[15:16, i * 256 : i * 256 + lwidth] = found[i]
    act_now(("norm", 0))
    again[0].wait()
    k_t, lk_t, cgrad_t, lcgrad = v_t, lv_t, h_t, lctx
    masked_c[...] = jnp.zeros_like(masked_c)

    def turn(j):
        x_t[tile(j), :] = jnp.transpose(x_ref[:, tile(j)])

    def context_back(j):
        cols = tile(j)
        value = low(dot_nt(mixed[...], wo_again[cols, :]))
        cgrad[:, cols] = value
        cgrad_t[cols, :] = jnp.transpose(value)
        shared[0:width, cols] = low(dot(ctx_t[...], mixed[:, cols]))
        k_t[cols, :] = jnp.transpose(kn[:, cols])

    loop(tiles, context_back)
    value = jnp.concatenate([low(dot_nt(lmixed[...], lwo[...])), pad], axis=1)
    lcgrad[...] = value
    lcgrad_t[...] = jnp.transpose(value)
    lk_t[...] = jnp.transpose(lkn[...])
    loop(tiles, turn)
    act_now(("context", 0))

    lane = lax.broadcasted_iota(jnp.int32, (PAGE, 128), 1)
    ldv[...] = jnp.zeros_like(ldv)
    ldk[...] = jnp.zeros_like(ldk)
    ldq_t[...] = jnp.zeros_like(ldq_t)

    def attend_back(pair):
        text, block = tile(pair, 128), tile(pair // 4, 128)
        keys = jnp.concatenate([kn[:, text], lkn[:, block]], axis=1)
        values = jnp.concatenate([vn[:, text], lvn[:, block]], axis=1)
        grads = jnp.concatenate([cgrad[:, text], lcgrad[:, block]], axis=1)
        found = []
        for side in range(2):
            head = 2 * pair + side
            head_rows(masked, q_t, lq_t, pair, side)
            head_rows(masked_c, cgrad_t, lcgrad_t, pair, side)
            span = slice(side * 256, side * 256 + 256)
            weights = jnp.exp(dot(keys, masked[span, :]) - lse[pl.ds(head, 1), :])
            value_grad = dot(low(weights), grads)
            text_wave = dot(vn[:, text], masked_c[side * 256 : side * 256 + 128, :])
            text_part = row_sum(text_wave * weights)
            text_score = low(weights * (text_wave - text_part))
            both_wave = dot(values, masked_c[span, :])
            both_part = row_sum(both_wave * weights)
            both_score = low(weights * (both_wave - both_part))
            query_grad = low(dot(k_t[tile(head, 64), :], text_score) * 0.125)
            ldq_t[tile(head, 16), :] = low(dot(lk_t[tile(head, 16), :], both_score) * 0.25)
            key_grad = dot(text_score, qn[:, text])
            lkey_grad = dot(both_score, lqn[:, block])
            own = (lane // 16) == (head % 8)
            ldv[:, block] = jnp.where(own, value_grad[:, 128:256], ldv[:, block])
            ldk[:, block] = jnp.where(own, lkey_grad, ldk[:, block])
            found.append((value_grad[:, 0:128], key_grad, query_grad))
        first_half = lane < 64
        dv[:, text] = low(jnp.where(first_half, found[0][0], found[1][0]))
        dk[:, text] = low(jnp.where(first_half, found[0][1], found[1][1]))
        dq[:, text] = jnp.transpose(jnp.concatenate([found[0][2], found[1][2]], axis=0))
        for k in range(HEADS // 2):

            @pl.when(pair == k)
            def _():
                act_now(("attend", k))

        @pl.when(pair % 2 == 1)
        def _():
            weight_grad(pair // 2)

        for k in range(tiles - 1):

            @pl.when(pair == 2 * k + 1)
            def _():
                act_now(("weight", k))

    def weight_grad(group):
        cols = tile(group)
        place = pl.ds(pl.multiple_of((1 + group) * width, 16), width)
        for i, source in enumerate((dq, dk, dv)):
            shared[place, i * TILE : (i + 1) * TILE] = low(dot(x_t[...], source[:, cols]))
        vec[10:11, cols] = row_sum(dq[:, cols].astype(F32))
        vec[11:12, cols] = row_sum(dv[:, cols].astype(F32))

    loop(HEADS // 2, attend_back)

    query = jnp.transpose(ldq_t[...])[:, 0:lwidth]
    key, value = low(ldk[:, 0:lwidth]), low(ldv[:, 0:lwidth])
    parts = [low(dot(lx_t[...], item)) for item in (query, key, value)]
    parts.append(low(dot(lctx_t[0:lwidth, :], lmixed[...])))
    base = 4 * width
    shared[base : base + lwidth, :] = jnp.concatenate(parts, axis=1)
    vec[9:10, 256 : 256 + lwidth] = row_sum(query.astype(F32))
    vec[9:10, 512 : 512 + lwidth] = row_sum(value.astype(F32))
    base += lwidth
    shared[base : base + 16, :] = low(vec[...])
    shared[base + 16 : shared_rows, :] = jnp.zeros((shared_rows - base - 16, width), BF16)
    act_now(("weight", tiles - 1))
    for copy in again[1:]:
        copy.wait()

    def input_back(j):
        cols = tile(j)
        feed[:, cols] += (
            dot_nt(dq[...], wq_again[cols, :])
            + dot_nt(dk[...], wk_again[cols, :])
            + dot_nt(dv[...], wv_again[cols, :])
        )
        for k in range(tiles):

            @pl.when(j == k)
            def _():
                act_now(("input", k))

    loop(tiles, input_back)
    in_grad_copy = load(4, feed, in_grad_out)
    lin_grad[...] = jnp.transpose(
        lfeed[...] + dot_nt(query, lwq[...]) + dot_nt(key, lwk[...]) + dot_nt(value, lwv[...])
    )
    act_now(("end", 0))
    act_now("tail")
    total = sums.shape[0]
    outs = [
        load(0, sums, sums_out.at[pl.ds(0, total)]),
        load(1, shared_sum, sums_out.at[pl.ds(total, shared_rows)]),
    ]
    for item in flows:
        item.drain()
    for copy in outs + [in_grad_copy]:
        copy.wait()


MOVES = {
    ("d", 0): (11,),
    ("d", 1): (12,),
    ("d", 2): (13, 0, 11, 1, 12),
    ("units", 2): (2, 13),
    ("up", 0): (14,),
    ("up", 1): (15,),
    ("up", 2): (16, 0, 11, 1, 12, 3),
    ("back", 0): (14, 4, 15, 5),
    ("back", 3): (0, 11, 1, 12),
    ("norm", 0): (16, 2, 13, 0, 11),
    ("context", 0): (17, 1, 12, 3, 14, 4),
    ("attend", 0): (15, 0, 11, 6, 17, 2),
    ("attend", 1): (13, 5, 1, 12, 0, 11, 3, 14),
    ("weight", 0): (18, 16, 4, 15),
    ("attend", 2): (1, 12, 2, 13, 7, 3, 6),
    ("attend", 3): (17, 18, 4, 0, 5),
    ("weight", 1): (19,),
    ("attend", 4): (16, 1, 2, 13, 8, 19, 14, 6),
    ("attend", 5): (7, 18, 17),
    ("weight", 2): (20, 21, 15, 2, 5),
    ("input", 0): (16, 8, 19, 7, 18, 9, 20, 3, 10, 21, 6),
    ("input", 1): (17,),
    ("input", 2): (7,),
    ("end", 0): (18, 8, 4),
    "tail": (10, 21, 5, 19, 9, 20, 6, 17, 10, 21, 9, 20, 7, 18, 14, 8, 6, 17, 19, 7, 18, 10, 9, 20, 3, 14, 21, 6, 17, 8, 19, 15, 7, 9, 20, 10, 21, 8, 19, 18, 3, 6, 17, 4, 15, 9, 20, 6, 10, 8, 19, 21, 9, 20, 16, 4, 13, 7, 18, 10, 21, 5, 16, 7, 8, 19, 9, 20, 8, 9, 10, 21, 2, 5, 10),
}
FEED_ORDERS = (("x", 0, 1), (0, "x", 1), (1, "x", 0), (0, "x", 1), ("x", 0, 1), (0, "x", 1))
SHARED_ORDERS = (("x", 0, 1), (1, 0, "x"), ("x", 0, 1), (0, "x", 1), ("x", 0, 1))


def on_device(dp, tensor, *args):
    (
        text_in,
        layout_in,
        token_mask,
        box_mask,
        cot_text,
        cot_layout,
    ) = args[:6]
    text, layout = args[6:21], args[21:36]
    width, lwidth = text_in.shape[1], layout_in.shape[1]
    dp_bits = dp.bit_length() - 1
    half = width // 2
    feed_flows = tuple(zip((TILE, TILE, TILE + 128, TILE, TILE, TILE), FEED_ORDERS))
    shared_flows = tuple(zip((width, width, width, half + 128, half + 128), SHARED_ORDERS))
    moves = MOVES if dp_bits == 3 else {}
    feed_rows = sum(rows for rows, _ in feed_flows)
    shared_rows = sum(rows for rows, _ in shared_flows)
    land = sum(landing(4 * rows, dp_bits + 2) for rows, _ in feed_flows)
    shared_land = sum(landing(rows, dp_bits + 2) for rows, _ in shared_flows)
    pool_rows = max(8 * width + 8 * PAGE, 2 * shared_rows + 4 * PAGE + width)
    count = (2 * dp_bits + 2) * len(feed_flows) + (2 * dp_bits + 4) * len(shared_flows)

    vmem = pl.BlockSpec(memory_space=pltpu.VMEM)
    hbm = pl.BlockSpec(memory_space=pl.ANY)
    page = PAGE

    def shape(*dims, dtype=BF16):
        return jax.ShapeDtypeStruct(dims, dtype)

    def row(vector):
        return vector.reshape(1, vector.shape[0])

    inputs = (text_in, layout_in.T, row(token_mask), row(box_mask), cot_text, cot_layout.T)
    inputs += text + layout
    specs = [vmem] * len(inputs)
    for i in (6, 8, 9, 11, 15, 17):
        specs[i] = hbm
    outs = (
        shape(page, width),
        shape(lwidth, page),
        shape(page, width, dtype=F32),
        shape(lwidth, page, dtype=F32),
        shape(feed_rows + shared_rows, width),
    )
    scratch = [
        pltpu.VMEM((pool_rows, width), BF16),
        pltpu.VMEM((2 * feed_rows, width), BF16),
        pltpu.VMEM((max(2 * feed_rows, shared_land), width), BF16),
        pltpu.VMEM((land, width), BF16),
        pltpu.VMEM((feed_rows, width), BF16),
        pltpu.VMEM((4, 2 * lwidth, 256), BF16),
        pltpu.VMEM((4, 8, 256), F32),
        pltpu.VMEM((page, width), BF16),
        pltpu.VMEM((page, width), BF16),
        pltpu.VMEM((page, width), BF16),
        pltpu.VMEM((width, page), BF16),
        pltpu.VMEM((width, page), BF16),
        pltpu.VMEM((page, 256), BF16),
        pltpu.VMEM((page, 256), BF16),
        pltpu.VMEM((page, 256), BF16),
        pltpu.VMEM((256, page), BF16),
        pltpu.VMEM((256, page), BF16),
        pltpu.VMEM((16, page), F32),
        pltpu.VMEM((512, page), BF16),
        pltpu.VMEM((512, page), BF16),
        pltpu.VMEM((width, page), BF16),
        pltpu.VMEM((256, page), BF16),
        pltpu.VMEM((page, 256), BF16),
        pltpu.VMEM((page, width), F32),
        pltpu.VMEM((page, lwidth), F32),
        pltpu.VMEM((page, width), BF16),
        pltpu.VMEM((page, lwidth), BF16),
        pltpu.VMEM((width, page), BF16),
        pltpu.VMEM((lwidth, page), BF16),
        pltpu.VMEM((page, width), F32),
        pltpu.VMEM((page, lwidth), F32),
        pltpu.VMEM((4, page, lwidth), BF16),
        pltpu.VMEM((4, page, lwidth), BF16),
        pltpu.VMEM((page, 16), F32),
        pltpu.VMEM((8, width), F32),
        pltpu.VMEM((page, lwidth), BF16),
        pltpu.VMEM((page, lwidth), BF16),
        pltpu.VMEM((256, page), BF16),
        pltpu.VMEM((256, page), BF16),
        pltpu.VMEM((page, 256), F32),
        pltpu.VMEM((page, 256), F32),
        pltpu.VMEM((16, width), F32),
        pltpu.SemaphoreType.DMA((6,)),
        pltpu.SemaphoreType.DMA((24,)),
        pltpu.SemaphoreType.DMA((24,)),
        pltpu.SemaphoreType.DMA((count,)),
        pltpu.SemaphoreType.DMA((count,)),
        pltpu.SemaphoreType.REGULAR((dp_bits + 2,)),
    ]
    text_out, layout_out, in_grad, lin_grad, sums = pl.pallas_call(
        functools.partial(layer_kernel, (dp_bits, feed_flows, shared_flows, moves)),
        out_shape=outs,
        in_specs=specs,
        out_specs=[vmem, vmem, hbm, vmem, hbm],
        scratch_shapes=scratch,
        compiler_params=pltpu.CompilerParams(
            collective_id=0, has_side_effects=True, vmem_limit_bytes=67043328
        ),
        name="layer",
    )(*inputs)

    me = lax.axis_index("tensor")
    shared = sums[feed_rows:]
    at = 4 * width
    packed = shared[at : at + lwidth].astype(F32)
    vec = shared[at + lwidth : at + lwidth + 16].astype(F32)

    def square(index):
        parts = [
            shared[(1 + g) * width : (2 + g) * width, index * TILE : (index + 1) * TILE]
            for g in range(width // TILE)
        ]
        return jnp.concatenate(parts, axis=1).astype(F32)

    def unpack(block):
        parts = [block[:, q * 256 : q * 256 + lwidth] for q in range(lwidth // 64)]
        return jnp.concatenate(parts, axis=0).astype(F32)

    def layout_square(index):
        return packed[:, index * lwidth : (index + 1) * lwidth]

    def strip(index, part):
        return vec[index, part * 256 : part * 256 + lwidth]

    up_bias = lax.dynamic_index_in_dim(vec, 3 + me, 0, keepdims=False)
    lup_bias = lax.dynamic_index_in_dim(
        jnp.stack([strip(8, 0), strip(8, 1), strip(8, 2), strip(9, 0)]), me, 0, keepdims=False
    )
    return (
        text_out,
        layout_out.T,
        in_grad,
        lin_grad.T,
        square(0),
        vec[10],
        square(1),
        square(2),
        vec[11],
        shared[0:width].astype(F32),
        vec[12],
        vec[13],
        vec[14],
        sums[width + 128 : 2 * width + 128].astype(F32),
        up_bias,
        sums[0:width].astype(F32),
        vec[2],
        vec[0],
        vec[1],
        layout_square(0),
        strip(9, 1),
        layout_square(1),
        layout_square(2),
        strip(9, 2),
        layout_square(3),
        strip(15, 0),
        strip(15, 1),
        strip(15, 2),
        unpack(sums[width : width + 64]),
        lup_bias,
        unpack(sums[width + 64 : width + 128]),
        strip(7, 2),
        strip(7, 0),
        strip(7, 1),
    )


def solution(mesh):
    rows = P(("dp", "tensor"), None)
    line = P(("dp", "tensor"))
    weights = (P(),) * 9 + (P(None, "tensor"), P("tensor"), P("tensor", None)) + (P(),) * 3
    in_specs = (rows, rows, line, line, rows, rows) + weights + weights
    out_specs = (rows,) * 4 + weights + weights
    return jax.shard_map(
        functools.partial(on_device, mesh.shape["dp"], mesh.shape["tensor"]),
        mesh=mesh,
        in_specs=in_specs,
        out_specs=out_specs,
        check_vma=False,
    )
```

```python
import functools

import jax
import jax.numpy as jnp
from jax import lax
from jax.experimental import pallas as pl
from jax.experimental.pallas import tpu as pltpu
from jax.sharding import PartitionSpec as P

HEADS = 12
PAGE = 512
NORM_EPS = 1e-05
MESH = pl.DeviceIdType.MESH
F32 = jnp.float32
BF16 = jnp.bfloat16
TILE = 256
ROWS = 128
CORE, ACROSS = 100, 101
SETUP, PROJECT, LAYOUT, HEAD, MIX, FIRST, FEED, FED, DOWN, DONE = range(10)
D, UNITS, UP, BACK, NORM, CONTEXT, ATTEND, WEIGHT, INPUT, END, TAIL, SYNC = range(10, 22)


def low(values):
    return values.astype(BF16)


def dot(first, second):
    return jnp.dot(first, second, preferred_element_type=F32)


def dot_nt(first, second):
    return lax.dot_general(first, second, (((1,), (1,)), ((), ())), preferred_element_type=F32)


def tile(index, size=TILE):
    return pl.ds(pl.multiple_of(index * size, size), size)


def loop(count, body):
    def step(index, carry):
        body(index)
        return carry

    lax.fori_loop(0, count, step, 0, unroll=count if count < 4 else 1)


def flip(bit):
    return 1 - 2 * bit


def wide(vector_ref):
    return vector_ref[...].astype(F32)[None, :]


def lane_mean(values):
    return jnp.mean(values, axis=-1, keepdims=True)


def row_sum(values):
    return jnp.sum(values, axis=0, keepdims=True)


def normed(values):
    centered = values - lane_mean(values)
    scale = lax.rsqrt(lane_mean(centered * centered) + NORM_EPS)
    return centered * scale, scale


def normed_back(unit, scale, grad):
    return (grad - lane_mean(grad) - unit * lane_mean(grad * unit)) * scale


def landing(rows, stages):
    total = 0
    for stage in range(stages):
        rows = rows // 2 if rows % 32 == 0 and stage + 1 < stages else rows
        total += rows
    return total


def copy_to(source, target, send, recv, device):
    return pltpu.make_async_remote_copy(
        src_ref=source,
        dst_ref=target,
        send_sem=send,
        recv_sem=recv,
        device_id=device,
        device_id_type=MESH,
    )


def greet(devices):
    barrier = pltpu.get_barrier_semaphore()
    for device in devices:
        pl.semaphore_signal(barrier, inc=1, device_id=device, device_id_type=MESH)
    pl.semaphore_wait(barrier, len(devices))


def mask_column(text_mask, layout_mask, column_ref):
    parts = []
    for mask_ref in (text_mask, layout_mask):
        scale = 0.5 + 1.5 * mask_ref[...].astype(F32)
        parts.append(jnp.broadcast_to(scale, (8, PAGE)))
    column_ref[...] = jnp.transpose(jnp.concatenate(parts, axis=0))


def head_rows(target, text_rows, layout_rows, pair, side):
    head = 2 * pair + side
    top = side * 256
    target[top + 128 : top + 256, :] = jnp.zeros((128, PAGE), BF16)
    target[top + side * 64 : top + side * 64 + 64, :] = text_rows[tile(head, 64), :]
    spot = pl.ds(pl.multiple_of(top + 128 + (head % 8) * 16, 16), 16)
    target[spot, :] = layout_rows[tile(head, 16), :]


class Flow:
    def __init__(self, where, axes, spread, rows, give, keep, lands, whole, sems, ready, result):
        self.steps, self.ready = [], ready
        self.result = pltpu.make_async_copy(whole, *result)
        send_sem, recv_sem, index = sems
        offset, size, place = 0, rows, 0
        halved = []
        for stage, axis in enumerate(axes):
            bit, device = where[axis]
            recv = lands[min(stage, 1)]
            if stage == 1:
                place = 0
            if size % 32 == 0 and stage + 1 < len(axes):
                half = size // 2
                kept, given = offset + bit * half, offset + (1 - bit) * half
                halved.append(axis)
            else:
                half, kept, given = size, offset, offset
            first = stage == 0 and give is not keep
            source = give.at[pl.ds(0, half)] if first else self.span(keep, given, half)
            kept = 0 if first else kept
            copy = copy_to(
                source,
                recv.at[pl.ds(place, half)],
                send_sem.at[index],
                recv_sem.at[index],
                device,
            )
            last = stage + 1 == len(axes)
            target, start = keep, kept
            if last:
                target, start = whole, 0
                step, gathers = whole.shape[0], []
                for other in spread:
                    if other in halved:
                        step //= 2
                        start = start + where[other][0] * step
                        gathers.insert(0, (other, step))
            swap = half == size and not last
            self.steps.append((axis, copy, (keep, kept, recv, place, target, start, half, swap)))
            offset, size = kept, half
            place += half
            index += 1
        spot = start
        for axis, step in gathers:
            bit, device = where[axis]
            span = self.span(whole, spot, step)
            copy = copy_to(span, span, send_sem.at[index], recv_sem.at[index], device)
            self.steps.append((axis, copy, None))
            spot = spot - bit * step
            index += 1

    def span(self, ref, offset, size):
        return ref.at[pl.ds(pl.multiple_of(offset, 16), size)]

    def launch(self, step, waits):
        axis, copy, _ = self.steps[step]
        if waits:
            pl.semaphore_wait(self.ready[axis], 1)
        copy.start()

    def absorb(self, step):
        _, copy, rest = self.steps[step]
        copy.wait_recv()
        if rest is not None:
            keep, kept, recv, place, target, start, half, swap = rest
            if swap:
                copy.wait_send()
            block = max(b for b in range(16, 129, 16) if half % b == 0)

            def add(i):
                mine = pl.ds(pl.multiple_of(kept + i * block, 16), block)
                theirs = pl.ds(pl.multiple_of(place + i * block, 16), block)
                result = pl.ds(pl.multiple_of(start + i * block, 16), block)
                target[result, :] = keep[mine, :] + recv[theirs, :]

            loop(half // block, add)
        if step + 1 == len(self.steps):
            self.result.start()

    def drain(self):
        self.result.wait()
        for _, copy, rest in self.steps[1 if self.ready is None else 0 :]:
            if rest is None or not rest[-1]:
                copy.wait_send()


class Script:
    def __init__(self, flows, greeted):
        self.flows, self.greeted = flows, greeted
        self.started, self.taken = [0] * len(flows), [0] * len(flows)
        self.points = {}

    def write(self, point, number):
        kind, flow = divmod(number, len(self.flows))
        done = self.started if kind else self.taken
        step = done[flow]
        done[flow] += 1
        waits = False
        if kind and self.flows[flow].ready is not None:
            axis = self.flows[flow].steps[step][0]
            waits = axis not in self.greeted
            self.greeted.add(axis)
        self.points.setdefault(point, []).append((kind, flow, step, waits))

    def play(self, point):
        for kind, flow, step, waits in self.points.get(point, ()):
            if kind:
                self.flows[flow].launch(step, waits)
            else:
                self.flows[flow].absorb(step)

    def finish(self, point):
        flows, going = self.flows, True
        while going:
            going = False
            for i, flow in enumerate(flows):
                if self.started[i] > self.taken[i]:
                    self.write(point, i)
                    going = True
                if self.started[i] == self.taken[i] and self.taken[i] < len(flow.steps):
                    self.write(point, len(flows) + i)
                    going = True


def layer_kernel(plan, *refs):
    (
        x_ref,
        lx_t,
        token_mask,
        box_mask,
        cot_ref,
        lcot_ref,
        wq_hbm,
        bq,
        wk_hbm,
        wv_hbm,
        bv,
        wo_hbm,
        bo,
        attend_gain,
        attend_shift,
        up_hbm,
        up_bias,
        down_hbm,
        down_bias,
        feed_gain,
        feed_shift,
        lwq,
        lbq,
        lwk,
        lwv,
        lbv,
        lwo,
        lbo,
        lattend_gain,
        lattend_shift,
        lup,
        lup_bias,
        ldown,
        ldown_bias,
        lfeed_gain,
        lfeed_shift,
        out_ref,
        lout_ref,
        in_grad_out,
        lin_grad,
        sums_out,
        pool,
        acc,
        staging,
        recv,
        sums,
        small,
        small_bias,
        qn,
        kn,
        vn,
        q_t,
        v_t,
        lqn,
        lkn,
        lvn,
        lq_t,
        lv_t,
        lse,
        masks,
        ctx_t,
        lctx_t,
        lctx,
        asum,
        hlow,
        lhlow,
        h_t,
        lh_t,
        feed,
        lfeed,
        lact,
        lslope,
        column,
        rises,
        lx,
        lcot,
        lcgrad_t,
        ldq_t,
        ldk,
        ldv,
        vec,
        local_sem,
        gather_send,
        gather_recv,
        send_sem,
        recv_sem,
        out_sem,
        ready_sem,
    ) = refs
    dp_bits, feed_flows, shared_flows, moves = plan
    fgrad, lfgrad, lout, lasum = hlow, lhlow, lx, ldk
    masked, masked_c = masks.at[pl.ds(0, 512)], masks.at[pl.ds(512, 512)]
    fgrad_t = masks.at[pl.ds(0, x_ref.shape[1])]
    d, me = lax.axis_index("dp"), lax.axis_index("tensor")
    c, x = me % 2, me // 2
    width, lwidth = x_ref.shape[1], lx_t.shape[0]
    tiles = width // TILE
    where = {CORE: (c, (d, me + flip(c))), ACROSS: (x, (d, me + 2 * flip(x)))}
    for k in range(dp_bits):
        bit = (d // 2**k) % 2
        where[k] = (bit, (d + 2**k * flip(bit), me))
    core, across = where[CORE][1], where[ACROSS][1]
    y, beside = where[0]
    z, ahead = where[1]
    other = me + 2 * flip(x)

    def part(start, size):
        return pool.at[pl.ds(start, size)]

    wu, wd = part(0, 4 * width), part(4 * width, 4 * width)
    act_at, slope_at = 8 * width, 8 * width + 4 * PAGE
    wq, wk = part(act_at, width), part(act_at + width, width)
    wv, wo = part(act_at + 2 * width, width), part(act_at + 3 * width, width)
    ctx = part(act_at + 4 * width, PAGE)
    shared_rows = sum(rows for rows, _ in shared_flows)
    shared, shared_sum = part(0, shared_rows), part(shared_rows, shared_rows)
    spot = 2 * shared_rows
    dq, dk, dv = part(spot, PAGE), part(spot + PAGE, PAGE), part(spot + 2 * PAGE, PAGE)
    cgrad = part(spot + 3 * PAGE, PAGE)
    x_t = pool.at[pl.ds(spot + 4 * PAGE, width), pl.ds(0, PAGE)]

    def shard_rows(base, t, start=0, size=width):
        return pl.ds(pl.multiple_of(base + t * width + start, 16), size)

    small[me, 0:lwidth, 0:lwidth] = lup[...]
    small[me, lwidth : 2 * lwidth, 0:lwidth] = ldown[...]
    for j in range(tiles):
        small_bias[me, j : j + 1, :] = wide(up_bias)[:, j * TILE : (j + 1) * TILE]
    small_bias[me, 3:4, 0:lwidth] = wide(lup_bias)

    def load(index, source, target):
        copy = pltpu.make_async_copy(source, target, local_sem.at[index])
        copy.start()
        return copy

    loads = [load(i, s, t) for i, (s, t) in enumerate(((wq_hbm, wq), (wk_hbm, wk), (wv_hbm, wv)))]
    load_wo = load(3, wo_hbm, wo)
    keep_up = load(4, up_hbm, pool.at[shard_rows(0, me)])
    keep_down = load(5, down_hbm, pool.at[shard_rows(4 * width, me)])
    greet([device for _, device in where.values()])

    messages, needs = [], []

    def message(source, target, device, *after):
        index = len(messages)
        copy = copy_to(source, target, gather_send.at[index], gather_recv.at[index], device)
        messages.append(copy)
        needs.append(set(after))

    for base, hbm in ((0, up_hbm), (4 * width, down_hbm)):
        grain = width // 12
        zero = len(messages)

        def relay(start, size, device, *after):
            place = pool.at[shard_rows(base, other, start * grain, size * grain)]
            message(place, place, device, *(zero + item for item in after))

        own = (y, 2 + z, 4 + 2 * z + y, 8 + 2 * y + z)
        for start in own:
            source = hbm.at[pl.ds(pl.multiple_of(start * grain, 16), grain)]
            message(source, pool.at[shard_rows(base, me, start * grain, grain)], across)
        relay(own[0], 1, beside, 0)
        relay(own[1], 1, ahead, 1)
        relay(own[2], 1, beside, 2)
        relay(4 + 2 * z, 2, ahead, 2, 6)
        relay(own[3], 1, ahead, 3)
        relay(8 + 2 * y, 2, beside, 3, 8)
        relay(own[0], 1, core, 0)
        relay(1 - y, 1, core, 4)
        relay(own[1], 1, core, 1)
        relay(3 - z, 1, core, 5)
        relay(4 + 2 * z, 2, core, 2, 6)
        relay(6 - 2 * z, 2, core, 7)
        relay(8 + 2 * y, 2, core, 3, 8)
        relay(10 - 2 * y, 2, core, 9)
        message(hbm, pool.at[shard_rows(base, me)], core)
    for ref in (small, small_bias):
        message(ref.at[me], ref.at[me], across)
        message(ref.at[me], ref.at[me], core)
        message(ref.at[other], ref.at[other], core, len(messages) - 2)
    begun, got = set(START), set()
    for index in START:
        messages[index].start()

    def take(stage, k=0):
        for index in GATHER.get((stage, k), ()):
            messages[index].wait_recv()
            got.add(index)
            for later, after in enumerate(needs):
                if later not in begun and after <= got:
                    messages[later].start()
                    begun.add(later)

    def take_at(index, stage):
        for k in range(8):
            if (stage, k) in GATHER:

                @pl.when(index == k)
                def _():
                    take(stage, k)

    lx[...] = jnp.transpose(lx_t[...])
    lcot[...] = jnp.transpose(lcot_ref[...])
    mask_column(token_mask, box_mask, column)
    masks[...] = jnp.zeros_like(masks)
    vec[...] = jnp.zeros_like(vec)
    rises[0:1, :] = wide(bq)
    rises[1:2, :] = wide(bv)
    rises[2:3, :] = wide(bo)
    for copy in loads:
        copy.wait()
    take(SETUP)

    def project(j):
        cols = tile(j)
        rows = x_ref[...]
        queries = low(dot(rows, wq[:, cols]) + rises[0:1, cols]) * 0.125
        qn[:, cols] = queries
        q_t[cols, :] = jnp.transpose(queries)
        kn[:, cols] = low(dot(rows, wk[:, cols]))
        values = low(dot(rows, wv[:, cols]) + rises[1:2, cols])
        vn[:, cols] = values
        v_t[cols, :] = jnp.transpose(values)
        take_at(j, PROJECT)

    loop(tiles, project)
    pad = jnp.zeros((PAGE, 256 - lwidth), BF16)
    rows = lx[...]
    queries = low(dot(rows, lwq[...]) + wide(lbq)) * 0.25
    queries = jnp.concatenate([queries, pad], axis=1)
    lqn[...] = queries
    lq_t[...] = jnp.transpose(queries)
    lkn[...] = jnp.concatenate([low(dot(rows, lwk[...])), pad], axis=1)
    values = low(dot(rows, lwv[...]) + wide(lbv))
    values = jnp.concatenate([values, pad], axis=1)
    lvn[...] = values
    lv_t[...] = jnp.transpose(values)
    lctx_t[...] = jnp.zeros_like(lctx_t)
    take(LAYOUT)

    def attend(pair):
        keys = jnp.concatenate([kn[:, tile(pair, 128)], lkn[:, tile(pair // 4, 128)]], axis=1)
        for side in range(2):
            head = 2 * pair + side
            head_rows(masked, q_t, lq_t, pair, side)
            joint = dot(keys, masked[side * 256 : side * 256 + 256, :])
            highest = jnp.max(joint, axis=0, keepdims=True)
            exponent = jnp.exp(joint - highest)
            totals = row_sum(exponent)
            weights = low(exponent * (1.0 / totals))
            lse[pl.ds(head, 1), :] = highest + jnp.log(totals)
            values = jnp.concatenate([v_t[tile(head, 64), :], lv_t[tile(head, 16), :]], axis=0)
            context = low(dot(values, weights))
            ctx_t[tile(head, 64), :] = context[0:64]
            lctx_t[tile(head, 16), :] = context[64:80]

        take_at(pair, HEAD)

    loop(HEADS // 2, attend)

    def untranspose(j):
        ctx[:, tile(j)] = jnp.transpose(ctx_t[tile(j), :])

    loop(tiles, untranspose)
    lctx[...] = jnp.transpose(lctx_t[...])
    load_wo.wait()

    def mix(j):
        cols = tile(j)
        asum[:, cols] = x_ref[:, cols].astype(F32) + dot(ctx[...], wo[:, cols]) + rises[2:3, cols]

    loop(tiles, mix)
    lasum[:, 0:lwidth] = lx[...].astype(F32) + dot(lctx[:, 0:lwidth], lwo[...]) + wide(lbo)

    def first_norm(r, source, gain, shift, hidden, hidden_low):
        unit, _ = normed(source[r, 0 : hidden.shape[1]])
        value = unit * gain + shift
        hidden[r, :] = value
        hidden_low[r, :] = low(value)

    gains = [wide(item) for item in (attend_gain, attend_shift, lattend_gain, lattend_shift)]

    def first_norms(i):
        r = tile(i, ROWS)
        first_norm(r, asum, gains[0], gains[1], feed, hlow)
        first_norm(r, lasum, gains[2], gains[3], lfeed, lhlow)

    take(MIX)
    loop(PAGE // ROWS, first_norms)
    h_t[...] = jnp.transpose(hlow[...])
    lh_t[...] = jnp.transpose(lhlow[...])
    take(FIRST)

    def shard_at(s):
        return (x + s // 2 - 2 * x * (s // 2)) * 2 + c + s % 2 - 2 * c * (s % 2)

    def page_rows(base, s):
        return pl.ds(pl.multiple_of(base + s * PAGE, PAGE), PAGE)

    def gelu(u):
        square = u * u
        inner = 0.7978845608028654 * (u + 0.044715 * (square * u))
        wave = jnp.tanh(inner)
        rise = 0.5 * (1.0 + wave)
        bend = 0.5 * u * (1.0 - wave * wave)
        grow = 0.7978845608028654 * (1.0 + 0.134145 * square)
        return u * rise, rise + bend * grow

    keep_up.wait()

    def feed_up(s):
        t = shard_at(s)

        take_at(s, FEED)

        def up(j):
            cols = tile(j)
            weights = pool[shard_rows(0, t), cols]
            preact = dot(hlow[...], weights) + small_bias[t, pl.ds(j, 1), :]
            value, gradient = gelu(preact)
            pool[page_rows(act_at, s), cols] = low(value)
            pool[page_rows(slope_at, s), cols] = low(gradient)

        loop(tiles, up)
        preact = dot(lhlow[...], small[t, 0:lwidth, 0:lwidth]) + small_bias[t, 3:4, 0:lwidth]
        value, gradient = gelu(preact)
        lact[s] = low(value)
        lslope[s] = low(gradient)
        take_at(s, FED)

    loop(4, feed_up)
    keep_down.wait()

    def feed_down(s):
        t = shard_at(s)

        take_at(s, DOWN)

        def down(j):
            cols = tile(j)
            active = pool[page_rows(act_at, s), :]
            feed[:, cols] += dot(active, pool[shard_rows(4 * width, t), cols])

        loop(tiles, down)
        lfeed[...] += dot(lact[s], small[t, lwidth : 2 * lwidth, 0:lwidth])
        take_at(s, DONE)

    loop(4, feed_down)

    def second_norm(r, sums, fed, bias, gain, shift, cot, scale, out, grad_low):
        unit, spread = normed(fed[r, :] + bias)
        out[r, :] = low(unit * gain + shift)
        outer = cot[r, :].astype(F32) * column[r, scale : scale + 1]
        value = normed_back(unit, spread, outer * gain)
        fed[r, :] = value
        rounded = low(value)
        grad_low[r, :] = rounded
        return (
            sums[0] + row_sum(outer * unit),
            sums[1] + row_sum(outer),
            sums[2] + row_sum(rounded.astype(F32)),
        )

    tops = [wide(item) for item in (down_bias, feed_gain, feed_shift)]
    ltops = [wide(item) for item in (ldown_bias, lfeed_gain, lfeed_shift)]

    def second_norms(i, sums):
        r = tile(i, ROWS)
        return (
            second_norm(r, sums[0], feed, *tops, cot_ref, 0, out_ref, fgrad),
            second_norm(r, sums[1], lfeed, *ltops, lcot, 8, lout, lfgrad),
        )

    none, lnone = jnp.zeros((1, width), F32), jnp.zeros((1, lwidth), F32)
    start = ((none, none, none), (lnone, lnone, lnone))
    found, lfound = lax.fori_loop(0, PAGE // ROWS, second_norms, start)
    lout_ref[...] = jnp.transpose(lout[...])
    for i in range(3):
        vec[i : i + 1, :] = found[i]
        vec[7:8, i * 256 : i * 256 + lwidth] = lfound[i]

    deep = tuple(range(2, dp_bits))
    flows = []
    index, keep_at, recv_at, sum_at = 0, 0, 2 * sums.shape[0], 0
    places = []
    for rows, order in feed_flows:
        order = order + deep
        depth = order.index(ACROSS)
        places.append((keep_at, rows >> depth))
        size = landing(4 * rows, len(order) + 1) - 2 * rows
        lands = recv.at[pl.ds(keep_at, 2 * rows)], recv.at[pl.ds(recv_at, size)]
        flows.append(
            Flow(
                where,
                (CORE,) + order,
                [axis for axis in order if axis != ACROSS],
                4 * rows,
                staging.at[pl.ds(keep_at, 2 * rows)],
                acc.at[pl.ds(keep_at, 2 * rows)],
                lands,
                sums.at[pl.ds(sum_at, rows)],
                (send_sem, recv_sem, index),
                None,
                (sums_out.at[pl.ds(sum_at, rows)], out_sem.at[len(flows)]),
            )
        )
        index += len(flows[-1].steps)
        keep_at += 2 * rows
        recv_at += size
        sum_at += rows
    feed_count = len(flows)
    ready = {axis: ready_sem.at[i] for i, axis in enumerate(where)}
    keep_at, recv_at = 0, 0
    for rows, order in shared_flows:
        order = (CORE,) + order + deep
        size = landing(rows, len(order))
        mine = shared.at[pl.ds(keep_at, rows)]
        lands = (
            staging.at[pl.ds(recv_at, rows // 2)],
            staging.at[pl.ds(recv_at + rows // 2, size - rows // 2)],
        )
        flows.append(
            Flow(
                where,
                order,
                order,
                rows,
                mine,
                mine,
                lands,
                shared_sum.at[pl.ds(keep_at, rows)],
                (send_sem, recv_sem, index),
                ready,
                (sums_out.at[pl.ds(sum_at + keep_at, rows)], out_sem.at[len(flows)]),
            )
        )
        index += len(flows[-1].steps)
        keep_at += rows
        recv_at += size

    script = Script(flows, set())
    last = len(flows) - 1
    made = [(D, i) for i in range(tiles)] + [(UP, i) for i in range(tiles)]
    made += [(CONTEXT, 0)] + [(WEIGHT, i) for i in range(tiles)]
    if moves:
        for point, numbers in moves.items():
            for number in numbers:
                script.write(point, number)
    else:
        for i, point in enumerate(made):
            script.write(point, len(flows) + i)
            if point[0] == UP and i + 1 == 2 * tiles:
                for k in range(feed_count):
                    script.write((SYNC, 0), k)
        script.write(made[-1], len(flows) + last)
    script.finish((TAIL, 0))
    act_now = script.play

    def put(number, target, xs, start, block, cols):
        base, grain = places[number]
        size = block.shape[0]
        row = start
        while row < start + size:
            high, inner = row // grain, row % grain
            length = min(grain - inner, start + size - row)
            place = pl.ds(pl.multiple_of(base + high * 2 * grain + xs * grain + inner, 16), length)
            target[place, cols] = block[row - start : row - start + length]
            row += length

    def outer_grad(number, rows_t, base, tile_index):
        def both(g):
            xs = x + g - 2 * x * g
            for parity, target in ((0, acc), (1, staging)):
                cols = slice(tile_index * TILE, (tile_index + 1) * TILE)
                value = low(dot(rows_t[...], pool[page_rows(base, 2 * g + parity), cols]))
                for q in range(tiles):
                    lanes = slice(q * TILE, (q + 1) * TILE)
                    put(number, target, xs, 0, value[q * TILE : (q + 1) * TILE], lanes)

        loop(2, both)

    fgrad_t[...] = jnp.transpose(fgrad[...])
    for i in range(tiles):
        outer_grad(i, fgrad_t, act_at, i)
        if i + 1 < tiles:
            act_now((D, i))
    empty = jnp.zeros((64, 256 - lwidth), BF16)

    def layout_grad(g):
        xs = x + g - 2 * x * g
        for parity, target in ((0, acc), (1, staging)):
            s = 2 * g + parity
            t = shard_at(s)
            active_grad = dot_nt(lfgrad[...], small[t, lwidth : 2 * lwidth, 0:lwidth])
            rounded = low(active_grad * lslope[s].astype(F32))
            total = row_sum(rounded.astype(F32))
            for k, (row, lane) in enumerate(((8, 0), (8, 256), (8, 512), (9, 0))):

                @pl.when(t == k)
                def _():
                    vec[row : row + 1, lane : lane + lwidth] = total

            lfeed[...] += dot_nt(rounded, small[t, 0:lwidth, 0:lwidth])
            up_block = low(dot(lh_t[...], rounded))
            down_block = low(dot(jnp.transpose(lact[s]), lfgrad[...]))
            for which, block in enumerate((up_block, down_block)):
                for q in range(lwidth // 64):
                    piece = jnp.concatenate([block[q * 64 : q * 64 + 64], empty], axis=1)
                    cols = slice(q * 256, q * 256 + 256)
                    put(tiles - 1, target, xs, TILE + 64 * which, piece, cols)

    loop(2, layout_grad)
    act_now((D, tiles - 1))

    def units_grad(s):
        t = shard_at(s)

        def units(j):
            cols = tile(j)
            place = pl.ds(pl.multiple_of(4 * width + t * width + j * TILE, 16), TILE)
            active_grad = dot_nt(fgrad[...], pool[place, :])
            slope = pool[page_rows(slope_at, s), cols].astype(F32)
            rounded = low(active_grad * slope)
            pool[page_rows(slope_at, s), cols] = rounded
            vec[pl.ds(3 + t, 1), cols] = row_sum(rounded.astype(F32))

        loop(tiles, units)
        for k in range(4):

            @pl.when(s == k)
            def _():
                act_now((UNITS, k))

    loop(4, units_grad)

    for i in range(tiles):
        outer_grad(tiles + i, h_t, slope_at, i)
        act_now((UP, i))

    def hidden_back(s):
        t = shard_at(s)

        def back(j):
            cols = tile(j)
            place = pl.ds(pl.multiple_of(t * width + j * TILE, 16), TILE)
            feed[:, cols] += dot_nt(pool[page_rows(slope_at, s), :], pool[place, :])

        loop(tiles, back)
        for k in range(4):

            @pl.when(s == k)
            def _():
                act_now((BACK, k))

    loop(4, hidden_back)
    for copy in messages:
        copy.wait_send()
    for item in flows[:feed_count]:
        item.steps[0][1].wait_send()
    for axis, (_, device) in where.items():
        pl.semaphore_signal(
            ready_sem.at[list(where).index(axis)],
            inc=1,
            device_id=device,
            device_id_type=MESH,
        )
    act_now((SYNC, 0))
    wo_again, wq_again, wk_again, wv_again = (
        recv.at[pl.ds(i * width, width)] for i in range(4)
    )
    again = [
        load(3, wo_hbm, wo_again),
        load(0, wq_hbm, wq_again),
        load(1, wk_hbm, wk_again),
        load(2, wv_hbm, wv_again),
    ]
    mixed, lmixed = fgrad, lfgrad

    def norm_grad(r, sums, source, gain, grad, grad_low):
        unit, spread = normed(source[r, 0 : grad.shape[1]])
        outer = grad[r, :]
        value = normed_back(unit, spread, outer * gain)
        grad[r, :] = value
        rounded = low(value)
        grad_low[r, :] = rounded
        return (
            sums[0] + row_sum(rounded.astype(F32)),
            sums[1] + row_sum(outer * unit),
            sums[2] + row_sum(outer),
        )

    def norm_grads(i, sums):
        r = tile(i, ROWS)
        return (
            norm_grad(r, sums[0], asum, gains[0], feed, mixed),
            norm_grad(r, sums[1], lasum, gains[2], lfeed, lmixed),
        )

    found, lfound = lax.fori_loop(0, PAGE // ROWS, norm_grads, start)
    for i in range(3):
        vec[12 + i : 13 + i, :] = found[i]
        vec[15:16, i * 256 : i * 256 + lwidth] = lfound[i]
    act_now((NORM, 0))
    again[0].wait()
    k_t, lk_t, cgrad_t, lcgrad = v_t, lv_t, h_t, lctx
    masks[...] = jnp.zeros_like(masks)

    def turn(j):
        x_t[tile(j), :] = jnp.transpose(x_ref[:, tile(j)])

    def context_back(j):
        cols = tile(j)
        value = low(dot_nt(mixed[...], wo_again[cols, :]))
        cgrad[:, cols] = value
        cgrad_t[cols, :] = jnp.transpose(value)
        shared[0:width, cols] = low(dot(ctx_t[...], mixed[:, cols]))
        k_t[cols, :] = jnp.transpose(kn[:, cols])

    loop(tiles, context_back)
    value = jnp.concatenate([low(dot_nt(lmixed[...], lwo[...])), pad], axis=1)
    lcgrad[...] = value
    lcgrad_t[...] = jnp.transpose(value)
    lk_t[...] = jnp.transpose(lkn[...])
    loop(tiles, turn)
    act_now((CONTEXT, 0))

    lane = lax.broadcasted_iota(jnp.int32, (PAGE, 128), 1)
    ldv[...] = jnp.zeros_like(ldv)
    ldk[...] = jnp.zeros_like(ldk)
    ldq_t[...] = jnp.zeros_like(ldq_t)

    def attend_back(pair):
        text, block = tile(pair, 128), tile(pair // 4, 128)
        keys = jnp.concatenate([kn[:, text], lkn[:, block]], axis=1)
        values = jnp.concatenate([vn[:, text], lvn[:, block]], axis=1)
        grads = jnp.concatenate([cgrad[:, text], lcgrad[:, block]], axis=1)
        found = []
        for side in range(2):
            head = 2 * pair + side
            head_rows(masked, q_t, lq_t, pair, side)
            head_rows(masked_c, cgrad_t, lcgrad_t, pair, side)
            span = slice(side * 256, side * 256 + 256)
            weights = jnp.exp(dot(keys, masked[span, :]) - lse[pl.ds(head, 1), :])
            value_grad = dot(low(weights), grads)
            text_wave = dot(vn[:, text], masked_c[side * 256 : side * 256 + 128, :])
            text_part = row_sum(text_wave * weights)
            text_score = low(weights * (text_wave - text_part))
            both_wave = dot(values, masked_c[span, :])
            both_part = row_sum(both_wave * weights)
            both_score = low(weights * (both_wave - both_part))
            query_grad = low(dot(k_t[tile(head, 64), :], text_score) * 0.125)
            ldq_t[tile(head, 16), :] = low(dot(lk_t[tile(head, 16), :], both_score) * 0.25)
            key_grad = dot(text_score, qn[:, text])
            lkey_grad = dot(both_score, lqn[:, block])
            own = (lane // 16) == (head % 8)
            ldv[:, block] = jnp.where(own, value_grad[:, 128:256], ldv[:, block])
            ldk[:, block] = jnp.where(own, lkey_grad, ldk[:, block])
            found.append((value_grad[:, 0:128], key_grad, query_grad))
        first_half = lane < 64
        dv[:, text] = low(jnp.where(first_half, found[0][0], found[1][0]))
        dk[:, text] = low(jnp.where(first_half, found[0][1], found[1][1]))
        dq[:, text] = jnp.transpose(jnp.concatenate([found[0][2], found[1][2]], axis=0))
        for k in range(HEADS // 2):

            @pl.when(pair == k)
            def _():
                act_now((ATTEND, k))

        @pl.when(pair % 2 == 1)
        def _():
            weight_grad(pair // 2)

        for k in range(tiles - 1):

            @pl.when(pair == 2 * k + 1)
            def _():
                act_now((WEIGHT, k))

    def weight_grad(group):
        cols = tile(group)
        place = pl.ds(pl.multiple_of((1 + group) * width, 16), width)
        for i, source in enumerate((dq, dk, dv)):
            shared[place, i * TILE : (i + 1) * TILE] = low(dot(x_t[...], source[:, cols]))
        vec[10:11, cols] = row_sum(dq[:, cols].astype(F32))
        vec[11:12, cols] = row_sum(dv[:, cols].astype(F32))

    loop(HEADS // 2, attend_back)

    query = jnp.transpose(ldq_t[...])[:, 0:lwidth]
    key, value = low(ldk[:, 0:lwidth]), low(ldv[:, 0:lwidth])
    parts = [low(dot(lx_t[...], item)) for item in (query, key, value)]
    parts.append(low(dot(lctx_t[0:lwidth, :], lmixed[...])))
    base = 4 * width
    shared[base : base + lwidth, :] = jnp.concatenate(parts, axis=1)
    vec[9:10, 256 : 256 + lwidth] = row_sum(query.astype(F32))
    vec[9:10, 512 : 512 + lwidth] = row_sum(value.astype(F32))
    base += lwidth
    shared[base : base + 16, :] = low(vec[...])
    shared[base + 16 : shared_rows, :] = jnp.zeros((shared_rows - base - 16, width), BF16)
    act_now((WEIGHT, tiles - 1))
    for copy in again[1:]:
        copy.wait()

    def input_back(j):
        cols = tile(j)
        feed[:, cols] += (
            dot_nt(dq[...], wq_again[cols, :])
            + dot_nt(dk[...], wk_again[cols, :])
            + dot_nt(dv[...], wv_again[cols, :])
        )
        for k in range(tiles):

            @pl.when(j == k)
            def _():
                act_now((INPUT, k))

    loop(tiles, input_back)
    in_grad_copy = load(4, feed, in_grad_out)
    lin_grad[...] = jnp.transpose(
        lfeed[...] + dot_nt(query, lwq[...]) + dot_nt(key, lwk[...]) + dot_nt(value, lwv[...])
    )
    act_now((END, 0))
    act_now((TAIL, 0))
    for item in flows:
        item.drain()
    in_grad_copy.wait()


def finish_kernel(feed_rows, sums_hbm, *refs):
    passed, outs = refs[0:4], refs[4:38]
    sums, wide_sums, vec = refs[38:41]
    through = refs[41:45]
    load_sem, store_sem, in_sem, out_sem = refs[45:49]
    width, lwidth = wide_sums.shape[1], through[1].shape[0]
    down_rows = width + 128
    starts = (feed_rows, 0, down_rows, feed_rows + width, feed_rows + 2 * width)
    starts += (feed_rows + 3 * width, feed_rows + 4 * width)
    sizes = [width, down_rows] + [width] * 4 + [sums.shape[0] - starts[-1]]
    loads = []
    for i, (start, size) in enumerate(zip(starts, sizes)):
        part = pl.ds(start, size)
        copy = pltpu.make_async_copy(sums_hbm.at[part], sums.at[part], load_sem.at[i])
        copy.start()
        loads.append(copy)
    takes = [
        pltpu.make_async_copy(a, b, in_sem.at[i]) for i, (a, b) in enumerate(zip(passed, through))
    ]
    gives = [
        pltpu.make_async_copy(a, b, out_sem.at[i]) for i, (a, b) in enumerate(zip(through, outs))
    ]
    for copy in takes:
        copy.start()

    def widen(slot, start, cols=None, lanes=None):
        def block(i):
            source = pl.ds(start + pl.multiple_of(i * 128, 128), 128)
            target = pl.ds(pl.multiple_of(i * 128, 128), 128)
            if cols is None:
                wide_sums[slot, target, :] = sums[source, :].astype(F32)
            else:
                wide_sums[slot, target, lanes] = sums[source, cols].astype(F32)

        loop(width // 128, block)

    text, layout = outs[4:19], outs[19:34]
    stores = []

    def store(slot, out):
        copy = pltpu.make_async_copy(wide_sums.at[slot], out, store_sem.at[slot])
        copy.start()
        stores.append(copy)

    loads[0].wait()
    widen(0, starts[0])
    store(0, text[5])
    blocks = range(width // TILE)
    for slot, out in ((1, text[11]), (2, text[9])):
        loads[slot].wait()
        for i in blocks:
            for q in blocks:
                rows = pl.ds(starts[slot] + i * TILE, TILE)
                value = sums[rows, q * TILE : (q + 1) * TILE].astype(F32)
                place = (i, q) if slot == 1 else (q, i)
                value = jnp.transpose(value) if slot == 1 else value
                down, across = (pl.ds(k * TILE, TILE) for k in place)
                wide_sums[slot, down, across] = value
        store(slot, out)
    for copy, give in zip(takes, gives):
        copy.wait()
        give.start()
    for g in range(width // TILE):
        loads[3 + g].wait()
        for i in range(3):
            lanes = slice(g * TILE, (g + 1) * TILE)
            widen(3 + i, starts[3 + g], slice(i * TILE, (i + 1) * TILE), lanes)
    for i, out in enumerate((text[0], text[2], text[3])):
        store(3 + i, out)
    loads[6].wait()
    base = starts[6]
    for i, out in enumerate((layout[0], layout[2], layout[3], layout[5])):
        out[...] = sums[base : base + lwidth, i * lwidth : (i + 1) * lwidth].astype(F32)
    for i, out in enumerate((layout[9], layout[11])):
        for q in range(lwidth // 64):
            rows = sums[width + 64 * i : width + 64 * i + 64, q * TILE : q * TILE + lwidth]
            out[q * 64 : q * 64 + 64, :] = rows.astype(F32)
    vec[...] = sums[base + lwidth : base + lwidth + 16, :].astype(F32)
    me = lax.axis_index("tensor")
    for row, out in ((10, 1), (11, 4), (12, 6), (13, 7), (14, 8), (2, 12), (0, 13), (1, 14)):
        text[out][...] = vec[row, :]
    text[10][...] = vec[pl.ds(3 + me, 1), :][0]

    def strip(row, part):
        return vec[row : row + 1, part * TILE : part * TILE + lwidth]

    places = ((9, 1, 1), (9, 2, 4), (15, 0, 6), (15, 1, 7), (15, 2, 8))
    for row, part, out in places + ((7, 2, 12), (7, 0, 13), (7, 1, 14)):
        layout[out][...] = strip(row, part)[0]
    rise = strip(8, 0)
    for k, (row, part) in enumerate(((8, 1), (8, 2), (9, 0))):
        rise = jnp.where(me == k + 1, strip(row, part), rise)
    layout[10][...] = rise[0]
    for copy in stores + gives:
        copy.wait()


MOVES = {
    (D, 0): (11,),
    (D, 1): (12,),
    (D, 2): (13, 0, 11, 1, 12),
    (UNITS, 2): (2, 13),
    (UP, 0): (14,),
    (UP, 1): (15,),
    (UP, 2): (16,),
    (BACK, 1): (3, 0, 11, 1, 12, 4),
    (BACK, 2): (5, 15),
    (BACK, 3): (16,),
    (NORM, 0): (14,),
    (CONTEXT, 0): (17, 0, 1, 2),
    (ATTEND, 0): (13, 6, 11, 17),
    (ATTEND, 1): (12, 4, 5, 3, 16),
    (WEIGHT, 0): (18, 14, 0, 11),
    (ATTEND, 2): (1, 15, 12, 2, 6, 17, 7),
    (ATTEND, 3): (18, 5, 13, 16, 0, 3, 14),
    (WEIGHT, 1): (19, 6, 1, 12, 17),
    (ATTEND, 4): (11, 4, 15, 5, 16, 8, 19, 3, 2),
    (ATTEND, 5): (13, 6, 7, 18, 1, 0, 4),
    (WEIGHT, 2): (20, 21, 11, 5, 17),
    (INPUT, 0): (7, 8, 9, 20, 18),
    (INPUT, 1): (10, 21, 14, 2),
    (INPUT, 2): (0,),
    (END, 0): (19, 6),
    (TAIL, 0): (7, 18, 9, 20, 13, 10, 17, 3, 8, 21, 19, 9, 20, 7, 6, 17, 18, 2, 15, 8, 9, 10, 7, 18, 6, 19, 4, 17, 21, 20, 7, 18, 8, 19, 10, 21, 9, 15, 20, 8, 14, 6, 17, 19, 16, 10, 7, 18, 9, 20, 4, 21, 6, 3, 14, 13, 7, 9, 5, 8, 19, 10, 21, 3, 20, 12, 10, 21, 2, 16, 8, 19, 15, 9, 20, 8, 1, 9, 10, 21, 5, 10, 4),
}
FEED_ORDERS = ((0, 1, ACROSS), (1, 0, ACROSS), (ACROSS, 1, 0), (ACROSS, 0, 1), (1, 0, ACROSS), (0, ACROSS, 1))
SHARED_ORDERS = ((0, ACROSS, 1), (ACROSS, 0, 1), (ACROSS, 0, 1), (0, ACROSS, 1), (ACROSS, 0, 1))

START = (3, 2, 39, 42, 18, 21, 22, 41, 1, 0, 19, 38, 20, 37)
GATHER = {
    (SETUP, 0): (39, 42),
    (PROJECT, 2): (3, 18),
    (HEAD, 0): (2, 37),
    (HEAD, 2): (21, 8),
    (HEAD, 3): (22, 41),
    (HEAD, 4): (6, 16),
    (HEAD, 5): (43, 1),
    (MIX, 0): (25, 14, 0, 27, 12),
    (FIRST, 0): (19, 33, 10),
    (FED, 0): (35, 9, 7, 29),
    (FED, 1): (4, 38, 5, 17),
    (FED, 2): (15, 11, 20),
    (FEED, 3): (40, 13),
    (FED, 3): (28, 31),
    (DONE, 0): (26, 23),
    (DONE, 1): (36,),
    (DOWN, 2): (24,),
    (DONE, 2): (34, 30),
    (DOWN, 3): (32,),
}


def on_device(dp, tensor, *args):
    (
        text_in,
        layout_in,
        token_mask,
        box_mask,
        cot_text,
        cot_layout,
    ) = args[:6]
    text, layout = args[6:21], args[21:36]
    width, lwidth = text_in.shape[1], layout_in.shape[1]
    dp_bits = dp.bit_length() - 1
    half = width // 2
    feed_flows = tuple(zip((TILE, TILE, TILE + 128, TILE, TILE, TILE), FEED_ORDERS))
    shared_flows = tuple(zip((width, width, width, half + 128, half + 128), SHARED_ORDERS))
    moves = MOVES if dp_bits == 3 else {}
    feed_rows = sum(rows for rows, _ in feed_flows)
    shared_rows = sum(rows for rows, _ in shared_flows)
    land = sum(landing(4 * rows, dp_bits + 2) for rows, _ in feed_flows)
    shared_land = sum(landing(rows, dp_bits + 2) for rows, _ in shared_flows)
    pool_rows = max(8 * width + 8 * PAGE, 2 * shared_rows + 4 * PAGE + width)
    count = (2 * dp_bits + 2) * len(feed_flows) + (2 * dp_bits + 4) * len(shared_flows)

    vmem = pl.BlockSpec(memory_space=pltpu.VMEM)
    hbm = pl.BlockSpec(memory_space=pl.ANY)
    page = PAGE

    def shape(*dims, dtype=BF16):
        return jax.ShapeDtypeStruct(dims, dtype)

    def row(vector):
        return vector.reshape(1, vector.shape[0])

    inputs = (text_in, layout_in.T, row(token_mask), row(box_mask), cot_text, cot_layout.T)
    inputs += text + layout
    specs = [vmem] * len(inputs)
    for i in (6, 8, 9, 11, 15, 17):
        specs[i] = hbm
    outs = (
        shape(page, width),
        shape(lwidth, page),
        shape(page, width, dtype=F32),
        shape(lwidth, page, dtype=F32),
        shape(feed_rows + shared_rows, width),
    )
    scratch = [
        pltpu.VMEM((pool_rows, width), BF16),
        pltpu.VMEM((2 * feed_rows, width), BF16),
        pltpu.VMEM((max(2 * feed_rows, shared_land), width), BF16),
        pltpu.VMEM((land, width), BF16),
        pltpu.VMEM((feed_rows, width), BF16),
        pltpu.VMEM((4, 2 * lwidth, 256), BF16),
        pltpu.VMEM((4, 8, 256), F32),
        pltpu.VMEM((page, width), BF16),
        pltpu.VMEM((page, width), BF16),
        pltpu.VMEM((page, width), BF16),
        pltpu.VMEM((width, page), BF16),
        pltpu.VMEM((width, page), BF16),
        pltpu.VMEM((page, 256), BF16),
        pltpu.VMEM((page, 256), BF16),
        pltpu.VMEM((page, 256), BF16),
        pltpu.VMEM((256, page), BF16),
        pltpu.VMEM((256, page), BF16),
        pltpu.VMEM((16, page), F32),
        pltpu.VMEM((1024, page), BF16),
        pltpu.VMEM((width, page), BF16),
        pltpu.VMEM((256, page), BF16),
        pltpu.VMEM((page, 256), BF16),
        pltpu.VMEM((page, width), F32),
        pltpu.VMEM((page, width), BF16),
        pltpu.VMEM((page, lwidth), BF16),
        pltpu.VMEM((width, page), BF16),
        pltpu.VMEM((lwidth, page), BF16),
        pltpu.VMEM((page, width), F32),
        pltpu.VMEM((page, lwidth), F32),
        pltpu.VMEM((4, page, lwidth), BF16),
        pltpu.VMEM((4, page, lwidth), BF16),
        pltpu.VMEM((page, 16), F32),
        pltpu.VMEM((8, width), F32),
        pltpu.VMEM((page, lwidth), BF16),
        pltpu.VMEM((page, lwidth), BF16),
        pltpu.VMEM((256, page), BF16),
        pltpu.VMEM((256, page), BF16),
        pltpu.VMEM((page, 256), F32),
        pltpu.VMEM((page, 256), F32),
        pltpu.VMEM((16, width), F32),
        pltpu.SemaphoreType.DMA((6,)),
        pltpu.SemaphoreType.DMA((48,)),
        pltpu.SemaphoreType.DMA((48,)),
        pltpu.SemaphoreType.DMA((count,)),
        pltpu.SemaphoreType.DMA((count,)),
        pltpu.SemaphoreType.DMA((len(feed_flows) + len(shared_flows),)),
        pltpu.SemaphoreType.REGULAR((dp_bits + 2,)),
    ]
    text_out, layout_out, in_grad, lin_grad, sums = pl.pallas_call(
        functools.partial(layer_kernel, (dp_bits, feed_flows, shared_flows, moves)),
        out_shape=outs,
        in_specs=specs,
        out_specs=[vmem, vmem, hbm, vmem, hbm],
        scratch_shapes=scratch,
        compiler_params=pltpu.CompilerParams(
            collective_id=0, has_side_effects=True, vmem_limit_bytes=67043328
        ),
        name="layer",
    )(*inputs)

    big, small_square = shape(width, width, dtype=F32), shape(lwidth, lwidth, dtype=F32)

    def stream(square, size):
        line = shape(size, dtype=F32)
        order = (square, line, square, square, line, square, line, line, line)
        return order + (square, line, square, line, line, line)

    outs = (
        shape(page, width),
        shape(lwidth, page),
        shape(page, width, dtype=F32),
        shape(lwidth, page, dtype=F32),
    )
    outs += stream(big, width) + stream(small_square, lwidth)
    specs = [hbm if i < 4 or out.shape == (width, width) else vmem for i, out in enumerate(outs)]
    done = pl.pallas_call(
        functools.partial(finish_kernel, feed_rows),
        out_shape=outs,
        in_specs=[hbm] * 5,
        out_specs=specs,
        scratch_shapes=[
            pltpu.VMEM((feed_rows + shared_rows, width), BF16),
            pltpu.VMEM((6, width, width), F32),
            pltpu.VMEM((16, width), F32),
            pltpu.VMEM((page, width), BF16),
            pltpu.VMEM((lwidth, page), BF16),
            pltpu.VMEM((page, width), F32),
            pltpu.VMEM((lwidth, page), F32),
            pltpu.SemaphoreType.DMA((7,)),
            pltpu.SemaphoreType.DMA((6,)),
            pltpu.SemaphoreType.DMA((4,)),
            pltpu.SemaphoreType.DMA((4,)),
        ],
        compiler_params=pltpu.CompilerParams(vmem_limit_bytes=60000000),
        name="finish",
    )(sums, text_out, layout_out, in_grad, lin_grad)
    return (done[0], done[1].T, done[2], done[3].T) + tuple(done[4:])


def solution(mesh):
    rows = P(("dp", "tensor"), None)
    line = P(("dp", "tensor"))
    weights = (P(),) * 9 + (P(None, "tensor"), P("tensor"), P("tensor", None)) + (P(),) * 3
    in_specs = (rows, rows, line, line, rows, rows) + weights + weights
    out_specs = (rows,) * 4 + weights + weights
    return jax.shard_map(
        functools.partial(on_device, mesh.shape["dp"], mesh.shape["tensor"]),
        mesh=mesh,
        in_specs=in_specs,
        out_specs=out_specs,
        check_vma=False,
    )
```

```python
import functools

import jax
import jax.numpy as jnp
from jax import lax
from jax.experimental import pallas as pl
from jax.experimental.pallas import tpu as pltpu
from jax.sharding import PartitionSpec as P

HEADS = 12
PAGE = 512
NORM_EPS = 1e-05
MESH = pl.DeviceIdType.MESH
F32 = jnp.float32
BF16 = jnp.bfloat16
TILE = 256
ROWS = 128
CORE, ACROSS = 100, 101
SETUP, PROJECT, LAYOUT, HEAD, MIX, FIRST, FEED, FED, DOWN, DONE = range(10)
D, UNITS, UP, BACK, NORM, CONTEXT, ATTEND, WEIGHT, INPUT, END, TAIL, SYNC, LAY = range(10, 23)


def low(values):
    return values.astype(BF16)


def dot(first, second):
    return jnp.dot(first, second, preferred_element_type=F32)


def dot_nt(first, second):
    return lax.dot_general(first, second, (((1,), (1,)), ((), ())), preferred_element_type=F32)


def tile(index, size=TILE):
    return pl.ds(pl.multiple_of(index * size, size), size)


def loop(count, body):
    def step(index, carry):
        body(index)
        return carry

    lax.fori_loop(0, count, step, 0, unroll=count if count < 4 else 1)


def flip(bit):
    return 1 - 2 * bit


def wide(vector_ref):
    return vector_ref[...].astype(F32)[None, :]


def lane_mean(values):
    return jnp.mean(values, axis=-1, keepdims=True)


def row_sum(values):
    return jnp.sum(values, axis=0, keepdims=True)


def normed(values):
    centered = values - lane_mean(values)
    scale = lax.rsqrt(lane_mean(centered * centered) + NORM_EPS)
    return centered * scale, scale


def normed_back(unit, scale, grad):
    return (grad - lane_mean(grad) - unit * lane_mean(grad * unit)) * scale


def landing(rows, stages):
    total = 0
    for stage in range(stages):
        rows = rows // 2 if rows % 32 == 0 and stage + 1 < stages else rows
        total += rows
    return total


def copy_to(source, target, send, recv, device):
    return pltpu.make_async_remote_copy(
        src_ref=source,
        dst_ref=target,
        send_sem=send,
        recv_sem=recv,
        device_id=device,
        device_id_type=MESH,
    )


def greet(devices):
    barrier = pltpu.get_barrier_semaphore()
    for device in devices:
        pl.semaphore_signal(barrier, inc=1, device_id=device, device_id_type=MESH)
    pl.semaphore_wait(barrier, len(devices))


def mask_column(text_mask, layout_mask, column_ref):
    parts = []
    for mask_ref in (text_mask, layout_mask):
        scale = 0.5 + 1.5 * mask_ref[...].astype(F32)
        parts.append(jnp.broadcast_to(scale, (8, PAGE)))
    column_ref[...] = jnp.transpose(jnp.concatenate(parts, axis=0))


def head_rows(target, text_rows, layout_rows, pair, side):
    head = 2 * pair + side
    top = side * 256
    target[top + 128 : top + 256, :] = jnp.zeros((128, PAGE), BF16)
    target[top + side * 64 : top + side * 64 + 64, :] = text_rows[tile(head, 64), :]
    spot = pl.ds(pl.multiple_of(top + 128 + (head % 8) * 16, 16), 16)
    target[spot, :] = layout_rows[tile(head, 16), :]


class Flow:
    def __init__(self, where, axes, spread, rows, give, keep, lands, whole, sems, ready, result):
        self.steps, self.ready = [], ready
        self.result = pltpu.make_async_copy(whole, *result)
        send_sem, recv_sem, index = sems
        offset, size, place = 0, rows, 0
        halved = []
        for stage, axis in enumerate(axes):
            bit, device = where[axis]
            recv = lands[min(stage, 1)]
            if stage == 1:
                place = 0
            if size % 32 == 0 and stage + 1 < len(axes):
                half = size // 2
                kept, given = offset + bit * half, offset + (1 - bit) * half
                halved.append(axis)
            else:
                half, kept, given = size, offset, offset
            first = stage == 0 and give is not keep
            source = give.at[pl.ds(0, half)] if first else self.span(keep, given, half)
            kept = 0 if first else kept
            copy = copy_to(
                source,
                recv.at[pl.ds(place, half)],
                send_sem.at[index],
                recv_sem.at[index],
                device,
            )
            last = stage + 1 == len(axes)
            target, start = keep, kept
            if last:
                target, start = whole, 0
                step, gathers = whole.shape[0], []
                for other in spread:
                    if other in halved:
                        step //= 2
                        start = start + where[other][0] * step
                        gathers.insert(0, (other, step))
            swap = half == size and not last
            self.steps.append((axis, copy, (keep, kept, recv, place, target, start, half, swap)))
            offset, size = kept, half
            place += half
            index += 1
        spot = start
        for axis, step in gathers:
            bit, device = where[axis]
            span = self.span(whole, spot, step)
            copy = copy_to(span, span, send_sem.at[index], recv_sem.at[index], device)
            self.steps.append((axis, copy, None))
            spot = spot - bit * step
            index += 1

    def span(self, ref, offset, size):
        return ref.at[pl.ds(pl.multiple_of(offset, 16), size)]

    def launch(self, step, waits):
        axis, copy, _ = self.steps[step]
        if waits:
            pl.semaphore_wait(self.ready[axis], 1)
        copy.start()

    def absorb(self, step):
        _, copy, rest = self.steps[step]
        copy.wait_recv()
        if rest is not None:
            keep, kept, recv, place, target, start, half, swap = rest
            if swap:
                copy.wait_send()
            block = max(b for b in range(16, 129, 16) if half % b == 0)

            def add(i):
                mine = pl.ds(pl.multiple_of(kept + i * block, 16), block)
                theirs = pl.ds(pl.multiple_of(place + i * block, 16), block)
                result = pl.ds(pl.multiple_of(start + i * block, 16), block)
                target[result, :] = keep[mine, :] + recv[theirs, :]

            loop(half // block, add)
        if step + 1 == len(self.steps):
            self.result.start()

    def drain(self):
        self.result.wait()
        for _, copy, rest in self.steps[1 if self.ready is None else 0 :]:
            if rest is None or not rest[-1]:
                copy.wait_send()


class Script:
    def __init__(self, flows, greeted):
        self.flows, self.greeted = flows, greeted
        self.started, self.taken = [0] * len(flows), [0] * len(flows)
        self.points = {}

    def write(self, point, number):
        kind, flow = divmod(number, len(self.flows))
        done = self.started if kind else self.taken
        step = done[flow]
        done[flow] += 1
        waits = False
        if kind and self.flows[flow].ready is not None:
            axis = self.flows[flow].steps[step][0]
            waits = axis not in self.greeted
            self.greeted.add(axis)
        self.points.setdefault(point, []).append((kind, flow, step, waits))

    def play(self, point):
        for kind, flow, step, waits in self.points.get(point, ()):
            if kind:
                self.flows[flow].launch(step, waits)
            else:
                self.flows[flow].absorb(step)

    def finish(self, point):
        flows, going = self.flows, True
        while going:
            going = False
            for i, flow in enumerate(flows):
                if self.started[i] > self.taken[i]:
                    self.write(point, i)
                    going = True
                if self.started[i] == self.taken[i] and self.taken[i] < len(flow.steps):
                    self.write(point, len(flows) + i)
                    going = True


def layer_kernel(plan, *refs):
    (
        x_ref,
        lx_t,
        token_mask,
        box_mask,
        cot_ref,
        lcot_ref,
        wq_hbm,
        bq,
        wk_hbm,
        wv_hbm,
        bv,
        wo_hbm,
        bo,
        attend_gain,
        attend_shift,
        up_hbm,
        up_bias,
        down_hbm,
        down_bias,
        feed_gain,
        feed_shift,
        lwq,
        lbq,
        lwk,
        lwv,
        lbv,
        lwo,
        lbo,
        lattend_gain,
        lattend_shift,
        lup,
        lup_bias,
        ldown,
        ldown_bias,
        lfeed_gain,
        lfeed_shift,
        out_ref,
        lout_ref,
        in_grad_out,
        lin_grad,
        sums_out,
        pool,
        acc,
        staging,
        recv,
        sums,
        small,
        small_bias,
        qn,
        kn,
        vn,
        q_t,
        v_t,
        lqn,
        lkn,
        lvn,
        lq_t,
        lv_t,
        lse,
        masks,
        ctx_t,
        lctx_t,
        lctx,
        asum,
        hlow,
        lhlow,
        h_t,
        lh_t,
        feed,
        lfeed,
        lact,
        lslope,
        column,
        rises,
        lx,
        lcot,
        lcgrad_t,
        ldq_t,
        ldk,
        ldv,
        vec,
        local_sem,
        gather_send,
        gather_recv,
        send_sem,
        recv_sem,
        out_sem,
        ready_sem,
    ) = refs
    dp_bits, feed_flows, shared_flows, moves = plan
    fgrad, lfgrad, lout, lasum = hlow, lhlow, lx, ldk
    masked, masked_c = masks.at[pl.ds(0, 512)], masks.at[pl.ds(512, 512)]
    fgrad_t = masks.at[pl.ds(0, x_ref.shape[1])]
    d, me = lax.axis_index("dp"), lax.axis_index("tensor")
    c, x = me % 2, me // 2
    width, lwidth = x_ref.shape[1], lx_t.shape[0]
    tiles = width // TILE
    where = {CORE: (c, (d, me + flip(c))), ACROSS: (x, (d, me + 2 * flip(x)))}
    for k in range(dp_bits):
        bit = (d // 2**k) % 2
        where[k] = (bit, (d + 2**k * flip(bit), me))
    core, across = where[CORE][1], where[ACROSS][1]
    y, beside = where[0]
    z, ahead = where[1]
    other = me + 2 * flip(x)

    def part(start, size):
        return pool.at[pl.ds(start, size)]

    wu, wd = part(0, 4 * width), part(4 * width, 4 * width)
    act_at, slope_at = 8 * width, 8 * width + 4 * PAGE
    wq, wk = part(act_at, width), part(act_at + width, width)
    wv, wo = part(act_at + 2 * width, width), part(act_at + 3 * width, width)
    ctx = part(act_at + 4 * width, PAGE)
    shared_rows = sum(rows for rows, _ in shared_flows)
    shared, shared_sum = part(0, shared_rows), part(shared_rows, shared_rows)
    spot = 2 * shared_rows
    dq, dk, dv = part(spot, PAGE), part(spot + PAGE, PAGE), part(spot + 2 * PAGE, PAGE)
    cgrad = part(spot + 3 * PAGE, PAGE)
    x_t = pool.at[pl.ds(spot + 4 * PAGE, width), pl.ds(0, PAGE)]

    def shard_rows(base, t, start=0, size=width):
        return pl.ds(pl.multiple_of(base + t * width + start, 16), size)

    small[me, 0:lwidth, 0:lwidth] = lup[...]
    small[me, lwidth : 2 * lwidth, 0:lwidth] = ldown[...]
    for j in range(tiles):
        small_bias[me, j : j + 1, :] = wide(up_bias)[:, j * TILE : (j + 1) * TILE]
    small_bias[me, 3:4, 0:lwidth] = wide(lup_bias)

    def load(index, source, target):
        copy = pltpu.make_async_copy(source, target, local_sem.at[index])
        copy.start()
        return copy

    loads = [load(i, s, t) for i, (s, t) in enumerate(((wq_hbm, wq), (wk_hbm, wk), (wv_hbm, wv)))]
    load_wo = load(3, wo_hbm, wo)
    keep_up = load(4, up_hbm, pool.at[shard_rows(0, me)])
    keep_down = load(5, down_hbm, pool.at[shard_rows(4 * width, me)])
    greet([device for _, device in where.values()])

    messages, needs = [], []

    def message(source, target, device, *after):
        index = len(messages)
        copy = copy_to(source, target, gather_send.at[index], gather_recv.at[index], device)
        messages.append(copy)
        needs.append(set(after))

    for base, hbm in ((0, up_hbm), (4 * width, down_hbm)):
        grain = width // 12
        zero = len(messages)

        def relay(start, size, device, *after):
            place = pool.at[shard_rows(base, other, start * grain, size * grain)]
            message(place, place, device, *(zero + item for item in after))

        own = (y, 2 + z, 4 + 2 * z + y, 8 + 2 * y + z)
        for start in own:
            source = hbm.at[pl.ds(pl.multiple_of(start * grain, 16), grain)]
            message(source, pool.at[shard_rows(base, me, start * grain, grain)], across)
        relay(own[0], 1, beside, 0)
        relay(own[1], 1, ahead, 1)
        relay(own[2], 1, beside, 2)
        relay(4 + 2 * z, 2, ahead, 2, 6)
        relay(own[3], 1, ahead, 3)
        relay(8 + 2 * y, 2, beside, 3, 8)
        relay(own[0], 1, core, 0)
        relay(1 - y, 1, core, 4)
        relay(own[1], 1, core, 1)
        relay(3 - z, 1, core, 5)
        relay(4 + 2 * z, 2, core, 2, 6)
        relay(6 - 2 * z, 2, core, 7)
        relay(8 + 2 * y, 2, core, 3, 8)
        relay(10 - 2 * y, 2, core, 9)
        message(hbm, pool.at[shard_rows(base, me)], core)
    for ref in (small, small_bias):
        message(ref.at[me], ref.at[me], across)
        message(ref.at[me], ref.at[me], core)
        message(ref.at[other], ref.at[other], core, len(messages) - 2)
    begun, got = set(START), set()
    for index in START:
        messages[index].start()

    def take(stage, k=0):
        for index in GATHER.get((stage, k), ()):
            messages[index].wait_recv()
            got.add(index)
            for later, after in enumerate(needs):
                if later not in begun and after <= got:
                    messages[later].start()
                    begun.add(later)

    def take_at(index, stage):
        for k in range(8):
            if (stage, k) in GATHER:

                @pl.when(index == k)
                def _():
                    take(stage, k)

    lx[...] = jnp.transpose(lx_t[...])
    lcot[...] = jnp.transpose(lcot_ref[...])
    mask_column(token_mask, box_mask, column)
    masks[...] = jnp.zeros_like(masks)
    vec[...] = jnp.zeros_like(vec)
    rises[0:1, :] = wide(bq)
    rises[1:2, :] = wide(bv)
    rises[2:3, :] = wide(bo)
    for copy in loads:
        copy.wait()
    take(SETUP)

    def project(j):
        cols = tile(j)
        rows = x_ref[...]
        queries = low(dot(rows, wq[:, cols]) + rises[0:1, cols]) * 0.125
        qn[:, cols] = queries
        q_t[cols, :] = jnp.transpose(queries)
        kn[:, cols] = low(dot(rows, wk[:, cols]))
        values = low(dot(rows, wv[:, cols]) + rises[1:2, cols])
        vn[:, cols] = values
        v_t[cols, :] = jnp.transpose(values)
        take_at(j, PROJECT)

    loop(tiles, project)
    pad = jnp.zeros((PAGE, 256 - lwidth), BF16)
    rows = lx[...]
    queries = low(dot(rows, lwq[...]) + wide(lbq)) * 0.25
    queries = jnp.concatenate([queries, pad], axis=1)
    lqn[...] = queries
    lq_t[...] = jnp.transpose(queries)
    lkn[...] = jnp.concatenate([low(dot(rows, lwk[...])), pad], axis=1)
    values = low(dot(rows, lwv[...]) + wide(lbv))
    values = jnp.concatenate([values, pad], axis=1)
    lvn[...] = values
    lv_t[...] = jnp.transpose(values)
    lctx_t[...] = jnp.zeros_like(lctx_t)
    take(LAYOUT)

    def attend(pair):
        keys = jnp.concatenate([kn[:, tile(pair, 128)], lkn[:, tile(pair // 4, 128)]], axis=1)
        for side in range(2):
            head = 2 * pair + side
            head_rows(masked, q_t, lq_t, pair, side)
            joint = dot(keys, masked[side * 256 : side * 256 + 256, :])
            highest = jnp.max(joint, axis=0, keepdims=True)
            exponent = jnp.exp(joint - highest)
            totals = row_sum(exponent)
            weights = low(exponent * (1.0 / totals))
            lse[pl.ds(head, 1), :] = highest + jnp.log(totals)
            values = jnp.concatenate([v_t[tile(head, 64), :], lv_t[tile(head, 16), :]], axis=0)
            context = low(dot(values, weights))
            ctx_t[tile(head, 64), :] = context[0:64]
            lctx_t[tile(head, 16), :] = context[64:80]

        take_at(pair, HEAD)

    loop(HEADS // 2, attend)

    def untranspose(j):
        ctx[:, tile(j)] = jnp.transpose(ctx_t[tile(j), :])

    loop(tiles, untranspose)
    lctx[...] = jnp.transpose(lctx_t[...])
    load_wo.wait()

    def mix(j):
        cols = tile(j)
        asum[:, cols] = x_ref[:, cols].astype(F32) + dot(ctx[...], wo[:, cols]) + rises[2:3, cols]

    loop(tiles, mix)
    lasum[:, 0:lwidth] = lx[...].astype(F32) + dot(lctx[:, 0:lwidth], lwo[...]) + wide(lbo)

    def first_norm(r, source, gain, shift, hidden, hidden_low):
        unit, _ = normed(source[r, 0 : hidden.shape[1]])
        value = unit * gain + shift
        hidden[r, :] = value
        hidden_low[r, :] = low(value)

    gains = [wide(item) for item in (attend_gain, attend_shift, lattend_gain, lattend_shift)]

    def first_norms(i):
        r = tile(i, ROWS)
        first_norm(r, asum, gains[0], gains[1], feed, hlow)
        first_norm(r, lasum, gains[2], gains[3], lfeed, lhlow)

    take(MIX)
    loop(PAGE // ROWS, first_norms)
    h_t[...] = jnp.transpose(hlow[...])
    lh_t[...] = jnp.transpose(lhlow[...])
    take(FIRST)

    def shard_at(s):
        return (x + s // 2 - 2 * x * (s // 2)) * 2 + c + s % 2 - 2 * c * (s % 2)

    def page_rows(base, s):
        return pl.ds(pl.multiple_of(base + s * PAGE, PAGE), PAGE)

    def gelu(u):
        square = u * u
        inner = 0.7978845608028654 * (u + 0.044715 * (square * u))
        wave = jnp.tanh(inner)
        rise = 0.5 * (1.0 + wave)
        bend = 0.5 * u * (1.0 - wave * wave)
        grow = 0.7978845608028654 * (1.0 + 0.134145 * square)
        return u * rise, rise + bend * grow

    keep_up.wait()

    def feed_up(s):
        t = shard_at(s)

        take_at(s, FEED)

        def up(j):
            cols = tile(j)
            weights = pool[shard_rows(0, t), cols]
            preact = dot(hlow[...], weights) + small_bias[t, pl.ds(j, 1), :]
            value, gradient = gelu(preact)
            pool[page_rows(act_at, s), cols] = low(value)
            pool[page_rows(slope_at, s), cols] = low(gradient)

        loop(tiles, up)
        preact = dot(lhlow[...], small[t, 0:lwidth, 0:lwidth]) + small_bias[t, 3:4, 0:lwidth]
        value, gradient = gelu(preact)
        lact[s] = low(value)
        lslope[s] = low(gradient)
        take_at(s, FED)

    loop(4, feed_up)
    keep_down.wait()

    def feed_down(s):
        t = shard_at(s)

        take_at(s, DOWN)

        def down(j):
            cols = tile(j)
            active = pool[page_rows(act_at, s), :]
            feed[:, cols] += dot(active, pool[shard_rows(4 * width, t), cols])

        loop(tiles, down)
        lfeed[...] += dot(lact[s], small[t, lwidth : 2 * lwidth, 0:lwidth])
        take_at(s, DONE)

    loop(4, feed_down)

    def second_norm(r, sums, fed, bias, gain, shift, cot, scale, out, grad_low):
        unit, spread = normed(fed[r, :] + bias)
        out[r, :] = low(unit * gain + shift)
        outer = cot[r, :].astype(F32) * column[r, scale : scale + 1]
        value = normed_back(unit, spread, outer * gain)
        fed[r, :] = value
        rounded = low(value)
        grad_low[r, :] = rounded
        return (
            sums[0] + row_sum(outer * unit),
            sums[1] + row_sum(outer),
            sums[2] + row_sum(rounded.astype(F32)),
        )

    tops = [wide(item) for item in (down_bias, feed_gain, feed_shift)]
    ltops = [wide(item) for item in (ldown_bias, lfeed_gain, lfeed_shift)]

    def second_norms(i, sums):
        r = tile(i, ROWS)
        return (
            second_norm(r, sums[0], feed, *tops, cot_ref, 0, out_ref, fgrad),
            second_norm(r, sums[1], lfeed, *ltops, lcot, 8, lout, lfgrad),
        )

    none, lnone = jnp.zeros((1, width), F32), jnp.zeros((1, lwidth), F32)
    start = ((none, none, none), (lnone, lnone, lnone))
    found, lfound = lax.fori_loop(0, PAGE // ROWS, second_norms, start)
    lout_ref[...] = jnp.transpose(lout[...])
    for i in range(3):
        vec[i : i + 1, :] = found[i]
        vec[7:8, i * 256 : i * 256 + lwidth] = lfound[i]

    deep = tuple(range(2, dp_bits))
    flows = []
    index, keep_at, recv_at, sum_at = 0, 0, 2 * sums.shape[0], 0
    places = []
    for rows, order in feed_flows:
        order = order + tuple(axis for axis in deep if axis not in order)
        depth = order.index(ACROSS)
        places.append((keep_at, rows >> depth))
        size = landing(4 * rows, len(order) + 1) - 2 * rows
        lands = recv.at[pl.ds(keep_at, 2 * rows)], recv.at[pl.ds(recv_at, size)]
        flows.append(
            Flow(
                where,
                (CORE,) + order,
                [axis for axis in order if axis != ACROSS],
                4 * rows,
                staging.at[pl.ds(keep_at, 2 * rows)],
                acc.at[pl.ds(keep_at, 2 * rows)],
                lands,
                sums.at[pl.ds(sum_at, rows)],
                (send_sem, recv_sem, index),
                None,
                (sums_out.at[pl.ds(sum_at, rows)], out_sem.at[len(flows)]),
            )
        )
        index += len(flows[-1].steps)
        keep_at += 2 * rows
        recv_at += size
        sum_at += rows
    feed_count = len(flows)
    ready = {axis: ready_sem.at[i] for i, axis in enumerate(where)}
    keep_at, recv_at = 0, 0
    for rows, order in shared_flows:
        order = (CORE,) + order + deep
        size = landing(rows, len(order))
        mine = shared.at[pl.ds(keep_at, rows)]
        lands = (
            staging.at[pl.ds(recv_at, rows // 2)],
            staging.at[pl.ds(recv_at + rows // 2, size - rows // 2)],
        )
        flows.append(
            Flow(
                where,
                order,
                order,
                rows,
                mine,
                mine,
                lands,
                shared_sum.at[pl.ds(keep_at, rows)],
                (send_sem, recv_sem, index),
                ready,
                (sums_out.at[pl.ds(sum_at + keep_at, rows)], out_sem.at[len(flows)]),
            )
        )
        index += len(flows[-1].steps)
        keep_at += rows
        recv_at += size

    script = Script(flows, set())
    made = [(D, i) for i in range(tiles)] + [(UP, i) for i in range(tiles)]
    made += [(WEIGHT, group - 1) if group else (CONTEXT, 0) for group in GROUPS]
    if moves:
        for point, numbers in moves.items():
            for number in numbers:
                script.write(point, number)
    else:
        for i, point in enumerate(made):
            script.write(point, len(flows) + i)
            if point[0] == UP and i + 1 == 2 * tiles:
                for k in range(feed_count):
                    script.write((SYNC, 0), k)
    script.finish((TAIL, 0))
    act_now = script.play

    def put(number, target, xs, start, block, cols):
        base, grain = places[number]
        size = block.shape[0]
        row = start
        while row < start + size:
            high, inner = row // grain, row % grain
            length = min(grain - inner, start + size - row)
            place = pl.ds(pl.multiple_of(base + high * 2 * grain + xs * grain + inner, 16), length)
            target[place, cols] = block[row - start : row - start + length]
            row += length

    def outer_grad(number, rows_t, base, tile_index):
        def both(g):
            xs = x + g - 2 * x * g
            for parity, target in ((0, acc), (1, staging)):
                cols = slice(tile_index * TILE, (tile_index + 1) * TILE)
                value = low(dot(rows_t[...], pool[page_rows(base, 2 * g + parity), cols]))
                for q in range(tiles):
                    lanes = slice(q * TILE, (q + 1) * TILE)
                    put(number, target, xs, 0, value[q * TILE : (q + 1) * TILE], lanes)

        loop(2, both)

    fgrad_t[...] = jnp.transpose(fgrad[...])
    for i in range(tiles):
        outer_grad(i, fgrad_t, act_at, i)
        act_now((D, i))
    empty = jnp.zeros((64, 256 - lwidth), BF16)

    def layout_grad(g):
        xs = x + g - 2 * x * g
        for parity, target in ((0, acc), (1, staging)):
            s = 2 * g + parity
            t = shard_at(s)
            active_grad = dot_nt(lfgrad[...], small[t, lwidth : 2 * lwidth, 0:lwidth])
            rounded = low(active_grad * lslope[s].astype(F32))
            total = row_sum(rounded.astype(F32))
            for k, (row, lane) in enumerate(((8, 0), (8, 256), (8, 512), (9, 0))):

                @pl.when(t == k)
                def _():
                    vec[row : row + 1, lane : lane + lwidth] = total

            lfeed[...] += dot_nt(rounded, small[t, 0:lwidth, 0:lwidth])
            up_block = low(dot(lh_t[...], rounded))
            down_block = low(dot(jnp.transpose(lact[s]), lfgrad[...]))
            for which, block in enumerate((up_block, down_block)):
                for q in range(lwidth // 64):
                    piece = jnp.concatenate([block[q * 64 : q * 64 + 64], empty], axis=1)
                    cols = slice(q * 256, q * 256 + 256)
                    put(2 * tiles - 1, target, xs, TILE + 64 * which, piece, cols)

    def units_grad(s):
        t = shard_at(s)

        def units(j):
            cols = tile(j)
            place = pl.ds(pl.multiple_of(4 * width + t * width + j * TILE, 16), TILE)
            active_grad = dot_nt(fgrad[...], pool[place, :])
            slope = pool[page_rows(slope_at, s), cols].astype(F32)
            rounded = low(active_grad * slope)
            pool[page_rows(slope_at, s), cols] = rounded
            vec[pl.ds(3 + t, 1), cols] = row_sum(rounded.astype(F32))

        loop(tiles, units)
        for k in range(4):

            @pl.when(s == k)
            def _():
                act_now((UNITS, k))

    loop(4, units_grad)

    for i in range(tiles):
        if i == 0:
            loop(2, layout_grad)
            act_now((LAY, 0))
        outer_grad(tiles + i, h_t, slope_at, i)
        act_now((UP, i))

    def hidden_back(s):
        t = shard_at(s)

        def back(j):
            cols = tile(j)
            place = pl.ds(pl.multiple_of(t * width + j * TILE, 16), TILE)
            feed[:, cols] += dot_nt(pool[page_rows(slope_at, s), :], pool[place, :])

        loop(tiles, back)
        for k in range(4):

            @pl.when(s == k)
            def _():
                act_now((BACK, k))

    loop(4, hidden_back)
    for copy in messages:
        copy.wait_send()
    for item in flows[:feed_count]:
        item.steps[0][1].wait_send()
    for axis, (_, device) in where.items():
        pl.semaphore_signal(
            ready_sem.at[list(where).index(axis)],
            inc=1,
            device_id=device,
            device_id_type=MESH,
        )
    act_now((SYNC, 0))
    wo_again, wq_again, wk_again, wv_again = (
        recv.at[pl.ds(i * width, width)] for i in range(4)
    )
    again = [
        load(3, wo_hbm, wo_again),
        load(0, wq_hbm, wq_again),
        load(1, wk_hbm, wk_again),
        load(2, wv_hbm, wv_again),
    ]
    mixed, lmixed = fgrad, lfgrad

    def norm_grad(r, sums, source, gain, grad, grad_low):
        unit, spread = normed(source[r, 0 : grad.shape[1]])
        outer = grad[r, :]
        value = normed_back(unit, spread, outer * gain)
        grad[r, :] = value
        rounded = low(value)
        grad_low[r, :] = rounded
        return (
            sums[0] + row_sum(rounded.astype(F32)),
            sums[1] + row_sum(outer * unit),
            sums[2] + row_sum(outer),
        )

    def norm_grads(i, sums):
        r = tile(i, ROWS)
        return (
            norm_grad(r, sums[0], asum, gains[0], feed, mixed),
            norm_grad(r, sums[1], lasum, gains[2], lfeed, lmixed),
        )

    found, lfound = lax.fori_loop(0, PAGE // ROWS, norm_grads, start)
    for i in range(3):
        vec[12 + i : 13 + i, :] = found[i]
        vec[15:16, i * 256 : i * 256 + lwidth] = lfound[i]
    act_now((NORM, 0))
    again[0].wait()
    k_t, lk_t, cgrad_t, lcgrad = v_t, lv_t, h_t, lctx
    masks[...] = jnp.zeros_like(masks)

    def turn(j):
        x_t[tile(j), :] = jnp.transpose(x_ref[:, tile(j)])

    def context_back(j):
        cols = tile(j)
        value = low(dot_nt(mixed[...], wo_again[cols, :]))
        cgrad[:, cols] = value
        cgrad_t[cols, :] = jnp.transpose(value)
        shared[0:width, cols] = low(dot(ctx_t[...], mixed[:, cols]))
        k_t[cols, :] = jnp.transpose(kn[:, cols])

    loop(tiles, context_back)
    value = jnp.concatenate([low(dot_nt(lmixed[...], lwo[...])), pad], axis=1)
    lcgrad[...] = value
    lcgrad_t[...] = jnp.transpose(value)
    lk_t[...] = jnp.transpose(lkn[...])
    loop(tiles, turn)
    act_now((CONTEXT, 0))

    lane = lax.broadcasted_iota(jnp.int32, (PAGE, 128), 1)
    ldv[...] = jnp.zeros_like(ldv)
    ldk[...] = jnp.zeros_like(ldk)
    ldq_t[...] = jnp.zeros_like(ldq_t)

    def attend_back(pair):
        text, block = tile(pair, 128), tile(pair // 4, 128)
        keys = jnp.concatenate([kn[:, text], lkn[:, block]], axis=1)
        values = jnp.concatenate([vn[:, text], lvn[:, block]], axis=1)
        grads = jnp.concatenate([cgrad[:, text], lcgrad[:, block]], axis=1)
        found = []
        for side in range(2):
            head = 2 * pair + side
            head_rows(masked, q_t, lq_t, pair, side)
            head_rows(masked_c, cgrad_t, lcgrad_t, pair, side)
            span = slice(side * 256, side * 256 + 256)
            weights = jnp.exp(dot(keys, masked[span, :]) - lse[pl.ds(head, 1), :])
            value_grad = dot(low(weights), grads)
            text_wave = dot(vn[:, text], masked_c[side * 256 : side * 256 + 128, :])
            text_part = row_sum(text_wave * weights)
            text_score = low(weights * (text_wave - text_part))
            both_wave = dot(values, masked_c[span, :])
            both_part = row_sum(both_wave * weights)
            both_score = low(weights * (both_wave - both_part))
            query_grad = low(dot(k_t[tile(head, 64), :], text_score) * 0.125)
            ldq_t[tile(head, 16), :] = low(dot(lk_t[tile(head, 16), :], both_score) * 0.25)
            key_grad = dot(text_score, qn[:, text])
            lkey_grad = dot(both_score, lqn[:, block])
            own = (lane // 16) == (head % 8)
            ldv[:, block] = jnp.where(own, value_grad[:, 128:256], ldv[:, block])
            ldk[:, block] = jnp.where(own, lkey_grad, ldk[:, block])
            found.append((value_grad[:, 0:128], key_grad, query_grad))
        first_half = lane < 64
        dv[:, text] = low(jnp.where(first_half, found[0][0], found[1][0]))
        dk[:, text] = low(jnp.where(first_half, found[0][1], found[1][1]))
        dq[:, text] = jnp.transpose(jnp.concatenate([found[0][2], found[1][2]], axis=0))
        for k in range(HEADS // 2):

            @pl.when(pair == k)
            def _():
                act_now((ATTEND, k))

        @pl.when(pair % 2 == 1)
        def _():
            weight_grad(pair // 2)

        for k in range(tiles - 1):

            @pl.when(pair == 2 * k + 1)
            def _():
                act_now((WEIGHT, k))

    def weight_grad(group):
        cols = tile(group)
        place = pl.ds(pl.multiple_of((1 + group) * width, 16), width)
        for i, source in enumerate((dq, dk, dv)):
            shared[place, i * TILE : (i + 1) * TILE] = low(dot(x_t[...], source[:, cols]))
        vec[10:11, cols] = row_sum(dq[:, cols].astype(F32))
        vec[11:12, cols] = row_sum(dv[:, cols].astype(F32))

    loop(HEADS // 2, attend_back)

    query = jnp.transpose(ldq_t[...])[:, 0:lwidth]
    key, value = low(ldk[:, 0:lwidth]), low(ldv[:, 0:lwidth])
    parts = [low(dot(lx_t[...], item)) for item in (query, key, value)]
    parts.append(low(dot(lctx_t[0:lwidth, :], lmixed[...])))
    base = 4 * width
    shared[base : base + lwidth, :] = jnp.concatenate(parts, axis=1)
    vec[9:10, 256 : 256 + lwidth] = row_sum(query.astype(F32))
    vec[9:10, 512 : 512 + lwidth] = row_sum(value.astype(F32))
    base += lwidth
    shared[base : base + 16, :] = low(vec[...])
    shared[base + 16 : shared_rows, :] = jnp.zeros((shared_rows - base - 16, width), BF16)
    act_now((WEIGHT, tiles - 1))
    for copy in again[1:]:
        copy.wait()

    def input_back(j):
        cols = tile(j)
        feed[:, cols] += (
            dot_nt(dq[...], wq_again[cols, :])
            + dot_nt(dk[...], wk_again[cols, :])
            + dot_nt(dv[...], wv_again[cols, :])
        )
        for k in range(tiles):

            @pl.when(j == k)
            def _():
                act_now((INPUT, k))

    loop(tiles, input_back)
    in_grad_copy = load(4, feed, in_grad_out)
    lin_grad[...] = jnp.transpose(
        lfeed[...] + dot_nt(query, lwq[...]) + dot_nt(key, lwk[...]) + dot_nt(value, lwv[...])
    )
    act_now((END, 0))
    act_now((TAIL, 0))
    for item in flows:
        item.drain()
    in_grad_copy.wait()


def finish_kernel(feed_rows, sums_hbm, *refs):
    passed, outs = refs[0:4], refs[4:38]
    sums, wide_sums, vec = refs[38:41]
    through = refs[41:45]
    load_sem, store_sem, in_sem, out_sem = refs[45:49]
    width, lwidth = wide_sums.shape[1], through[1].shape[0]
    starts = (feed_rows, 0, width, feed_rows + width, feed_rows + 2 * width)
    starts += (feed_rows + 3 * width, feed_rows + 4 * width)
    sizes = [width, width, width + 128] + [width] * 3 + [sums.shape[0] - starts[-1]]
    loads = []
    for i, (start, size) in enumerate(zip(starts, sizes)):
        part = pl.ds(start, size)
        copy = pltpu.make_async_copy(sums_hbm.at[part], sums.at[part], load_sem.at[i])
        copy.start()
        loads.append(copy)
    takes = [
        pltpu.make_async_copy(a, b, in_sem.at[i]) for i, (a, b) in enumerate(zip(passed, through))
    ]
    gives = [
        pltpu.make_async_copy(a, b, out_sem.at[i]) for i, (a, b) in enumerate(zip(through, outs))
    ]
    for copy in takes:
        copy.start()

    def widen(slot, start, cols=None, lanes=None):
        def block(i):
            source = pl.ds(start + pl.multiple_of(i * 128, 128), 128)
            target = pl.ds(pl.multiple_of(i * 128, 128), 128)
            if cols is None:
                wide_sums[slot, target, :] = sums[source, :].astype(F32)
            else:
                wide_sums[slot, target, lanes] = sums[source, cols].astype(F32)

        loop(width // 128, block)

    text, layout = outs[4:19], outs[19:34]
    stores = []

    def store(slot, out):
        copy = pltpu.make_async_copy(wide_sums.at[slot], out, store_sem.at[slot])
        copy.start()
        stores.append(copy)

    loads[0].wait()
    widen(0, starts[0])
    store(0, text[5])
    blocks = range(width // TILE)
    for slot, out in ((1, text[11]), (2, text[9])):
        loads[slot].wait()
        for i in blocks:
            for q in blocks:
                rows = pl.ds(starts[slot] + i * TILE, TILE)
                value = sums[rows, q * TILE : (q + 1) * TILE].astype(F32)
                place = (i, q) if slot == 1 else (q, i)
                value = jnp.transpose(value) if slot == 1 else value
                down, across = (pl.ds(k * TILE, TILE) for k in place)
                wide_sums[slot, down, across] = value
        store(slot, out)
    for copy, give in zip(takes, gives):
        copy.wait()
        give.start()
    for g in range(width // TILE):
        loads[3 + g].wait()
        for i in range(3):
            lanes = slice(g * TILE, (g + 1) * TILE)
            widen(3 + i, starts[3 + g], slice(i * TILE, (i + 1) * TILE), lanes)
    for i, out in enumerate((text[0], text[2], text[3])):
        store(3 + i, out)
    loads[6].wait()
    base = starts[6]
    for i, out in enumerate((layout[0], layout[2], layout[3], layout[5])):
        out[...] = sums[base : base + lwidth, i * lwidth : (i + 1) * lwidth].astype(F32)
    for i, out in enumerate((layout[9], layout[11])):
        for q in range(lwidth // 64):
            top = 2 * width + 64 * i
            rows = sums[top : top + 64, q * TILE : q * TILE + lwidth]
            out[q * 64 : q * 64 + 64, :] = rows.astype(F32)
    vec[...] = sums[base + lwidth : base + lwidth + 16, :].astype(F32)
    me = lax.axis_index("tensor")
    for row, out in ((10, 1), (11, 4), (12, 6), (13, 7), (14, 8), (2, 12), (0, 13), (1, 14)):
        text[out][...] = vec[row, :]
    text[10][...] = vec[pl.ds(3 + me, 1), :][0]

    def strip(row, part):
        return vec[row : row + 1, part * TILE : part * TILE + lwidth]

    places = ((9, 1, 1), (9, 2, 4), (15, 0, 6), (15, 1, 7), (15, 2, 8))
    for row, part, out in places + ((7, 2, 12), (7, 0, 13), (7, 1, 14)):
        layout[out][...] = strip(row, part)[0]
    rise = strip(8, 0)
    for k, (row, part) in enumerate(((8, 1), (8, 2), (9, 0))):
        rise = jnp.where(me == k + 1, strip(row, part), rise)
    layout[10][...] = rise[0]
    for copy in stores + gives:
        copy.wait()


MOVES = {
    (D, 0): (14,),
    (D, 1): (15,),
    (D, 2): (16,),
    (UNITS, 1): (0, 14),
    (UNITS, 2): (1, 15),
    (UNITS, 3): (2, 16),
    (UP, 0): (17,),
    (UP, 1): (18,),
    (UP, 2): (19,),
    (BACK, 1): (3, 17, 0, 14, 4, 1, 15),
    (BACK, 2): (2, 18, 5, 19),
    (NORM, 0): (0, 14),
    (CONTEXT, 0): (21, 20, 1, 15),
    (ATTEND, 0): (16, 3, 7, 0, 14, 6, 1, 4, 21),
    (ATTEND, 1): (18, 15),
    (WEIGHT, 0): (23, 22, 20, 2, 5, 16, 0, 14),
    (ATTEND, 2): (19, 9, 23, 8, 7, 1, 15, 4, 18, 6, 0),
    (ATTEND, 3): (22, 21, 2, 20, 16, 1),
    (WEIGHT, 1): (25, 24, 17, 14, 9, 4, 18),
    (ATTEND, 4): (23, 15, 5, 19, 7, 11, 10, 8, 25, 6, 2),
    (ATTEND, 5): (22, 16, 24, 3, 21, 0, 4, 9, 23),
    (WEIGHT, 2): (26, 27, 17, 20, 18, 5, 1, 19, 8, 10, 24, 11, 25, 7, 2, 9, 12, 26, 6, 13),
    (INPUT, 0): (3, 27, 4, 18, 10, 21),
    (INPUT, 1): (11, 25),
    (INPUT, 2): (23,),
    (END, 0): (24, 12, 26),
    (TAIL, 0): (5, 22, 4, 20, 7, 21, 11, 13, 27, 25, 10, 12, 8, 26, 9, 6, 23, 7, 21, 13, 27, 11, 25, 22, 12, 9, 23, 26, 7, 21, 13, 27, 11, 25, 8, 24, 20, 9, 23, 12, 26, 22, 11, 25, 17, 13, 6, 20, 10, 7, 21, 12, 24, 26, 8, 27, 9, 23, 22, 19, 7, 6, 20, 9, 11, 25, 10, 24, 12, 26, 16, 3, 17, 13, 8, 27, 11, 6, 20, 10, 22, 6, 5, 19, 3, 24, 12, 26, 13, 27, 17, 2, 12, 8, 22, 10, 24, 8, 10, 13, 27, 5, 3, 13),
}
FEED_ORDERS = ((0, ACROSS, 1), (ACROSS, 0, 1), (1, ACROSS, 0), (1, ACROSS, 0), (ACROSS, 0, 1), (0, ACROSS, 1))
SHARED_ORDERS = ((ACROSS, 0, 1), (ACROSS, 0, 1), (ACROSS, 0, 1), (0, ACROSS, 1), (1, 0, ACROSS), (ACROSS, 0, 1), (ACROSS, 0, 1), (ACROSS, 0, 1))
SHARED_ROWS = (256, 512, 256, 512, 256, 512, 512, 512)
GROUPS = (0, 0, 1, 1, 2, 2, 3, 3)

START = (3, 2, 39, 42, 18, 21, 22, 41, 1, 0, 19, 38, 20, 37)
GATHER = {
    (SETUP, 0): (39, 42),
    (PROJECT, 2): (3, 18),
    (HEAD, 0): (2, 37),
    (HEAD, 2): (21, 8),
    (HEAD, 3): (22, 41),
    (HEAD, 4): (6, 16),
    (HEAD, 5): (43, 1),
    (MIX, 0): (25, 14, 0, 27, 12),
    (FIRST, 0): (19, 33, 10),
    (FED, 0): (35, 9, 7, 29),
    (FED, 1): (4, 38, 5, 17),
    (FED, 2): (15, 11, 20),
    (FEED, 3): (40, 13),
    (FED, 3): (28, 31),
    (DONE, 0): (26, 23),
    (DONE, 1): (36,),
    (DOWN, 2): (24,),
    (DONE, 2): (34, 30),
    (DOWN, 3): (32,),
}


def on_device(dp, tensor, *args):
    (
        text_in,
        layout_in,
        token_mask,
        box_mask,
        cot_text,
        cot_layout,
    ) = args[:6]
    text, layout = args[6:21], args[21:36]
    width, lwidth = text_in.shape[1], layout_in.shape[1]
    dp_bits = dp.bit_length() - 1
    half = width // 2
    feed_flows = tuple(zip((TILE, TILE, TILE, TILE, TILE, TILE + 128), FEED_ORDERS))
    shared_flows = tuple(zip(SHARED_ROWS, SHARED_ORDERS))
    moves = MOVES if dp_bits == 3 else {}
    feed_rows = sum(rows for rows, _ in feed_flows)
    shared_rows = sum(rows for rows, _ in shared_flows)
    land = sum(landing(4 * rows, dp_bits + 2) for rows, _ in feed_flows)
    shared_land = sum(landing(rows, dp_bits + 2) for rows, _ in shared_flows)
    pool_rows = max(8 * width + 8 * PAGE, 2 * shared_rows + 4 * PAGE + width)
    count = (2 * dp_bits + 2) * len(feed_flows) + (2 * dp_bits + 4) * len(shared_flows)

    vmem = pl.BlockSpec(memory_space=pltpu.VMEM)
    hbm = pl.BlockSpec(memory_space=pl.ANY)
    page = PAGE

    def shape(*dims, dtype=BF16):
        return jax.ShapeDtypeStruct(dims, dtype)

    def row(vector):
        return vector.reshape(1, vector.shape[0])

    inputs = (text_in, layout_in.T, row(token_mask), row(box_mask), cot_text, cot_layout.T)
    inputs += text + layout
    specs = [vmem] * len(inputs)
    for i in (6, 8, 9, 11, 15, 17):
        specs[i] = hbm
    outs = (
        shape(page, width),
        shape(lwidth, page),
        shape(page, width, dtype=F32),
        shape(lwidth, page, dtype=F32),
        shape(feed_rows + shared_rows, width),
    )
    scratch = [
        pltpu.VMEM((pool_rows, width), BF16),
        pltpu.VMEM((2 * feed_rows, width), BF16),
        pltpu.VMEM((max(2 * feed_rows, shared_land), width), BF16),
        pltpu.VMEM((land, width), BF16),
        pltpu.VMEM((feed_rows, width), BF16),
        pltpu.VMEM((4, 2 * lwidth, 256), BF16),
        pltpu.VMEM((4, 8, 256), F32),
        pltpu.VMEM((page, width), BF16),
        pltpu.VMEM((page, width), BF16),
        pltpu.VMEM((page, width), BF16),
        pltpu.VMEM((width, page), BF16),
        pltpu.VMEM((width, page), BF16),
        pltpu.VMEM((page, 256), BF16),
        pltpu.VMEM((page, 256), BF16),
        pltpu.VMEM((page, 256), BF16),
        pltpu.VMEM((256, page), BF16),
        pltpu.VMEM((256, page), BF16),
        pltpu.VMEM((16, page), F32),
        pltpu.VMEM((1024, page), BF16),
        pltpu.VMEM((width, page), BF16),
        pltpu.VMEM((256, page), BF16),
        pltpu.VMEM((page, 256), BF16),
        pltpu.VMEM((page, width), F32),
        pltpu.VMEM((page, width), BF16),
        pltpu.VMEM((page, lwidth), BF16),
        pltpu.VMEM((width, page), BF16),
        pltpu.VMEM((lwidth, page), BF16),
        pltpu.VMEM((page, width), F32),
        pltpu.VMEM((page, lwidth), F32),
        pltpu.VMEM((4, page, lwidth), BF16),
        pltpu.VMEM((4, page, lwidth), BF16),
        pltpu.VMEM((page, 16), F32),
        pltpu.VMEM((8, width), F32),
        pltpu.VMEM((page, lwidth), BF16),
        pltpu.VMEM((page, lwidth), BF16),
        pltpu.VMEM((256, page), BF16),
        pltpu.VMEM((256, page), BF16),
        pltpu.VMEM((page, 256), F32),
        pltpu.VMEM((page, 256), F32),
        pltpu.VMEM((16, width), F32),
        pltpu.SemaphoreType.DMA((6,)),
        pltpu.SemaphoreType.DMA((48,)),
        pltpu.SemaphoreType.DMA((48,)),
        pltpu.SemaphoreType.DMA((count,)),
        pltpu.SemaphoreType.DMA((count,)),
        pltpu.SemaphoreType.DMA((len(feed_flows) + len(shared_flows),)),
        pltpu.SemaphoreType.REGULAR((dp_bits + 2,)),
    ]
    text_out, layout_out, in_grad, lin_grad, sums = pl.pallas_call(
        functools.partial(layer_kernel, (dp_bits, feed_flows, shared_flows, moves)),
        out_shape=outs,
        in_specs=specs,
        out_specs=[vmem, vmem, hbm, vmem, hbm],
        scratch_shapes=scratch,
        compiler_params=pltpu.CompilerParams(
            collective_id=0, has_side_effects=True, vmem_limit_bytes=67043328
        ),
        name="layer",
    )(*inputs)

    big, small_square = shape(width, width, dtype=F32), shape(lwidth, lwidth, dtype=F32)

    def stream(square, size):
        line = shape(size, dtype=F32)
        order = (square, line, square, square, line, square, line, line, line)
        return order + (square, line, square, line, line, line)

    outs = (
        shape(page, width),
        shape(lwidth, page),
        shape(page, width, dtype=F32),
        shape(lwidth, page, dtype=F32),
    )
    outs += stream(big, width) + stream(small_square, lwidth)
    specs = [hbm if i < 4 or out.shape == (width, width) else vmem for i, out in enumerate(outs)]
    done = pl.pallas_call(
        functools.partial(finish_kernel, feed_rows),
        out_shape=outs,
        in_specs=[hbm] * 5,
        out_specs=specs,
        scratch_shapes=[
            pltpu.VMEM((feed_rows + shared_rows, width), BF16),
            pltpu.VMEM((6, width, width), F32),
            pltpu.VMEM((16, width), F32),
            pltpu.VMEM((page, width), BF16),
            pltpu.VMEM((lwidth, page), BF16),
            pltpu.VMEM((page, width), F32),
            pltpu.VMEM((lwidth, page), F32),
            pltpu.SemaphoreType.DMA((7,)),
            pltpu.SemaphoreType.DMA((6,)),
            pltpu.SemaphoreType.DMA((4,)),
            pltpu.SemaphoreType.DMA((4,)),
        ],
        compiler_params=pltpu.CompilerParams(vmem_limit_bytes=60000000),
        name="finish",
    )(sums, text_out, layout_out, in_grad, lin_grad)
    return (done[0], done[1].T, done[2], done[3].T) + tuple(done[4:])


def solution(mesh):
    rows = P(("dp", "tensor"), None)
    line = P(("dp", "tensor"))
    weights = (P(),) * 9 + (P(None, "tensor"), P("tensor"), P("tensor", None)) + (P(),) * 3
    in_specs = (rows, rows, line, line, rows, rows) + weights + weights
    out_specs = (rows,) * 4 + weights + weights
    return jax.shard_map(
        functools.partial(on_device, mesh.shape["dp"], mesh.shape["tensor"]),
        mesh=mesh,
        in_specs=in_specs,
        out_specs=out_specs,
        check_vma=False,
    )
```

```python
import functools

import jax
import jax.numpy as jnp
from jax import lax
from jax.experimental import pallas as pl
from jax.experimental.pallas import tpu as pltpu
from jax.sharding import PartitionSpec as P

HEADS = 12
PAGE = 512
NORM_EPS = 1e-05
MESH = pl.DeviceIdType.MESH
F32 = jnp.float32
BF16 = jnp.bfloat16
TILE = 256
ROWS = 128
CORE, ACROSS = 100, 101
SETUP, PROJECT, LAYOUT, HEAD, MIX, FIRST, FEED, FED, DOWN, DONE = range(10)
D, UNITS, UP, BACK, NORM, CONTEXT, ATTEND, WEIGHT, INPUT, END, TAIL, SYNC, LAY = range(10, 23)


def low(values):
    return values.astype(BF16)


def dot(first, second):
    return jnp.dot(first, second, preferred_element_type=F32)


def dot_nt(first, second):
    return lax.dot_general(first, second, (((1,), (1,)), ((), ())), preferred_element_type=F32)


def tile(index, size=TILE):
    return pl.ds(pl.multiple_of(index * size, size), size)


def loop(count, body):
    def step(index, carry):
        body(index)
        return carry

    lax.fori_loop(0, count, step, 0, unroll=count if count < 4 else 1)


def flip(bit):
    return 1 - 2 * bit


def wide(vector_ref):
    return vector_ref[...].astype(F32)[None, :]


def lane_mean(values):
    return jnp.mean(values, axis=-1, keepdims=True)


def row_sum(values):
    return jnp.sum(values, axis=0, keepdims=True)


def normed(values):
    centered = values - lane_mean(values)
    scale = lax.rsqrt(lane_mean(centered * centered) + NORM_EPS)
    return centered * scale, scale


def normed_back(unit, scale, grad):
    return (grad - lane_mean(grad) - unit * lane_mean(grad * unit)) * scale


def landing(rows, stages):
    total = 0
    for stage in range(stages):
        rows = rows // 2 if rows % 32 == 0 and stage + 1 < stages else rows
        total += rows
    return total


def copy_to(source, target, send, recv, device):
    return pltpu.make_async_remote_copy(
        src_ref=source,
        dst_ref=target,
        send_sem=send,
        recv_sem=recv,
        device_id=device,
        device_id_type=MESH,
    )


def greet(devices):
    barrier = pltpu.get_barrier_semaphore()
    for device in devices:
        pl.semaphore_signal(barrier, inc=1, device_id=device, device_id_type=MESH)
    pl.semaphore_wait(barrier, len(devices))


def mask_column(text_mask, layout_mask, column_ref):
    parts = []
    for mask_ref in (text_mask, layout_mask):
        scale = 0.5 + 1.5 * mask_ref[...].astype(F32)
        parts.append(jnp.broadcast_to(scale, (8, PAGE)))
    column_ref[...] = jnp.transpose(jnp.concatenate(parts, axis=0))


def head_rows(target, text_rows, layout_rows, pair, side):
    head = 2 * pair + side
    top = side * 256
    target[top + 128 : top + 256, :] = jnp.zeros((128, PAGE), BF16)
    target[top + side * 64 : top + side * 64 + 64, :] = text_rows[tile(head, 64), :]
    spot = pl.ds(pl.multiple_of(top + 128 + (head % 8) * 16, 16), 16)
    target[spot, :] = layout_rows[tile(head, 16), :]


class Flow:
    def __init__(self, where, axes, spread, rows, give, keep, lands, whole, sems, ready, result):
        self.steps, self.ready = [], ready
        self.result = pltpu.make_async_copy(whole, *result)
        send_sem, recv_sem, index = sems
        offset, size, place = 0, rows, 0
        halved = []
        for stage, axis in enumerate(axes):
            bit, device = where[axis]
            recv = lands[min(stage, 1)]
            if stage == 1:
                place = 0
            if size % 32 == 0 and stage + 1 < len(axes):
                half = size // 2
                kept, given = offset + bit * half, offset + (1 - bit) * half
                halved.append(axis)
            else:
                half, kept, given = size, offset, offset
            first = stage == 0 and give is not keep
            source = give.at[pl.ds(0, half)] if first else self.span(keep, given, half)
            kept = 0 if first else kept
            copy = copy_to(
                source,
                recv.at[pl.ds(place, half)],
                send_sem.at[index],
                recv_sem.at[index],
                device,
            )
            last = stage + 1 == len(axes)
            target, start = keep, kept
            if last:
                target, start = whole, 0
                step, gathers = whole.shape[0], []
                for other in spread:
                    if other in halved:
                        step //= 2
                        start = start + where[other][0] * step
                        gathers.insert(0, (other, step))
            swap = half == size and not last
            self.steps.append((axis, copy, (keep, kept, recv, place, target, start, half, swap)))
            offset, size = kept, half
            place += half
            index += 1
        spot = start
        for axis, step in gathers:
            bit, device = where[axis]
            span = self.span(whole, spot, step)
            copy = copy_to(span, span, send_sem.at[index], recv_sem.at[index], device)
            self.steps.append((axis, copy, None))
            spot = spot - bit * step
            index += 1

    def span(self, ref, offset, size):
        return ref.at[pl.ds(pl.multiple_of(offset, 16), size)]

    def launch(self, step, waits):
        axis, copy, _ = self.steps[step]
        if waits:
            pl.semaphore_wait(self.ready[axis], 1)
        copy.start()

    def absorb(self, step):
        _, copy, rest = self.steps[step]
        copy.wait_recv()
        if rest is not None:
            keep, kept, recv, place, target, start, half, swap = rest
            if swap:
                copy.wait_send()
            block = max(b for b in range(16, 129, 16) if half % b == 0)

            def add(i):
                mine = pl.ds(pl.multiple_of(kept + i * block, 16), block)
                theirs = pl.ds(pl.multiple_of(place + i * block, 16), block)
                result = pl.ds(pl.multiple_of(start + i * block, 16), block)
                target[result, :] = keep[mine, :] + recv[theirs, :]

            loop(half // block, add)
        if step + 1 == len(self.steps):
            self.result.start()

    def drain(self):
        self.result.wait()
        for _, copy, rest in self.steps[1 if self.ready is None else 0 :]:
            if rest is None or not rest[-1]:
                copy.wait_send()


class Script:
    def __init__(self, flows, greeted):
        self.flows, self.greeted = flows, greeted
        self.started, self.taken = [0] * len(flows), [0] * len(flows)
        self.points = {}

    def write(self, point, number):
        kind, flow = divmod(number, len(self.flows))
        done = self.started if kind else self.taken
        step = done[flow]
        done[flow] += 1
        waits = False
        if kind and self.flows[flow].ready is not None:
            axis = self.flows[flow].steps[step][0]
            waits = axis not in self.greeted
            self.greeted.add(axis)
        self.points.setdefault(point, []).append((kind, flow, step, waits))

    def play(self, point):
        for kind, flow, step, waits in self.points.get(point, ()):
            if kind:
                self.flows[flow].launch(step, waits)
            else:
                self.flows[flow].absorb(step)

    def finish(self, point):
        flows, going = self.flows, True
        while going:
            going = False
            for i, flow in enumerate(flows):
                if self.started[i] > self.taken[i]:
                    self.write(point, i)
                    going = True
                if self.started[i] == self.taken[i] and self.taken[i] < len(flow.steps):
                    self.write(point, len(flows) + i)
                    going = True


def layer_kernel(plan, *refs):
    (
        x_ref,
        lx_t,
        token_mask,
        box_mask,
        cot_ref,
        lcot_ref,
        wq_hbm,
        bq,
        wk_hbm,
        wv_hbm,
        bv,
        wo_hbm,
        bo,
        attend_gain,
        attend_shift,
        up_hbm,
        up_bias,
        down_hbm,
        down_bias,
        feed_gain,
        feed_shift,
        lwq,
        lbq,
        lwk,
        lwv,
        lbv,
        lwo,
        lbo,
        lattend_gain,
        lattend_shift,
        lup,
        lup_bias,
        ldown,
        ldown_bias,
        lfeed_gain,
        lfeed_shift,
        out_ref,
        lout_ref,
        in_grad_out,
        lin_grad,
        sums_out,
        pool,
        acc,
        staging,
        recv,
        sums,
        small,
        small_bias,
        qn,
        kn,
        vn,
        q_t,
        v_t,
        lqn,
        lkn,
        lvn,
        lq_t,
        lv_t,
        lse,
        masks,
        ctx_t,
        lctx_t,
        lctx,
        asum,
        hlow,
        lhlow,
        h_t,
        lh_t,
        feed,
        lfeed,
        lact,
        lslope,
        column,
        rises,
        lx,
        lcot,
        lcgrad_t,
        ldq_t,
        ldk,
        ldv,
        vec,
        local_sem,
        gather_send,
        gather_recv,
        send_sem,
        recv_sem,
        out_sem,
        ready_sem,
    ) = refs
    dp_bits, feed_flows, shared_flows, moves = plan
    fgrad, lfgrad, lout, lasum = hlow, lhlow, lx, ldk
    masked, masked_c = masks.at[pl.ds(0, 512)], masks.at[pl.ds(512, 512)]
    fgrad_t = masks.at[pl.ds(0, x_ref.shape[1])]
    d, me = lax.axis_index("dp"), lax.axis_index("tensor")
    c, x = me % 2, me // 2
    width, lwidth = x_ref.shape[1], lx_t.shape[0]
    tiles = width // TILE
    where = {CORE: (c, (d, me + flip(c))), ACROSS: (x, (d, me + 2 * flip(x)))}
    for k in range(dp_bits):
        bit = (d // 2**k) % 2
        where[k] = (bit, (d + 2**k * flip(bit), me))
    core, across = where[CORE][1], where[ACROSS][1]
    y, beside = where[0]
    z, ahead = where[1]
    other = me + 2 * flip(x)

    def part(start, size):
        return pool.at[pl.ds(start, size)]

    wu, wd = part(0, 4 * width), part(4 * width, 4 * width)
    act_at, slope_at = 8 * width, 8 * width + 4 * PAGE
    wq, wk = part(act_at, width), part(act_at + width, width)
    wv, wo = part(act_at + 2 * width, width), part(act_at + 3 * width, width)
    ctx = part(act_at + 4 * width, PAGE)
    shared_rows = sum(rows for rows, _ in shared_flows)
    shared, shared_sum = part(0, shared_rows), part(shared_rows, shared_rows)
    spot = 2 * shared_rows
    dq, dk, dv = part(spot, PAGE), part(spot + PAGE, PAGE), part(spot + 2 * PAGE, PAGE)
    cgrad = part(spot + 3 * PAGE, PAGE)
    x_t = pool.at[pl.ds(spot + 4 * PAGE, width), pl.ds(0, PAGE)]

    def shard_rows(base, t, start=0, size=width):
        return pl.ds(pl.multiple_of(base + t * width + start, 16), size)

    small[me, 0:lwidth, 0:lwidth] = lup[...]
    small[me, lwidth : 2 * lwidth, 0:lwidth] = ldown[...]
    for j in range(tiles):
        small_bias[me, j : j + 1, :] = wide(up_bias)[:, j * TILE : (j + 1) * TILE]
    small_bias[me, 3:4, 0:lwidth] = wide(lup_bias)

    def load(index, source, target):
        copy = pltpu.make_async_copy(source, target, local_sem.at[index])
        copy.start()
        return copy

    loads = [load(i, s, t) for i, (s, t) in enumerate(((wq_hbm, wq), (wk_hbm, wk), (wv_hbm, wv)))]
    load_wo = load(3, wo_hbm, wo)
    keep_up = load(4, up_hbm, pool.at[shard_rows(0, me)])
    keep_down = load(5, down_hbm, pool.at[shard_rows(4 * width, me)])
    greet([device for _, device in where.values()])

    messages, needs = [], []

    def message(source, target, device, *after):
        index = len(messages)
        copy = copy_to(source, target, gather_send.at[index], gather_recv.at[index], device)
        messages.append(copy)
        needs.append(set(after))

    for base, hbm in ((0, up_hbm), (4 * width, down_hbm)):
        grain = width // 12
        zero = len(messages)

        def relay(start, size, device, *after):
            place = pool.at[shard_rows(base, other, start * grain, size * grain)]
            message(place, place, device, *(zero + item for item in after))

        own = (y, 2 + z, 4 + 2 * z + y, 8 + 2 * y + z)
        for start in own:
            source = hbm.at[pl.ds(pl.multiple_of(start * grain, 16), grain)]
            message(source, pool.at[shard_rows(base, me, start * grain, grain)], across)
        relay(own[0], 1, beside, 0)
        relay(own[1], 1, ahead, 1)
        relay(own[2], 1, beside, 2)
        relay(4 + 2 * z, 2, ahead, 2, 6)
        relay(own[3], 1, ahead, 3)
        relay(8 + 2 * y, 2, beside, 3, 8)
        relay(own[0], 1, core, 0)
        relay(1 - y, 1, core, 4)
        relay(own[1], 1, core, 1)
        relay(3 - z, 1, core, 5)
        relay(4 + 2 * z, 2, core, 2, 6)
        relay(6 - 2 * z, 2, core, 7)
        relay(8 + 2 * y, 2, core, 3, 8)
        relay(10 - 2 * y, 2, core, 9)
        message(hbm, pool.at[shard_rows(base, me)], core)
    for ref in (small, small_bias):
        message(ref.at[me], ref.at[me], across)
        message(ref.at[me], ref.at[me], core)
        message(ref.at[other], ref.at[other], core, len(messages) - 2)
    begun, got = set(START), set()
    for index in START:
        messages[index].start()

    def take(stage, k=0):
        for index in GATHER.get((stage, k), ()):
            messages[index].wait_recv()
            got.add(index)
            for later, after in enumerate(needs):
                if later not in begun and after <= got:
                    messages[later].start()
                    begun.add(later)

    def take_at(index, stage):
        for k in range(8):
            if (stage, k) in GATHER:

                @pl.when(index == k)
                def _():
                    take(stage, k)

    lx[...] = jnp.transpose(lx_t[...])
    lcot[...] = jnp.transpose(lcot_ref[...])
    mask_column(token_mask, box_mask, column)
    masks[...] = jnp.zeros_like(masks)
    vec[...] = jnp.zeros_like(vec)
    rises[0:1, :] = wide(bq)
    rises[1:2, :] = wide(bv)
    rises[2:3, :] = wide(bo)
    for copy in loads:
        copy.wait()
    take(SETUP)

    def project(j):
        cols = tile(j)
        rows = x_ref[...]
        queries = low(dot(rows, wq[:, cols]) + rises[0:1, cols]) * 0.125
        qn[:, cols] = queries
        q_t[cols, :] = jnp.transpose(queries)
        kn[:, cols] = low(dot(rows, wk[:, cols]))
        values = low(dot(rows, wv[:, cols]) + rises[1:2, cols])
        vn[:, cols] = values
        v_t[cols, :] = jnp.transpose(values)
        take_at(j, PROJECT)

    loop(tiles, project)
    pad = jnp.zeros((PAGE, 256 - lwidth), BF16)
    rows = lx[...]
    queries = low(dot(rows, lwq[...]) + wide(lbq)) * 0.25
    queries = jnp.concatenate([queries, pad], axis=1)
    lqn[...] = queries
    lq_t[...] = jnp.transpose(queries)
    lkn[...] = jnp.concatenate([low(dot(rows, lwk[...])), pad], axis=1)
    values = low(dot(rows, lwv[...]) + wide(lbv))
    values = jnp.concatenate([values, pad], axis=1)
    lvn[...] = values
    lv_t[...] = jnp.transpose(values)
    lctx_t[...] = jnp.zeros_like(lctx_t)
    take(LAYOUT)

    def attend(pair):
        keys = jnp.concatenate([kn[:, tile(pair, 128)], lkn[:, tile(pair // 4, 128)]], axis=1)
        for side in range(2):
            head = 2 * pair + side
            head_rows(masked, q_t, lq_t, pair, side)
            joint = dot(keys, masked[side * 256 : side * 256 + 256, :])
            highest = jnp.max(joint, axis=0, keepdims=True)
            exponent = jnp.exp(joint - highest)
            totals = row_sum(exponent)
            weights = low(exponent * (1.0 / totals))
            lse[pl.ds(head, 1), :] = highest + jnp.log(totals)
            values = jnp.concatenate([v_t[tile(head, 64), :], lv_t[tile(head, 16), :]], axis=0)
            context = low(dot(values, weights))
            ctx_t[tile(head, 64), :] = context[0:64]
            lctx_t[tile(head, 16), :] = context[64:80]

        take_at(pair, HEAD)

    loop(HEADS // 2, attend)

    def untranspose(j):
        ctx[:, tile(j)] = jnp.transpose(ctx_t[tile(j), :])

    loop(tiles, untranspose)
    lctx[...] = jnp.transpose(lctx_t[...])
    load_wo.wait()

    def mix(j):
        cols = tile(j)
        asum[:, cols] = x_ref[:, cols].astype(F32) + dot(ctx[...], wo[:, cols]) + rises[2:3, cols]

    loop(tiles, mix)
    lasum[:, 0:lwidth] = lx[...].astype(F32) + dot(lctx[:, 0:lwidth], lwo[...]) + wide(lbo)

    def first_norm(r, source, gain, shift, hidden, hidden_low):
        unit, _ = normed(source[r, 0 : hidden.shape[1]])
        value = unit * gain + shift
        hidden[r, :] = value
        hidden_low[r, :] = low(value)

    gains = [wide(item) for item in (attend_gain, attend_shift, lattend_gain, lattend_shift)]

    def first_norms(i):
        r = tile(i, ROWS)
        first_norm(r, asum, gains[0], gains[1], feed, hlow)
        first_norm(r, lasum, gains[2], gains[3], lfeed, lhlow)

    take(MIX)
    loop(PAGE // ROWS, first_norms)
    h_t[...] = jnp.transpose(hlow[...])
    lh_t[...] = jnp.transpose(lhlow[...])
    take(FIRST)

    def shard_at(s):
        return (x + s // 2 - 2 * x * (s // 2)) * 2 + c + s % 2 - 2 * c * (s % 2)

    def page_rows(base, s):
        return pl.ds(pl.multiple_of(base + s * PAGE, PAGE), PAGE)

    def gelu(u):
        square = u * u
        inner = 0.7978845608028654 * (u + 0.044715 * (square * u))
        wave = jnp.tanh(inner)
        rise = 0.5 * (1.0 + wave)
        bend = 0.5 * u * (1.0 - wave * wave)
        grow = 0.7978845608028654 * (1.0 + 0.134145 * square)
        return u * rise, rise + bend * grow

    keep_up.wait()

    def feed_up(s):
        t = shard_at(s)

        take_at(s, FEED)

        def up(j):
            cols = tile(j)
            weights = pool[shard_rows(0, t), cols]
            preact = dot(hlow[...], weights) + small_bias[t, pl.ds(j, 1), :]
            value, gradient = gelu(preact)
            pool[page_rows(act_at, s), cols] = low(value)
            pool[page_rows(slope_at, s), cols] = low(gradient)

        loop(tiles, up)
        preact = dot(lhlow[...], small[t, 0:lwidth, 0:lwidth]) + small_bias[t, 3:4, 0:lwidth]
        value, gradient = gelu(preact)
        lact[s] = low(value)
        lslope[s] = low(gradient)
        take_at(s, FED)

    loop(4, feed_up)
    keep_down.wait()

    def feed_down(s):
        t = shard_at(s)

        take_at(s, DOWN)

        def down(j):
            cols = tile(j)
            active = pool[page_rows(act_at, s), :]
            feed[:, cols] += dot(active, pool[shard_rows(4 * width, t), cols])

        loop(tiles, down)
        lfeed[...] += dot(lact[s], small[t, lwidth : 2 * lwidth, 0:lwidth])
        take_at(s, DONE)

    loop(4, feed_down)

    def second_norm(r, sums, fed, bias, gain, shift, cot, scale, out, grad_low):
        unit, spread = normed(fed[r, :] + bias)
        out[r, :] = low(unit * gain + shift)
        outer = cot[r, :].astype(F32) * column[r, scale : scale + 1]
        value = normed_back(unit, spread, outer * gain)
        fed[r, :] = value
        rounded = low(value)
        grad_low[r, :] = rounded
        return (
            sums[0] + row_sum(outer * unit),
            sums[1] + row_sum(outer),
            sums[2] + row_sum(rounded.astype(F32)),
        )

    tops = [wide(item) for item in (down_bias, feed_gain, feed_shift)]
    ltops = [wide(item) for item in (ldown_bias, lfeed_gain, lfeed_shift)]

    def second_norms(i, sums):
        r = tile(i, ROWS)
        return (
            second_norm(r, sums[0], feed, *tops, cot_ref, 0, out_ref, fgrad),
            second_norm(r, sums[1], lfeed, *ltops, lcot, 8, lout, lfgrad),
        )

    none, lnone = jnp.zeros((1, width), F32), jnp.zeros((1, lwidth), F32)
    start = ((none, none, none), (lnone, lnone, lnone))
    found, lfound = lax.fori_loop(0, PAGE // ROWS, second_norms, start)
    lout_ref[...] = jnp.transpose(lout[...])
    for i in range(3):
        vec[i : i + 1, :] = found[i]
        vec[7:8, i * 256 : i * 256 + lwidth] = lfound[i]

    deep = tuple(range(2, dp_bits))
    flows = []
    index, keep_at, recv_at, sum_at = 0, 0, 2 * sums.shape[0], 0
    places = []
    for rows, order in feed_flows:
        order = order + tuple(axis for axis in deep if axis not in order)
        depth = order.index(ACROSS)
        places.append((keep_at, rows >> depth))
        size = landing(4 * rows, len(order) + 1) - 2 * rows
        lands = recv.at[pl.ds(keep_at, 2 * rows)], recv.at[pl.ds(recv_at, size)]
        flows.append(
            Flow(
                where,
                (CORE,) + order,
                [axis for axis in order if axis != ACROSS],
                4 * rows,
                staging.at[pl.ds(keep_at, 2 * rows)],
                acc.at[pl.ds(keep_at, 2 * rows)],
                lands,
                sums.at[pl.ds(sum_at, rows)],
                (send_sem, recv_sem, index),
                None,
                (sums_out.at[pl.ds(sum_at, rows)], out_sem.at[len(flows)]),
            )
        )
        index += len(flows[-1].steps)
        keep_at += 2 * rows
        recv_at += size
        sum_at += rows
    feed_count = len(flows)
    ready = {axis: ready_sem.at[i] for i, axis in enumerate(where)}
    keep_at, recv_at = 0, 0
    for rows, order in shared_flows:
        order = (CORE,) + order + deep
        size = landing(rows, len(order))
        mine = shared.at[pl.ds(keep_at, rows)]
        lands = (
            staging.at[pl.ds(recv_at, rows // 2)],
            staging.at[pl.ds(recv_at + rows // 2, size - rows // 2)],
        )
        flows.append(
            Flow(
                where,
                order,
                order,
                rows,
                mine,
                mine,
                lands,
                shared_sum.at[pl.ds(keep_at, rows)],
                (send_sem, recv_sem, index),
                ready,
                (sums_out.at[pl.ds(sum_at + keep_at, rows)], out_sem.at[len(flows)]),
            )
        )
        index += len(flows[-1].steps)
        keep_at += rows
        recv_at += size

    script = Script(flows, set())
    made = [(D, i) for i in range(tiles)] + [(UP, i) for i in range(tiles)]
    made += [(WEIGHT, group - 1) if group else (CONTEXT, 0) for group in GROUPS]
    if moves:
        for point, numbers in moves.items():
            for number in numbers:
                script.write(point, number)
    else:
        for i, point in enumerate(made):
            script.write(point, len(flows) + i)
            if point[0] == UP and i + 1 == 2 * tiles:
                for k in range(feed_count):
                    script.write((SYNC, 0), k)
    script.finish((TAIL, 0))
    act_now = script.play

    def put(number, target, xs, start, block, cols):
        base, grain = places[number]
        size = block.shape[0]
        row = start
        while row < start + size:
            high, inner = row // grain, row % grain
            length = min(grain - inner, start + size - row)
            place = pl.ds(pl.multiple_of(base + high * 2 * grain + xs * grain + inner, 16), length)
            target[place, cols] = block[row - start : row - start + length]
            row += length

    def outer_grad(number, rows_t, base, tile_index):
        def both(g):
            xs = x + g - 2 * x * g
            for parity, target in ((0, acc), (1, staging)):
                cols = slice(tile_index * TILE, (tile_index + 1) * TILE)
                value = low(dot(rows_t[...], pool[page_rows(base, 2 * g + parity), cols]))
                for q in range(tiles):
                    lanes = slice(q * TILE, (q + 1) * TILE)
                    put(number, target, xs, 0, value[q * TILE : (q + 1) * TILE], lanes)

        loop(2, both)

    fgrad_t[...] = jnp.transpose(fgrad[...])
    for i in range(tiles):
        outer_grad(i, fgrad_t, act_at, i)
        act_now((D, i))
    empty = jnp.zeros((64, 256 - lwidth), BF16)

    def layout_grad(g):
        xs = x + g - 2 * x * g
        for parity, target in ((0, acc), (1, staging)):
            s = 2 * g + parity
            t = shard_at(s)
            active_grad = dot_nt(lfgrad[...], small[t, lwidth : 2 * lwidth, 0:lwidth])
            rounded = low(active_grad * lslope[s].astype(F32))
            total = row_sum(rounded.astype(F32))
            for k, (row, lane) in enumerate(((8, 0), (8, 256), (8, 512), (9, 0))):

                @pl.when(t == k)
                def _():
                    vec[row : row + 1, lane : lane + lwidth] = total

            lfeed[...] += dot_nt(rounded, small[t, 0:lwidth, 0:lwidth])
            up_block = low(dot(lh_t[...], rounded))
            down_block = low(dot(jnp.transpose(lact[s]), lfgrad[...]))
            for which, block in enumerate((up_block, down_block)):
                for q in range(lwidth // 64):
                    piece = jnp.concatenate([block[q * 64 : q * 64 + 64], empty], axis=1)
                    cols = slice(q * 256, q * 256 + 256)
                    put(2 * tiles - 1, target, xs, TILE + 64 * which, piece, cols)

    def units_grad(s):
        t = shard_at(s)

        def units(j):
            cols = tile(j)
            place = pl.ds(pl.multiple_of(4 * width + t * width + j * TILE, 16), TILE)
            active_grad = dot_nt(fgrad[...], pool[place, :])
            slope = pool[page_rows(slope_at, s), cols].astype(F32)
            rounded = low(active_grad * slope)
            pool[page_rows(slope_at, s), cols] = rounded
            vec[pl.ds(3 + t, 1), cols] = row_sum(rounded.astype(F32))

        loop(tiles, units)
        for k in range(4):

            @pl.when(s == k)
            def _():
                act_now((UNITS, k))

    loop(4, units_grad)

    for i in range(tiles):
        if i == 0:
            loop(2, layout_grad)
            act_now((LAY, 0))
        outer_grad(tiles + i, h_t, slope_at, i)
        act_now((UP, i))

    def hidden_back(s):
        t = shard_at(s)

        def back(j):
            cols = tile(j)
            place = pl.ds(pl.multiple_of(t * width + j * TILE, 16), TILE)
            feed[:, cols] += dot_nt(pool[page_rows(slope_at, s), :], pool[place, :])

        loop(tiles, back)
        for k in range(4):

            @pl.when(s == k)
            def _():
                act_now((BACK, k))

    loop(4, hidden_back)
    for copy in messages:
        copy.wait_send()
    for item in flows[:feed_count]:
        item.steps[0][1].wait_send()
    for axis, (_, device) in where.items():
        pl.semaphore_signal(
            ready_sem.at[list(where).index(axis)],
            inc=1,
            device_id=device,
            device_id_type=MESH,
        )
    act_now((SYNC, 0))
    wo_again, wq_again, wk_again, wv_again = (
        recv.at[pl.ds(i * width, width)] for i in range(4)
    )
    again = [
        load(3, wo_hbm, wo_again),
        load(0, wq_hbm, wq_again),
        load(1, wk_hbm, wk_again),
        load(2, wv_hbm, wv_again),
    ]
    mixed, lmixed = fgrad, lfgrad

    def norm_grad(r, sums, source, gain, grad, grad_low):
        unit, spread = normed(source[r, 0 : grad.shape[1]])
        outer = grad[r, :]
        value = normed_back(unit, spread, outer * gain)
        grad[r, :] = value
        rounded = low(value)
        grad_low[r, :] = rounded
        return (
            sums[0] + row_sum(rounded.astype(F32)),
            sums[1] + row_sum(outer * unit),
            sums[2] + row_sum(outer),
        )

    def norm_grads(i, sums):
        r = tile(i, ROWS)
        return (
            norm_grad(r, sums[0], asum, gains[0], feed, mixed),
            norm_grad(r, sums[1], lasum, gains[2], lfeed, lmixed),
        )

    found, lfound = lax.fori_loop(0, PAGE // ROWS, norm_grads, start)
    for i in range(3):
        vec[12 + i : 13 + i, :] = found[i]
        vec[15:16, i * 256 : i * 256 + lwidth] = lfound[i]
    act_now((NORM, 0))
    again[0].wait()
    k_t, lk_t, cgrad_t, lcgrad = v_t, lv_t, h_t, lctx
    masks[...] = jnp.zeros_like(masks)

    def turn(j):
        x_t[tile(j), :] = jnp.transpose(x_ref[:, tile(j)])

    def context_back(j):
        cols = tile(j)
        value = low(dot_nt(mixed[...], wo_again[cols, :]))
        cgrad[:, cols] = value
        cgrad_t[cols, :] = jnp.transpose(value)
        shared[0:width, cols] = low(dot(ctx_t[...], mixed[:, cols]))
        k_t[cols, :] = jnp.transpose(kn[:, cols])

    loop(tiles, context_back)
    value = jnp.concatenate([low(dot_nt(lmixed[...], lwo[...])), pad], axis=1)
    lcgrad[...] = value
    lcgrad_t[...] = jnp.transpose(value)
    lk_t[...] = jnp.transpose(lkn[...])
    loop(tiles, turn)
    act_now((CONTEXT, 0))

    lane = lax.broadcasted_iota(jnp.int32, (PAGE, 128), 1)
    ldv[...] = jnp.zeros_like(ldv)
    ldk[...] = jnp.zeros_like(ldk)
    ldq_t[...] = jnp.zeros_like(ldq_t)

    def attend_back(pair):
        text, block = tile(pair, 128), tile(pair // 4, 128)
        keys = jnp.concatenate([kn[:, text], lkn[:, block]], axis=1)
        values = jnp.concatenate([vn[:, text], lvn[:, block]], axis=1)
        grads = jnp.concatenate([cgrad[:, text], lcgrad[:, block]], axis=1)
        found = []
        for side in range(2):
            head = 2 * pair + side
            head_rows(masked, q_t, lq_t, pair, side)
            head_rows(masked_c, cgrad_t, lcgrad_t, pair, side)
            span = slice(side * 256, side * 256 + 256)
            weights = jnp.exp(dot(keys, masked[span, :]) - lse[pl.ds(head, 1), :])
            value_grad = dot(low(weights), grads)
            text_wave = dot(vn[:, text], masked_c[side * 256 : side * 256 + 128, :])
            text_part = row_sum(text_wave * weights)
            text_score = low(weights * (text_wave - text_part))
            both_wave = dot(values, masked_c[span, :])
            both_part = row_sum(both_wave * weights)
            both_score = low(weights * (both_wave - both_part))
            query_grad = low(dot(k_t[tile(head, 64), :], text_score) * 0.125)
            ldq_t[tile(head, 16), :] = low(dot(lk_t[tile(head, 16), :], both_score) * 0.25)
            key_grad = dot(text_score, qn[:, text])
            lkey_grad = dot(both_score, lqn[:, block])
            own = (lane // 16) == (head % 8)
            ldv[:, block] = jnp.where(own, value_grad[:, 128:256], ldv[:, block])
            ldk[:, block] = jnp.where(own, lkey_grad, ldk[:, block])
            found.append((value_grad[:, 0:128], key_grad, query_grad))
        first_half = lane < 64
        dv[:, text] = low(jnp.where(first_half, found[0][0], found[1][0]))
        dk[:, text] = low(jnp.where(first_half, found[0][1], found[1][1]))
        dq[:, text] = jnp.transpose(jnp.concatenate([found[0][2], found[1][2]], axis=0))
        for k in range(HEADS // 2):

            @pl.when(pair == k)
            def _():
                act_now((ATTEND, k))

        @pl.when(pair % 2 == 1)
        def _():
            weight_grad(pair // 2)

        for k in range(tiles - 1):

            @pl.when(pair == 2 * k + 1)
            def _():
                act_now((WEIGHT, k))

    def weight_grad(group):
        cols = tile(group)
        place = pl.ds(pl.multiple_of((1 + group) * width, 16), width)
        for i, source in enumerate((dq, dk, dv)):
            shared[place, i * TILE : (i + 1) * TILE] = low(dot(x_t[...], source[:, cols]))
        vec[10:11, cols] = row_sum(dq[:, cols].astype(F32))
        vec[11:12, cols] = row_sum(dv[:, cols].astype(F32))

    loop(HEADS // 2, attend_back)

    query = jnp.transpose(ldq_t[...])[:, 0:lwidth]
    key, value = low(ldk[:, 0:lwidth]), low(ldv[:, 0:lwidth])
    parts = [low(dot(lx_t[...], item)) for item in (query, key, value)]
    parts.append(low(dot(lctx_t[0:lwidth, :], lmixed[...])))
    base = 4 * width
    shared[base : base + lwidth, :] = jnp.concatenate(parts, axis=1)
    vec[9:10, 256 : 256 + lwidth] = row_sum(query.astype(F32))
    vec[9:10, 512 : 512 + lwidth] = row_sum(value.astype(F32))
    base += lwidth
    shared[base : base + 16, :] = low(vec[...])
    shared[base + 16 : shared_rows, :] = jnp.zeros((shared_rows - base - 16, width), BF16)
    act_now((WEIGHT, tiles - 1))
    for copy in again[1:]:
        copy.wait()

    def input_back(j):
        cols = tile(j)
        feed[:, cols] += (
            dot_nt(dq[...], wq_again[cols, :])
            + dot_nt(dk[...], wk_again[cols, :])
            + dot_nt(dv[...], wv_again[cols, :])
        )
        for k in range(tiles):

            @pl.when(j == k)
            def _():
                act_now((INPUT, k))

    loop(tiles, input_back)
    in_grad_copy = load(4, feed, in_grad_out)
    lin_grad[...] = jnp.transpose(
        lfeed[...] + dot_nt(query, lwq[...]) + dot_nt(key, lwk[...]) + dot_nt(value, lwv[...])
    )
    act_now((END, 0))
    act_now((TAIL, 0))
    for item in flows:
        item.drain()
    in_grad_copy.wait()


def small_places(outs):
    large = max(out.shape[0] for out in outs if len(out.shape) == 2)
    return [i for i, out in enumerate(outs) if i > 3 and out.shape != (large, large)]


def finish_kernel(feed_rows, sums_hbm, *refs):
    passed, outs = refs[0:4], refs[4:38]
    sums, wide_sums, vec = refs[38:41]
    through = refs[41:45]
    load_sem, store_sem, in_sem, out_sem, small_sem = refs[45:50]
    stage = dict(zip(small_places(outs), refs[50:]))
    width, lwidth = wide_sums.shape[1], through[1].shape[0]
    starts = (feed_rows, 0, width, feed_rows + width, feed_rows + 2 * width)
    starts += (feed_rows + 3 * width, feed_rows + 4 * width)
    sizes = [width, width, width + 128] + [width] * 3 + [sums.shape[0] - starts[-1]]
    loads = []
    for i, (start, size) in enumerate(zip(starts, sizes)):
        part = pl.ds(start, size)
        copy = pltpu.make_async_copy(sums_hbm.at[part], sums.at[part], load_sem.at[i])
        copy.start()
        loads.append(copy)
    takes = [
        pltpu.make_async_copy(a, b, in_sem.at[i]) for i, (a, b) in enumerate(zip(passed, through))
    ]
    gives = [
        pltpu.make_async_copy(a, b, out_sem.at[i]) for i, (a, b) in enumerate(zip(through, outs))
    ]
    for copy in takes:
        copy.start()

    def widen(slot, start, cols=None, lanes=None):
        def block(i):
            source = pl.ds(start + pl.multiple_of(i * 128, 128), 128)
            target = pl.ds(pl.multiple_of(i * 128, 128), 128)
            if cols is None:
                wide_sums[slot, target, :] = sums[source, :].astype(F32)
            else:
                wide_sums[slot, target, lanes] = sums[source, cols].astype(F32)

        loop(width // 128, block)

    results = [stage.get(i, out) for i, out in enumerate(outs)]
    text, layout = results[4:19], results[19:34]
    stores = []

    def store(slot, out):
        copy = pltpu.make_async_copy(wide_sums.at[slot], out, store_sem.at[slot])
        copy.start()
        stores.append(copy)

    loads[0].wait()
    widen(0, starts[0])
    store(0, text[5])
    blocks = range(width // TILE)
    for slot, out in ((1, text[11]), (2, text[9])):
        loads[slot].wait()
        for i in blocks:
            for q in blocks:
                rows = pl.ds(starts[slot] + i * TILE, TILE)
                value = sums[rows, q * TILE : (q + 1) * TILE].astype(F32)
                place = (i, q) if slot == 1 else (q, i)
                value = jnp.transpose(value) if slot == 1 else value
                down, across = (pl.ds(k * TILE, TILE) for k in place)
                wide_sums[slot, down, across] = value
        store(slot, out)
    for copy, give in zip(takes, gives):
        copy.wait()
        give.start()
    for g in range(width // TILE):
        loads[3 + g].wait()
        for i in range(3):
            lanes = slice(g * TILE, (g + 1) * TILE)
            widen(3 + i, starts[3 + g], slice(i * TILE, (i + 1) * TILE), lanes)
    for i, out in enumerate((text[0], text[2], text[3])):
        store(3 + i, out)
    loads[6].wait()
    base = starts[6]
    for i, out in enumerate((layout[0], layout[2], layout[3], layout[5])):
        out[...] = sums[base : base + lwidth, i * lwidth : (i + 1) * lwidth].astype(F32)
    for i, out in enumerate((layout[9], layout[11])):
        for q in range(lwidth // 64):
            top = 2 * width + 64 * i
            rows = sums[top : top + 64, q * TILE : q * TILE + lwidth]
            out[q * 64 : q * 64 + 64, :] = rows.astype(F32)
    vec[...] = sums[base + lwidth : base + lwidth + 16, :].astype(F32)
    me = lax.axis_index("tensor")
    for row, out in ((10, 1), (11, 4), (12, 6), (13, 7), (14, 8), (2, 12), (0, 13), (1, 14)):
        text[out][...] = vec[row, :]
    text[10][...] = vec[pl.ds(3 + me, 1), :][0]

    def strip(row, part):
        return vec[row : row + 1, part * TILE : part * TILE + lwidth]

    places = ((9, 1, 1), (9, 2, 4), (15, 0, 6), (15, 1, 7), (15, 2, 8))
    for row, part, out in places + ((7, 2, 12), (7, 0, 13), (7, 1, 14)):
        layout[out][...] = strip(row, part)[0]
    rise = strip(8, 0)
    for k, (row, part) in enumerate(((8, 1), (8, 2), (9, 0))):
        rise = jnp.where(me == k + 1, strip(row, part), rise)
    layout[10][...] = rise[0]
    for k, (i, ref) in enumerate(stage.items()):
        copy = pltpu.make_async_copy(ref, outs[i], small_sem.at[k])
        copy.start()
        stores.append(copy)
    for copy in stores + gives:
        copy.wait()


MOVES = {
    (D, 0): (14,),
    (D, 1): (15,),
    (D, 2): (16,),
    (UNITS, 1): (0, 14),
    (UNITS, 2): (1, 15),
    (UNITS, 3): (2, 16),
    (UP, 0): (17,),
    (UP, 1): (18,),
    (UP, 2): (19,),
    (BACK, 1): (3, 17, 0, 14, 4, 1, 15),
    (BACK, 2): (2, 18, 5, 19),
    (NORM, 0): (0, 14),
    (CONTEXT, 0): (21, 20, 1, 15),
    (ATTEND, 0): (16, 3, 7, 0, 14, 6, 1, 4, 21),
    (ATTEND, 1): (18, 15),
    (WEIGHT, 0): (23, 22, 20, 2, 5, 16, 0, 14),
    (ATTEND, 2): (19, 9, 23, 8, 7, 1, 15, 4, 18, 6, 0),
    (ATTEND, 3): (22, 21, 2, 20, 16, 1),
    (WEIGHT, 1): (25, 24, 17, 14, 9, 4, 18),
    (ATTEND, 4): (23, 15, 5, 19, 7, 11, 10, 8, 25, 6, 2),
    (ATTEND, 5): (22, 16, 24, 3, 21, 0, 4, 9, 23),
    (WEIGHT, 2): (26, 27, 17, 20, 18, 5, 1, 19, 8, 10, 24, 11, 25, 7, 2, 9, 12, 26, 6, 13),
    (INPUT, 0): (3, 27, 4, 18, 10, 21),
    (INPUT, 1): (11, 25),
    (INPUT, 2): (23,),
    (END, 0): (24, 12, 26),
    (TAIL, 0): (5, 22, 4, 20, 7, 21, 11, 13, 27, 25, 10, 12, 8, 26, 9, 6, 23, 7, 21, 13, 27, 11, 25, 22, 12, 9, 23, 26, 7, 21, 13, 27, 11, 25, 8, 24, 20, 9, 23, 12, 26, 22, 11, 25, 17, 13, 6, 20, 10, 7, 21, 12, 24, 26, 8, 27, 9, 23, 22, 19, 7, 6, 20, 9, 11, 25, 10, 24, 12, 26, 16, 3, 17, 13, 8, 27, 11, 6, 20, 10, 22, 6, 5, 19, 3, 24, 12, 26, 13, 27, 17, 2, 12, 8, 22, 10, 24, 8, 10, 13, 27, 5, 3, 13),
}
FEED_ORDERS = ((0, ACROSS, 1), (ACROSS, 0, 1), (1, ACROSS, 0), (1, ACROSS, 0), (ACROSS, 0, 1), (0, ACROSS, 1))
SHARED_ORDERS = ((ACROSS, 0, 1), (ACROSS, 0, 1), (ACROSS, 0, 1), (0, ACROSS, 1), (1, 0, ACROSS), (ACROSS, 0, 1), (ACROSS, 0, 1), (ACROSS, 0, 1))
SHARED_ROWS = (256, 512, 256, 512, 256, 512, 512, 512)
GROUPS = (0, 0, 1, 1, 2, 2, 3, 3)

START = (3, 2, 39, 42, 18, 21, 22, 41, 1, 0, 19, 38, 20, 37)
GATHER = {
    (SETUP, 0): (39, 42),
    (PROJECT, 2): (3, 18),
    (HEAD, 0): (2, 37),
    (HEAD, 2): (21, 8),
    (HEAD, 3): (22, 41),
    (HEAD, 4): (6, 16),
    (HEAD, 5): (43, 1),
    (MIX, 0): (25, 14, 0, 27, 12),
    (FIRST, 0): (19, 33, 10),
    (FED, 0): (35, 9, 7, 29),
    (FED, 1): (4, 38, 5, 17),
    (FED, 2): (15, 11, 20),
    (FEED, 3): (40, 13),
    (FED, 3): (28, 31),
    (DONE, 0): (26, 23),
    (DONE, 1): (36,),
    (DOWN, 2): (24,),
    (DONE, 2): (34, 30),
    (DOWN, 3): (32,),
}


def on_device(dp, tensor, *args):
    (
        text_in,
        layout_in,
        token_mask,
        box_mask,
        cot_text,
        cot_layout,
    ) = args[:6]
    text, layout = args[6:21], args[21:36]
    width, lwidth = text_in.shape[1], layout_in.shape[1]
    dp_bits = dp.bit_length() - 1
    half = width // 2
    feed_flows = tuple(zip((TILE, TILE, TILE, TILE, TILE, TILE + 128), FEED_ORDERS))
    shared_flows = tuple(zip(SHARED_ROWS, SHARED_ORDERS))
    moves = MOVES if dp_bits == 3 else {}
    feed_rows = sum(rows for rows, _ in feed_flows)
    shared_rows = sum(rows for rows, _ in shared_flows)
    land = sum(landing(4 * rows, dp_bits + 2) for rows, _ in feed_flows)
    shared_land = sum(landing(rows, dp_bits + 2) for rows, _ in shared_flows)
    pool_rows = max(8 * width + 8 * PAGE, 2 * shared_rows + 4 * PAGE + width)
    count = (2 * dp_bits + 2) * len(feed_flows) + (2 * dp_bits + 4) * len(shared_flows)

    vmem = pl.BlockSpec(memory_space=pltpu.VMEM)
    hbm = pl.BlockSpec(memory_space=pl.ANY)
    page = PAGE

    def shape(*dims, dtype=BF16):
        return jax.ShapeDtypeStruct(dims, dtype)

    def row(vector):
        return vector.reshape(1, vector.shape[0])

    inputs = (text_in, layout_in.T, row(token_mask), row(box_mask), cot_text, cot_layout.T)
    inputs += text + layout
    specs = [vmem] * len(inputs)
    for i in (6, 8, 9, 11, 15, 17):
        specs[i] = hbm
    outs = (
        shape(page, width),
        shape(lwidth, page),
        shape(page, width, dtype=F32),
        shape(lwidth, page, dtype=F32),
        shape(feed_rows + shared_rows, width),
    )
    scratch = [
        pltpu.VMEM((pool_rows, width), BF16),
        pltpu.VMEM((2 * feed_rows, width), BF16),
        pltpu.VMEM((max(2 * feed_rows, shared_land), width), BF16),
        pltpu.VMEM((land, width), BF16),
        pltpu.VMEM((feed_rows, width), BF16),
        pltpu.VMEM((4, 2 * lwidth, 256), BF16),
        pltpu.VMEM((4, 8, 256), F32),
        pltpu.VMEM((page, width), BF16),
        pltpu.VMEM((page, width), BF16),
        pltpu.VMEM((page, width), BF16),
        pltpu.VMEM((width, page), BF16),
        pltpu.VMEM((width, page), BF16),
        pltpu.VMEM((page, 256), BF16),
        pltpu.VMEM((page, 256), BF16),
        pltpu.VMEM((page, 256), BF16),
        pltpu.VMEM((256, page), BF16),
        pltpu.VMEM((256, page), BF16),
        pltpu.VMEM((16, page), F32),
        pltpu.VMEM((1024, page), BF16),
        pltpu.VMEM((width, page), BF16),
        pltpu.VMEM((256, page), BF16),
        pltpu.VMEM((page, 256), BF16),
        pltpu.VMEM((page, width), F32),
        pltpu.VMEM((page, width), BF16),
        pltpu.VMEM((page, lwidth), BF16),
        pltpu.VMEM((width, page), BF16),
        pltpu.VMEM((lwidth, page), BF16),
        pltpu.VMEM((page, width), F32),
        pltpu.VMEM((page, lwidth), F32),
        pltpu.VMEM((4, page, lwidth), BF16),
        pltpu.VMEM((4, page, lwidth), BF16),
        pltpu.VMEM((page, 16), F32),
        pltpu.VMEM((8, width), F32),
        pltpu.VMEM((page, lwidth), BF16),
        pltpu.VMEM((page, lwidth), BF16),
        pltpu.VMEM((256, page), BF16),
        pltpu.VMEM((256, page), BF16),
        pltpu.VMEM((page, 256), F32),
        pltpu.VMEM((page, 256), F32),
        pltpu.VMEM((16, width), F32),
        pltpu.SemaphoreType.DMA((6,)),
        pltpu.SemaphoreType.DMA((48,)),
        pltpu.SemaphoreType.DMA((48,)),
        pltpu.SemaphoreType.DMA((count,)),
        pltpu.SemaphoreType.DMA((count,)),
        pltpu.SemaphoreType.DMA((len(feed_flows) + len(shared_flows),)),
        pltpu.SemaphoreType.REGULAR((dp_bits + 2,)),
    ]
    text_out, layout_out, in_grad, lin_grad, sums = pl.pallas_call(
        functools.partial(layer_kernel, (dp_bits, feed_flows, shared_flows, moves)),
        out_shape=outs,
        in_specs=specs,
        out_specs=[vmem, vmem, hbm, vmem, hbm],
        scratch_shapes=scratch,
        compiler_params=pltpu.CompilerParams(
            collective_id=0, has_side_effects=True, vmem_limit_bytes=67043328
        ),
        name="layer",
    )(*inputs)

    big, small_square = shape(width, width, dtype=F32), shape(lwidth, lwidth, dtype=F32)

    def stream(square, size):
        line = shape(size, dtype=F32)
        order = (square, line, square, square, line, square, line, line, line)
        return order + (square, line, square, line, line, line)

    outs = (
        shape(page, width),
        shape(lwidth, page),
        shape(page, width, dtype=F32),
        shape(lwidth, page, dtype=F32),
    )
    outs += stream(big, width) + stream(small_square, lwidth)
    stage = [pltpu.VMEM(outs[i].shape, F32) for i in small_places(outs)]
    done = pl.pallas_call(
        functools.partial(finish_kernel, feed_rows),
        out_shape=outs,
        in_specs=[hbm] * 5,
        out_specs=[hbm] * len(outs),
        scratch_shapes=[
            pltpu.VMEM((feed_rows + shared_rows, width), BF16),
            pltpu.VMEM((6, width, width), F32),
            pltpu.VMEM((16, width), F32),
            pltpu.VMEM((page, width), BF16),
            pltpu.VMEM((lwidth, page), BF16),
            pltpu.VMEM((page, width), F32),
            pltpu.VMEM((lwidth, page), F32),
            pltpu.SemaphoreType.DMA((7,)),
            pltpu.SemaphoreType.DMA((6,)),
            pltpu.SemaphoreType.DMA((4,)),
            pltpu.SemaphoreType.DMA((4,)),
            pltpu.SemaphoreType.DMA((len(stage),)),
            *stage,
        ],
        compiler_params=pltpu.CompilerParams(vmem_limit_bytes=60000000),
        name="finish",
    )(sums, text_out, layout_out, in_grad, lin_grad)
    return (done[0], done[1].T, done[2], done[3].T) + tuple(done[4:])


def solution(mesh):
    rows = P(("dp", "tensor"), None)
    line = P(("dp", "tensor"))
    weights = (P(),) * 9 + (P(None, "tensor"), P("tensor"), P("tensor", None)) + (P(),) * 3
    in_specs = (rows, rows, line, line, rows, rows) + weights + weights
    out_specs = (rows,) * 4 + weights + weights
    return jax.shard_map(
        functools.partial(on_device, mesh.shape["dp"], mesh.shape["tensor"]),
        mesh=mesh,
        in_specs=in_specs,
        out_specs=out_specs,
        check_vma=False,
    )
```
